256 devices in a mesh: sec: 2 (over x_hi), tile: 128 (over z, y, x_lo, core).
Axes of the slice: x: 4 (x_hi: 2, x_lo: 2; x = x_hi * 2 + x_lo), y: 4, z: 8, core: 2. Of those that a mesh axis runs over, the one named last changes fastest.
Arguments:
- load_field: float32 [3, 512, 256, 128], P(None, 'tile', 'sec'), may hold values from -6 to 6
- iterate: float32 [3, 512, 256, 128], P(None, 'tile', 'sec'), may hold values from -3 to 3
- phase_label: int32 [512, 256, 128], P('tile', 'sec'), may hold values from 0 to 3
- damage: int32 [512, 256, 128], P('tile', 'sec'), may hold values from 0 to 3
Outputs:
- correction: float32 [3, 512, 256, 128], P(None, 'tile', 'sec')
The draws below stay inside these ranges and needn't reach their ends.
All inputs are finite; a program needn't handle non-finite values.
Results may differ from the reference program's by a relative error of at most 0.0001.
Values sent between devices are 32-bit elements; how exact they have to be, the bound alone decides.
A program may use at most 64 MiB of HBM per device.

```python
import jax
import jax.numpy as jnp

COMPONENTS = 3
NZ = 128
NX = 512
NY = 256


def place_ends(values, rng, least, high):
    shape = values.shape
    index_at = [jax.random.randint(jax.random.fold_in(rng, axis), (), 0, shape[axis]) for axis in range(len(shape))]
    values = values.at[tuple(index_at)].set(least)
    longest = shape.index(max(shape))
    index_at[longest] = (index_at[longest] + 1) % shape[longest]
    return values.at[tuple(index_at)].set(high)


def shard_levels(own_key, dims, pieces, low, largest):
    level = 1.0
    for dim, blocks in pieces:
        heights = jax.random.uniform(jax.random.fold_in(jax.random.fold_in(own_key, 6), dim), (blocks,), jnp.float32, low / len(pieces), largest / len(pieces))
        level = level * jnp.repeat(jnp.exp(heights), dims[dim] // blocks).reshape((-1,) + (1,) * (len(dims) - 1 - dim))
    return level


def bell_draw(rng, shape, scale, limit, split=(), held_as=jnp.bfloat16):
    values = jax.random.normal(rng, shape, jnp.float32) * scale
    if len(split) > 0:
        values = shard_levels(rng, shape, split, -0.22, 0.18) * values
    return jnp.clip(values, min=-limit, max=limit).astype(held_as)


def setup_inputs(seed: int = 0) -> dict:
    seeds = jax.random.split(jax.random.key(seed), 5)
    return {
        "load_field": bell_draw(seeds[0], (COMPONENTS, NX, NY, NZ), 1.0, 6.0, ((1, 128), (2, 2)), jnp.float32),
        "iterate": bell_draw(seeds[1], (COMPONENTS, NX, NY, NZ), 0.5, 3.0, ((1, 128), (2, 2)), jnp.float32),
        "phase_label": place_ends(jax.random.randint(seeds[2], (NX, NY, NZ), 0, 4), jax.random.fold_in(seeds[2], 1), 0, 3).astype(jnp.int32),
        "damage": place_ends(jax.random.randint(seeds[3], (NX, NY, NZ), 0, 4), jax.random.fold_in(seeds[3], 1), 0, 3).astype(jnp.int32),
    }


shear_table = (1.0, 0.6, 1.8, 0.35)
bulk_table = (1.2, 0.9, 2.5, 0.5)
damage_step = 0.25
damage_floor = 0.01
relaxation = 2.0 / 3.0


def material(phase_label, damage):
    shear = jnp.zeros(phase_label.shape, jnp.float32)
    bulk = jnp.zeros(phase_label.shape, jnp.float32)
    for label in range(len(shear_table)):
        hit = phase_label == label
        shear = shear + jnp.where(hit, shear_table[label], 0.0)
        bulk = bulk + jnp.where(hit, bulk_table[label], 0.0)
    soft = 1.0 - damage_step * damage.astype(jnp.float32)
    degrade = soft * soft + damage_floor
    return shear * degrade, bulk * degrade


def neighbour(array, direction, offset):
    leading = array.ndim - 3
    selector = [slice(None)] * leading + [slice(1, extent - 1) for extent in array.shape[leading:]]
    extent = array.shape[leading + direction]
    selector[leading + direction] = slice(offset, offset + extent - 2)
    return array[tuple(selector)]


def face_weights(padded_shear, padded_bulk):
    result = []
    for direction in range(3):
        unit_row = jnp.array([1.0 if comp_index == direction else 0.0 for comp_index in range(3)], jnp.float32)
        for offset in (0, 2):
            face_shear = 0.5 * (neighbour(padded_shear, direction, 1) + neighbour(padded_shear, direction, offset))
            face_bulk = 0.5 * (neighbour(padded_bulk, direction, 1) + neighbour(padded_bulk, direction, offset))
            result.append(face_shear[None] + unit_row[:, None, None, None] * (face_bulk + face_shear)[None])
    return result


def operate(padded, weights):
    running = None
    counter = 0
    for direction in range(3):
        for offset in (0, 2):
            term = weights[counter] * (neighbour(padded, direction, 1) - neighbour(padded, direction, offset))
            running = term if running is None else running + term
            counter += 1
    return running


def diagonal_of(weights):
    running = weights[0]
    for face_weight in weights[1:]:
        running = running + face_weight
    return running


def coarsen(weights):
    result = []
    counter = 0
    for direction in range(3):
        for child_pos in (0, 1):
            face_weight = weights[counter]
            comps, rows, cols, depth = face_weight.shape
            blocks = face_weight.reshape(comps, rows // 2, 2, cols // 2, 2, depth // 2, 2)
            removed = 2 + 2 * direction
            selector = [slice(None)] * 7
            selector[removed] = child_pos
            picked = blocks[tuple(selector)]
            summed_axes = tuple(place if place < removed else place - 1 for place in (2, 4, 6) if place != removed)
            result.append(jnp.sum(picked, axis=summed_axes))
            counter += 1
    return result


def restrict(field):
    comps, rows, cols, depth = field.shape
    return field.reshape(comps, rows // 2, 2, cols // 2, 2, depth // 2, 2).sum(axis=(2, 4, 6))


def prolong(field):
    return jnp.repeat(jnp.repeat(jnp.repeat(field, 2, axis=1), 2, axis=2), 2, axis=3)


def smooth(residual, weights, padder):
    diagonal = diagonal_of(weights)
    first_sweep = relaxation * residual / diagonal
    extended = padder(first_sweep)
    return first_sweep + relaxation * (residual - operate(extended, weights)) / diagonal


def pad_cells(field):
    return jnp.pad(field, ((0, 0), (1, 1), (1, 1), (1, 1)))


def reference(load_field, iterate, phase_label, damage):
    shear, bulk = material(phase_label, damage)
    weights = face_weights(jnp.pad(shear, 1), jnp.pad(bulk, 1))
    residual = load_field - operate(pad_cells(iterate), weights)
    fine_corr = smooth(residual, weights, pad_cells)
    weights_two = coarsen(weights)
    residual_two = restrict(residual)
    middle_corr = smooth(residual_two, weights_two, pad_cells)
    weights_three = coarsen(weights_two)
    residual_three = restrict(residual_two)
    bottom_corr = smooth(residual_three, weights_three, pad_cells)
    return fine_corr + prolong(middle_corr + prolong(bottom_corr))
```

```python
import functools

import jax
import jax.numpy as jnp
from jax import lax
from jax.experimental import pallas as pl
from jax.experimental.pallas import tpu as pltpu
from jax.sharding import PartitionSpec as P

shear_table = (1.0, 0.6, 1.8, 0.35)
bulk_table = (1.2, 0.9, 2.5, 0.5)
damage_step = 0.25
damage_floor = 0.01
relaxation = 2.0 / 3.0

MESH = pl.DeviceIdType.MESH
X = 4
Y = 128
Z = 128
OFF = 8


def lanes(shape):
    return lax.broadcasted_iota(jnp.int32, shape, len(shape) - 1)


def roll(v, shift):
    return pltpu.roll(v, shift % Z, v.ndim - 1)


def from_above(v, step):
    return jnp.where(lanes(v.shape) < Z - step, roll(v, -step), 0.0)


def from_below(v, step):
    return jnp.where(lanes(v.shape) >= step, roll(v, step), 0.0)


def moduli(phase, damage):
    soft = 1.0 - damage_step * damage.astype(jnp.float32)
    degrade = soft * soft + damage_floor

    def table(values):
        picked = jnp.full(phase.shape, values[3], jnp.float32)
        for label in (2, 1, 0):
            picked = jnp.where(phase == label, values[label], picked)
        return picked

    half = table([0.5 * s for s in shear_table])
    normal = table([0.5 * b + s for s, b in zip(shear_table, bulk_table)])
    return half * degrade, normal * degrade


def kernel(tiles, load_hbm, u_hbm, lab_hbm, dam_hbm, out, U, F, L, INV, R, E, H, K, LAB, DAM, S1, S1R, S2, S2R,
           PS, PR, W2, F2, I2, F3, EX, local_sem, send_sem, recv_sem):
    me = lax.axis_index("tile")
    sec = lax.axis_index("sec")
    has_up = me < tiles - 1
    has_down = me > 0
    up = {"tile": jnp.minimum(me + 1, tiles - 1)}
    down = {"tile": jnp.maximum(me - 1, 0)}
    across = {"sec": 1 - sec}

    loads = [
        pltpu.make_async_copy(lab_hbm, LAB.at[pl.ds(1, X)], local_sem.at[0]),
        pltpu.make_async_copy(dam_hbm, DAM.at[pl.ds(1, X)], local_sem.at[1]),
        pltpu.make_async_copy(u_hbm, U.at[:, pl.ds(1, X), pl.ds(OFF, Y)], local_sem.at[2]),
        pltpu.make_async_copy(load_hbm, L, local_sem.at[3]),
    ]
    for copy in loads:
        copy.start()

    barrier = pltpu.get_barrier_semaphore()

    @pl.when(has_up)
    def _():
        pl.semaphore_signal(barrier, inc=1, device_id=up, device_id_type=MESH)

    @pl.when(has_down)
    def _():
        pl.semaphore_signal(barrier, inc=1, device_id=down, device_id_type=MESH)

    pl.semaphore_signal(barrier, inc=1, device_id=across, device_id_type=MESH)
    pl.semaphore_wait(barrier, 1 + has_up.astype(jnp.int32) + has_down.astype(jnp.int32))

    def remote(src, dst, index, device):
        return pltpu.make_async_remote_copy(
            src_ref=src, dst_ref=dst, send_sem=send_sem.at[index], recv_sem=recv_sem.at[index],
            device_id=device, device_id_type=MESH)

    rows = pl.ds(OFF, Y)
    ups = [
        remote(lab_hbm.at[X - 1], LAB.at[0], 0, up),
        remote(dam_hbm.at[X - 1], DAM.at[0], 1, up),
        remote(u_hbm.at[:, X - 1], U.at[:, 0, rows], 2, up),
    ]
    downs = [
        remote(lab_hbm.at[0], LAB.at[X + 1], 3, down),
        remote(dam_hbm.at[0], DAM.at[X + 1], 4, down),
        remote(u_hbm.at[:, 0], U.at[:, X + 1, rows], 5, down),
    ]

    @pl.when(has_up)
    def _():
        for copy in ups:
            copy.start()

    @pl.when(has_down)
    def _():
        for copy in downs:
            copy.start()

    loads[0].wait()
    loads[1].wait()

    @pl.loop(0, Y // 8)
    def _(i):
        y = pl.multiple_of(i * 8, 8)
        for p in range(1, X + 1):
            h, k = moduli(LAB[p, pl.ds(y, 8), :], DAM[p, pl.ds(y, 8), :])
            H[p, pl.ds(OFF + y, 8), :] = h
            K[p, pl.ds(OFF + y, 8), :] = k

    loads[2].wait()

    own_row = jnp.where(sec == 0, OFF + Y - 1, OFF)
    halo_row = jnp.where(sec == 0, OFF + Y, OFF - 1)
    edge_row = jnp.where(sec == 0, OFF - 1, OFF + Y)
    faces = [H.at[pl.ds(1, X)], K.at[pl.ds(1, X)]] + [U.at[c, pl.ds(1, X)] for c in range(3)]
    for f, ref in enumerate(faces):
        for p in range(X):
            S1[pl.ds(X * f + p, 1), :] = ref[p, pl.ds(own_row, 1), :]
    for r in range(20, 24):
        S1[pl.ds(r, 1), :] = jnp.zeros((1, Z), jnp.float32)
    cross1 = remote(S1, S1R, 6, across)
    cross1.start()
    zero_row = jnp.zeros((1, Z), jnp.float32)
    for ref in faces:
        for p in range(X):
            ref[p, pl.ds(edge_row, 1), :] = zero_row
    for c in range(3):
        for p in range(1, X + 1):
            F[c, p, pl.ds(edge_row, 1), :] = zero_row

    @pl.when(jnp.logical_not(has_down))
    def _():
        H[0] = jnp.zeros(H.shape[1:], jnp.float32)
        K[0] = jnp.zeros(K.shape[1:], jnp.float32)
        for c in range(3):
            U[c, 0] = jnp.zeros(U.shape[2:], jnp.float32)
            F[c, 0] = jnp.zeros(F.shape[2:], jnp.float32)

    @pl.when(jnp.logical_not(has_up))
    def _():
        H[X + 1] = jnp.zeros(H.shape[1:], jnp.float32)
        K[X + 1] = jnp.zeros(K.shape[1:], jnp.float32)
        for c in range(3):
            U[c, X + 1] = jnp.zeros(U.shape[2:], jnp.float32)
            F[c, X + 1] = jnp.zeros(F.shape[2:], jnp.float32)

    loads[3].wait()
    cross1.wait()
    for f, ref in enumerate(faces):
        for p in range(X):
            ref[p, pl.ds(halo_row, 1), :] = S1R[pl.ds(X * f + p, 1), :]

    def weights(p, y):
        result = {}
        for name, M in (("s", H), ("t", K)):
            m = M[p, pl.ds(OFF + y, 8), :]
            if p > 1:
                result[name, "xl"] = m + M[p - 1, pl.ds(OFF + y, 8), :]
            if p < X:
                result[name, "xu"] = m + M[p + 1, pl.ds(OFF + y, 8), :]
            result[name, "yl"] = m + M[p, pl.ds(OFF + y - 1, 8), :]
            result[name, "yu"] = m + M[p, pl.ds(OFF + y + 1, 8), :]
            result[name, "zl"] = m + from_below(m, 1)
            result[name, "zu"] = m + from_above(m, 1)
        return result

    def neighbours(V, c, p, y, w):
        v = V[c, p, pl.ds(OFF + y, 8), :]
        kind = ["t" if c == a else "s" for a in range(3)]
        total = w[kind[1], "yl"] * V[c, p, pl.ds(OFF + y - 1, 8), :]
        total = total + w[kind[1], "yu"] * V[c, p, pl.ds(OFF + y + 1, 8), :]
        total = total + w[kind[2], "zl"] * from_below(v, 1)
        total = total + w[kind[2], "zu"] * from_above(v, 1)
        if p > 1:
            total = total + w[kind[0], "xl"] * V[c, p - 1, pl.ds(OFF + y, 8), :]
        if p < X:
            total = total + w[kind[0], "xu"] * V[c, p + 1, pl.ds(OFF + y, 8), :]
        return total, v

    @pl.loop(0, Y // 8)
    def _(i):
        y = pl.multiple_of(i * 8, 8)
        here = pl.ds(y, 8)
        for p in range(1, X + 1):
            w = weights(p, y)
            sides = {}
            for name in ("s", "t"):
                xs = [w[name, side] for side in ("xl", "xu") if (name, side) in w]
                sides[name, 0] = xs[0] if len(xs) == 1 else xs[0] + xs[1]
                sides[name, 1] = w[name, "yl"] + w[name, "yu"]
                sides[name, 2] = w[name, "zl"] + w[name, "zu"]
            for c in range(3):
                total, v = neighbours(U, c, p, y, w)
                others = [a for a in range(3) if a != c]
                diag = sides["t", c] + sides["s", others[0]] + sides["s", others[1]]
                acc = L[c, p - 1, here, :] + total
                if 1 < p < X:
                    r = acc - diag * v
                    inv = relaxation / diag
                    R[c, p - 2, here, :] = r
                    INV[c, p - 1, here, :] = inv
                    F[c, p, pl.ds(OFF + y, 8), :] = r * inv
                else:
                    L[c, p - 1, here, :] = acc
                    INV[c, p - 1, here, :] = diag

    @pl.when(has_down)
    def _():
        for copy in ups:
            copy.wait_recv()

    @pl.when(has_up)
    def _():
        for copy in downs:
            copy.wait_recv()

    @pl.loop(0, Y // 8)
    def _(i):
        y = pl.multiple_of(i * 8, 8)
        here = pl.ds(y, 8)
        there = pl.ds(OFF + y, 8)
        for p, q, present in ((1, 0, has_down), (X, X + 1, has_up)):
            h, k = moduli(LAB[q, here, :], DAM[q, here, :])
            scale = present.astype(jnp.float32)
            h = jnp.where(present, h, 0.0)
            k = jnp.where(present, k, 0.0)
            H[q, there, :] = h
            K[q, there, :] = k
            s = h + H[p, there, :]
            t = k + K[p, there, :]
            for c in range(3):
                w = t if c == 0 else s
                diag = INV[c, p - 1, here, :] + w
                r = L[c, p - 1, here, :] + w * U[c, q, there, :] - diag * U[c, p, there, :]
                inv = relaxation / diag
                INV[c, p - 1, here, :] = inv
                F[c, p, there, :] = r * inv
                R[c, (p - 1) // 2, here, :] = R[c, (p - 1) // 2, here, :] + r

    f_up = remote(F.at[:, X, rows], F.at[:, 0, rows], 7, up)
    f_down = remote(F.at[:, 1, rows], F.at[:, X + 1, rows], 8, down)

    @pl.when(has_up)
    def _():
        f_up.start()

    @pl.when(has_down)
    def _():
        f_down.start()

    Y2, Y3 = Y // 2, Y // 4
    shape2, shape3 = (Y2, Z), (Y3, Z)
    odd2 = (lanes(shape2) & 1) == 1

    def pairs(v):
        return v + jnp.where(odd2, roll(v, 1), roll(v, -1))

    def every_other(M, p, first):
        return M[p, pl.ds(first, Y2, stride=2), :]

    for m, M in enumerate((H, K)):
        for j in range(3):
            face = every_other(M, 2 * j, OFF) + every_other(M, 2 * j, OFF + 1)
            face = face + every_other(M, 2 * j + 1, OFF) + every_other(M, 2 * j + 1, OFF + 1)
            W2[m, j] = pairs(face)
        for j in range(2):
            r7, r8, r9, r10 = [
                every_other(M, 1 + 2 * j, OFF + d) + every_other(M, 2 + 2 * j, OFF + d) for d in (-1, 0, 1, 2)]
            W2[m, 3 + j] = pairs(r7 + r8)
            W2[m, 5 + j] = pairs(r9 + r10)
            cell = r8 + r9
            low = cell + from_below(cell, 1)
            high = cell + from_above(cell, 1)
            W2[m, 7 + j] = jnp.where(odd2, roll(low, 1), low)
            W2[m, 9 + j] = jnp.where(odd2, high, roll(high, -1))

    def kinds(c):
        return [1 if c == a else 0 for a in range(3)]

    for c in range(3):
        kx, ky, kz = kinds(c)
        for j in range(2):
            diag = W2[kx, j] + W2[kx, j + 1] + W2[ky, 3 + j] + W2[ky, 5 + j] + W2[kz, 7 + j] + W2[kz, 9 + j]
            inv = relaxation / diag
            I2[c, j] = inv
            res = R[c, j, pl.ds(0, Y2, stride=2), :] + R[c, j, pl.ds(1, Y2, stride=2), :]
            res = pairs(res)
            EX[c, j] = res
            F2[c, 1 + j, pl.ds(OFF, Y2), :] = res * inv

    quad = lanes(shape3) & 3
    high3 = quad >= 2

    def quads(v):
        return v + jnp.where(high3, roll(v, 2), roll(v, -2))

    def row_of(m, slot, first):
        return W2[m, slot, pl.ds(first, Y3, stride=2), :]

    w3 = {}
    for m in range(2):
        w3[m, "xl"] = quads(row_of(m, 0, 0) + row_of(m, 0, 1))
        w3[m, "xu"] = quads(row_of(m, 2, 0) + row_of(m, 2, 1))
        w3[m, "yl"] = quads(row_of(m, 3, 0) + row_of(m, 4, 0))
        w3[m, "yu"] = quads(row_of(m, 5, 1) + row_of(m, 6, 1))
        low = row_of(m, 7, 0) + row_of(m, 7, 1) + row_of(m, 8, 0) + row_of(m, 8, 1)
        high = row_of(m, 9, 0) + row_of(m, 9, 1) + row_of(m, 10, 0) + row_of(m, 10, 1)
        w3[m, "zl"] = jnp.where(high3, roll(low, 2), low)
        w3[m, "zu"] = jnp.where(high3, high, roll(high, -2))
    inv3 = []
    for c in range(3):
        kx, ky, kz = kinds(c)
        diag = w3[kx, "xl"] + w3[kx, "xu"] + w3[ky, "yl"] + w3[ky, "yu"] + w3[kz, "zl"] + w3[kz, "zu"]
        inv3.append(relaxation / diag)
        res = EX[c, 0, pl.ds(0, Y3, stride=2), :] + EX[c, 0, pl.ds(1, Y3, stride=2), :]
        res = res + EX[c, 1, pl.ds(0, Y3, stride=2), :] + EX[c, 1, pl.ds(1, Y3, stride=2), :]
        F3[c, 1, pl.ds(OFF, Y3), :] = quads(res) * inv3[c]

    half = Y2 // 2
    odd_half = odd2[:half]
    quad8 = quad[:8]
    for side, p2 in ((0, 2), (1, 1)):
        for c in range(3):
            a = F2[c, p2, pl.ds(OFF, half), :]
            b = F2[c, p2, pl.ds(OFF + half, half), :]
            PS[side, pl.ds(half * c, half), :] = jnp.where(odd_half, b, a)
            v = F3[c, 1, pl.ds(OFF, 8), :]
            for q in range(1, 4):
                v = jnp.where(quad8 == q, F3[c, 1, pl.ds(OFF + 8 * q, 8), :], v)
            PS[side, pl.ds(3 * half + 8 * c, 8), :] = v
    c_up = remote(PS.at[0], PR.at[0], 9, up)
    c_down = remote(PS.at[1], PR.at[1], 10, down)

    @pl.when(has_up)
    def _():
        c_up.start()

    @pl.when(has_down)
    def _():
        c_down.start()

    own2 = jnp.where(sec == 0, OFF + Y2 - 1, OFF)
    own3 = jnp.where(sec == 0, OFF + Y3 - 1, OFF)
    halo2 = jnp.where(sec == 0, OFF + Y2, OFF - 1)
    halo3 = jnp.where(sec == 0, OFF + Y3, OFF - 1)
    edge2 = jnp.where(sec == 0, OFF - 1, OFF + Y2)
    edge3 = jnp.where(sec == 0, OFF - 1, OFF + Y3)
    face_rows = []
    for c in range(3):
        for p in range(1, X + 1):
            face_rows.append((F, c, p, own_row, halo_row))
        for p in (1, 2):
            face_rows.append((F2, c, p, own2, halo2))
            F2[c, p, pl.ds(edge2, 1), :] = zero_row
        face_rows.append((F3, c, 1, own3, halo3))
        F3[c, 1, pl.ds(edge3, 1), :] = zero_row
    for r, (V, c, p, own, halo) in enumerate(face_rows):
        S2[pl.ds(r, 1), :] = V[c, p, pl.ds(own, 1), :]
    for r in range(21, 24):
        S2[pl.ds(r, 1), :] = zero_row
    cross2 = remote(S2, S2R, 11, across)
    cross2.start()
    cross2.wait()
    for r, (V, c, p, own, halo) in enumerate(face_rows):
        V[c, p, pl.ds(halo, 1), :] = S2R[pl.ds(r, 1), :]

    @pl.loop(0, Y // 8)
    def _(i):
        y = pl.multiple_of(i * 8, 8)
        here = pl.ds(y, 8)
        for p in range(1, X + 1):
            w = weights(p, y)
            for c in range(3):
                total, v = neighbours(F, c, p, y, w)
                E[c, p - 1, here, :] = (4.0 / 3.0) * v + INV[c, p - 1, here, :] * total

    @pl.when(has_down)
    def _():
        f_up.wait_recv()
        c_up.wait_recv()

    @pl.when(has_up)
    def _():
        f_down.wait_recv()
        c_down.wait_recv()

    for side, p2, p3, present in ((0, 0, 0, has_down), (1, 3, 2, has_up)):
        for c in range(3):
            v = jnp.where(present, PR[side, pl.ds(half * c, half), :], 0.0)
            F2[c, p2, pl.ds(OFF, half), :] = jnp.where(odd_half, roll(v, 1), v)
            F2[c, p2, pl.ds(OFF + half, half), :] = jnp.where(odd_half, v, roll(v, -1))
            v = jnp.where(present, PR[side, pl.ds(3 * half + 8 * c, 8), :], 0.0)
            for q in range(4):
                spread = v
                for lane in range(4):
                    if lane != q:
                        spread = jnp.where(quad8 == lane, roll(v, lane - q), spread)
                F3[c, p3, pl.ds(OFF + 8 * q, 8), :] = spread

    for c in range(3):
        kx, ky, kz = kinds(c)
        v = F3[c, 1, pl.ds(OFF, Y3), :]
        total = w3[kx, "xl"] * F3[c, 0, pl.ds(OFF, Y3), :] + w3[kx, "xu"] * F3[c, 2, pl.ds(OFF, Y3), :]
        total = total + w3[ky, "yl"] * F3[c, 1, pl.ds(OFF - 1, Y3), :] + w3[ky, "yu"] * F3[c, 1, pl.ds(OFF + 1, Y3), :]
        total = total + w3[kz, "zl"] * from_below(v, 4) + w3[kz, "zu"] * from_above(v, 4)
        e3 = (4.0 / 3.0) * v + inv3[c] * total
        EX[c, 0, pl.ds(0, Y3, stride=2), :] = e3
        EX[c, 0, pl.ds(1, Y3, stride=2), :] = e3
        e3 = EX[c, 0]
        for j in range(2):
            p = 1 + j
            v = F2[c, p, pl.ds(OFF, Y2), :]
            total = W2[kx, j] * F2[c, p - 1, pl.ds(OFF, Y2), :] + W2[kx, j + 1] * F2[c, p + 1, pl.ds(OFF, Y2), :]
            total = total + W2[ky, 3 + j] * F2[c, p, pl.ds(OFF - 1, Y2), :]
            total = total + W2[ky, 5 + j] * F2[c, p, pl.ds(OFF + 1, Y2), :]
            total = total + W2[kz, 7 + j] * from_below(v, 2) + W2[kz, 9 + j] * from_above(v, 2)
            e2 = (4.0 / 3.0) * v + I2[c, j] * total + e3
            R[c, j, pl.ds(0, Y2, stride=2), :] = e2
            R[c, j, pl.ds(1, Y2, stride=2), :] = e2

    @pl.loop(0, Y // 8)
    def _(i):
        y = pl.multiple_of(i * 8, 8)
        here = pl.ds(y, 8)
        there = pl.ds(OFF + y, 8)
        for p, q in ((1, 0), (2, None), (3, None), (4, X + 1)):
            if q is not None:
                s = H[q, there, :] + H[p, there, :]
                t = K[q, there, :] + K[p, there, :]
            for c in range(3):
                value = E[c, p - 1, here, :] + R[c, (p - 1) // 2, here, :]
                if q is not None:
                    w = t if c == 0 else s
                    value = value + INV[c, p - 1, here, :] * (w * F[c, q, there, :])
                out[c, p - 1, here, :] = value

    @pl.when(has_up)
    def _():
        for copy in ups + [f_up, c_up]:
            copy.wait_send()

    @pl.when(has_down)
    def _():
        for copy in downs + [f_down, c_down]:
            copy.wait_send()


def per_device(tiles, load_field, iterate, phase_label, damage):
    f32, i32 = jnp.float32, jnp.int32
    padded = Y + 2 * OFF
    return pl.pallas_call(
        functools.partial(kernel, tiles),
        out_shape=jax.ShapeDtypeStruct(load_field.shape, f32),
        in_specs=[pl.BlockSpec(memory_space=pl.ANY)] * 4,
        out_specs=pl.BlockSpec(memory_space=pltpu.VMEM),
        scratch_shapes=[
            pltpu.VMEM((3, X + 2, padded, Z), f32),
            pltpu.VMEM((3, X + 2, padded, Z), f32),
            pltpu.VMEM((3, X, Y, Z), f32),
            pltpu.VMEM((3, X, Y, Z), f32),
            pltpu.VMEM((3, X // 2, Y, Z), f32),
            pltpu.VMEM((3, X, Y, Z), f32),
            pltpu.VMEM((X + 2, padded, Z), f32),
            pltpu.VMEM((X + 2, padded, Z), f32),
            pltpu.VMEM((X + 2, Y, Z), i32),
            pltpu.VMEM((X + 2, Y, Z), i32),
            pltpu.VMEM((24, Z), f32),
            pltpu.VMEM((24, Z), f32),
            pltpu.VMEM((24, Z), f32),
            pltpu.VMEM((24, Z), f32),
            pltpu.VMEM((2, 120, Z), f32),
            pltpu.VMEM((2, 120, Z), f32),
            pltpu.VMEM((2, 11, Y // 2, Z), f32),
            pltpu.VMEM((3, 4, Y // 2 + 2 * OFF, Z), f32),
            pltpu.VMEM((3, 2, Y // 2, Z), f32),
            pltpu.VMEM((3, 3, Y // 4 + 2 * OFF, Z), f32),
            pltpu.VMEM((3, 2, Y // 2, Z), f32),
            pltpu.SemaphoreType.DMA((4,)),
            pltpu.SemaphoreType.DMA((12,)),
            pltpu.SemaphoreType.DMA((12,)),
        ],
        compiler_params=pltpu.CompilerParams(
            collective_id=0, has_side_effects=True, vmem_limit_bytes=48 * 1024 * 1024),
    )(load_field, iterate, phase_label, damage)


def solution(mesh):
    tiles = mesh.shape["tile"]
    in_specs = (
        P(None, "tile", "sec", None),
        P(None, "tile", "sec", None),
        P("tile", "sec", None),
        P("tile", "sec", None),
    )
    out_specs = P(None, "tile", "sec", None)
    return jax.shard_map(
        functools.partial(per_device, tiles), mesh=mesh, in_specs=in_specs, out_specs=out_specs, check_vma=False
    )
```

```python
import functools

import jax
import jax.numpy as jnp
from jax import lax
from jax.experimental import pallas as pl
from jax.experimental.pallas import tpu as pltpu
from jax.sharding import PartitionSpec as P

shear_table = (1.0, 0.6, 1.8, 0.35)
bulk_table = (1.2, 0.9, 2.5, 0.5)
damage_step = 0.25
damage_floor = 0.01
relaxation = 2.0 / 3.0

MESH = pl.DeviceIdType.MESH
X = 4
Y = 128
Z = 128
PARTS = 4
OFF = 8


def lanes(shape):
    return lax.broadcasted_iota(jnp.int32, shape, len(shape) - 1)


def roll(v, shift):
    return pltpu.roll(v, shift % Z, v.ndim - 1)


def from_above(v, step):
    return jnp.where(lanes(v.shape) < Z - step, roll(v, -step), 0.0)


def from_below(v, step):
    return jnp.where(lanes(v.shape) >= step, roll(v, step), 0.0)


def moduli(phase, damage):
    soft = 1.0 - damage_step * damage.astype(jnp.float32)
    degrade = soft * soft + damage_floor

    def table(values):
        picked = jnp.full(phase.shape, values[3], jnp.float32)
        for label in (2, 1, 0):
            picked = jnp.where(phase == label, values[label], picked)
        return picked

    half = table([0.5 * s for s in shear_table])
    normal = table([0.5 * b + s for s, b in zip(shear_table, bulk_table)])
    return half * degrade, normal * degrade


def kernel(tiles, load_hbm, u_hbm, lab_hbm, dam_hbm, out, U, F, L, INV, R, E, H, K, LAB, DAM, S1, S1R, S2, S2R,
           PS, PR, W2, F2, I2, F3, EX, local_sem, send_sem, recv_sem):
    me = lax.axis_index("tile")
    sec = lax.axis_index("sec")
    odd = lax.rem(me, 2)
    has_far = jnp.logical_and(me > 0, me < tiles - 1)
    near = {"tile": me + 1 - 2 * odd}
    far = {"tile": jnp.clip(me - 1 + 2 * odd, 0, tiles - 1)}
    across = {"sec": 1 - sec}
    p_near, q_near = X - (X - 1) * odd, (X + 1) * (1 - odd)
    p_far, q_far = 1 + (X - 1) * odd, (X + 1) * odd

    barrier = pltpu.get_barrier_semaphore()
    pl.semaphore_signal(barrier, inc=1, device_id=near, device_id_type=MESH)

    @pl.when(has_far)
    def _():
        pl.semaphore_signal(barrier, inc=1, device_id=far, device_id_type=MESH)

    pl.semaphore_signal(barrier, inc=1, device_id=across, device_id_type=MESH)

    loads = [
        pltpu.make_async_copy(lab_hbm, LAB.at[pl.ds(1, X)], local_sem.at[0]),
        pltpu.make_async_copy(dam_hbm, DAM.at[pl.ds(1, X)], local_sem.at[1]),
        pltpu.make_async_copy(u_hbm, U.at[:, pl.ds(1, X), pl.ds(OFF, Y)], local_sem.at[2]),
        pltpu.make_async_copy(load_hbm, L, local_sem.at[3]),
    ]
    for copy in loads:
        copy.start()

    own_row = jnp.where(sec == 0, OFF + Y - 1, OFF)
    halo_row = jnp.where(sec == 0, OFF + Y, OFF - 1)
    edge_row = jnp.where(sec == 0, OFF - 1, OFF + Y)
    faces = [H.at[pl.ds(1, X)], K.at[pl.ds(1, X)]] + [U.at[c, pl.ds(1, X)] for c in range(3)]
    zero_row = jnp.zeros((1, Z), jnp.float32)
    for r in range(20, 24):
        S1[pl.ds(r, 1), :] = zero_row
    for copy in loads[:2]:
        copy.wait()
    for p in range(X):
        h, k = moduli(LAB[1 + p, pl.ds(own_row - OFF, 1), :], DAM[1 + p, pl.ds(own_row - OFF, 1), :])
        S1[pl.ds(p, 1), :] = h
        S1[pl.ds(X + p, 1), :] = k
    loads[2].wait()
    for f in range(2, 5):
        for p in range(X):
            S1[pl.ds(X * f + p, 1), :] = faces[f][p, pl.ds(own_row, 1), :]
    pl.semaphore_wait(barrier, 2 + has_far.astype(jnp.int32))

    def remote(src, dst, index, device):
        return pltpu.make_async_remote_copy(
            src_ref=src, dst_ref=dst, send_sem=send_sem.at[index], recv_sem=recv_sem.at[index],
            device_id=device, device_id_type=MESH)

    rows = pl.ds(OFF, Y)
    part = Y // PARTS
    far1 = []
    for n in range(PARTS):
        here, there = pl.ds(n * part, part), pl.ds(OFF + n * part, part)
        far1.append([
            remote(lab_hbm.at[p_far - 1, here], LAB.at[X + 1 - q_far, here], 3 * n, far),
            remote(dam_hbm.at[p_far - 1, here], DAM.at[X + 1 - q_far, here], 3 * n + 1, far),
            remote(u_hbm.at[:, p_far - 1, here], U.at[:, X + 1 - q_far, there], 3 * n + 2, far),
        ])
    base = 3 * PARTS
    near1 = [
        remote(lab_hbm.at[p_near - 1], LAB.at[X + 1 - q_near], base, near),
        remote(dam_hbm.at[p_near - 1], DAM.at[X + 1 - q_near], base + 1, near),
        remote(u_hbm.at[:, p_near - 1], U.at[:, X + 1 - q_near, rows], base + 2, near),
    ]

    cross1 = remote(S1, S1R, base + 3, across)
    cross1.start()

    @pl.when(has_far)
    def _():
        for copies in far1:
            for copy in copies:
                copy.start()

    for copy in near1:
        copy.start()

    @pl.loop(0, Y // 8)
    def _(i):
        y = pl.multiple_of(i * 8, 8)
        for p in range(1, X + 1):
            h, k = moduli(LAB[p, pl.ds(y, 8), :], DAM[p, pl.ds(y, 8), :])
            H[p, pl.ds(OFF + y, 8), :] = h
            K[p, pl.ds(OFF + y, 8), :] = k

    for ref in faces:
        for p in range(X):
            ref[p, pl.ds(edge_row, 1), :] = zero_row
    for c in range(3):
        for p in range(1, X + 1):
            F[c, p, pl.ds(edge_row, 1), :] = zero_row

    @pl.when(jnp.logical_not(has_far))
    def _():
        for ref in (H, K):
            ref[q_far] = jnp.zeros(H.shape[1:], jnp.float32)
        for c in range(3):
            U[c, q_far] = jnp.zeros(U.shape[2:], jnp.float32)
            F[c, q_far] = jnp.zeros(F.shape[2:], jnp.float32)

    def weights(p, y):
        result = {}
        for name, M in (("s", H), ("t", K)):
            m = M[p, pl.ds(OFF + y, 8), :]
            if p > 1:
                result[name, "xl"] = m + M[p - 1, pl.ds(OFF + y, 8), :]
            if p < X:
                result[name, "xu"] = m + M[p + 1, pl.ds(OFF + y, 8), :]
            result[name, "yl"] = m + M[p, pl.ds(OFF + y - 1, 8), :]
            result[name, "yu"] = m + M[p, pl.ds(OFF + y + 1, 8), :]
            result[name, "zl"] = m + from_below(m, 1)
            result[name, "zu"] = m + from_above(m, 1)
        return result

    def neighbours(V, c, p, y, w):
        v = V[c, p, pl.ds(OFF + y, 8), :]
        kind = ["t" if c == a else "s" for a in range(3)]
        total = w[kind[1], "yl"] * V[c, p, pl.ds(OFF + y - 1, 8), :]
        total = total + w[kind[1], "yu"] * V[c, p, pl.ds(OFF + y + 1, 8), :]
        total = total + w[kind[2], "zl"] * from_below(v, 1)
        total = total + w[kind[2], "zu"] * from_above(v, 1)
        if p > 1:
            total = total + w[kind[0], "xl"] * V[c, p - 1, pl.ds(OFF + y, 8), :]
        if p < X:
            total = total + w[kind[0], "xu"] * V[c, p + 1, pl.ds(OFF + y, 8), :]
        return total, v

    def inner_residual(y):
        here = pl.ds(y, 8)
        for p in range(1, X + 1):
            w = weights(p, y)
            sides = {}
            for name in ("s", "t"):
                xs = [w[name, side] for side in ("xl", "xu") if (name, side) in w]
                sides[name, 0] = xs[0] if len(xs) == 1 else xs[0] + xs[1]
                sides[name, 1] = w[name, "yl"] + w[name, "yu"]
                sides[name, 2] = w[name, "zl"] + w[name, "zu"]
            for c in range(3):
                total, v = neighbours(U, c, p, y, w)
                others = [a for a in range(3) if a != c]
                diag = sides["t", c] + sides["s", others[0]] + sides["s", others[1]]
                acc = L[c, p - 1, here, :] + total
                if 1 < p < X:
                    r = acc - diag * v
                    inv = relaxation / diag
                    R[c, p - 2, here, :] = r
                    INV[c, p - 1, here, :] = inv
                    F[c, p, pl.ds(OFF + y, 8), :] = r * inv
                else:
                    L[c, p - 1, here, :] = acc
                    INV[c, p - 1, here, :] = diag

    halo_chunk = pl.multiple_of((1 - sec) * (Y - 8), 8)
    loads[3].wait()

    @pl.loop(0, Y // 8 - 1)
    def _(i):
        inner_residual(pl.multiple_of((i + sec) * 8, 8))

    cross1.wait()
    for f, ref in enumerate(faces):
        for p in range(X):
            ref[p, pl.ds(halo_row, 1), :] = S1R[pl.ds(X * f + p, 1), :]
    inner_residual(halo_chunk)

    def outer_face(p, q, y, present):
        here, there = pl.ds(y, 8), pl.ds(OFF + y, 8)
        h, k = moduli(LAB[q, here, :], DAM[q, here, :])
        if present is not None:
            h = jnp.where(present, h, 0.0)
            k = jnp.where(present, k, 0.0)
        H[q, there, :] = h
        K[q, there, :] = k
        s = h + H[p, there, :]
        t = k + K[p, there, :]
        j = (p - 1) // 2
        for c in range(3):
            w = t if c == 0 else s
            diag = INV[c, p - 1, here, :] + w
            r = L[c, p - 1, here, :] + w * U[c, q, there, :] - diag * U[c, p, there, :]
            inv = relaxation / diag
            INV[c, p - 1, here, :] = inv
            F[c, p, there, :] = r * inv
            R[c, j, here, :] = R[c, j, here, :] + r

    for copy in near1:
        copy.wait_recv()

    @pl.loop(0, Y // 8)
    def _(i):
        outer_face(p_near, q_near, pl.multiple_of(i * 8, 8), None)

    f_near = remote(F.at[:, p_near, rows], F.at[:, X + 1 - q_near, rows], base + 4, near)
    f_near.start()
    f_far = []
    for n in range(PARTS):
        @pl.when(has_far)
        def _():
            for copy in far1[n]:
                copy.wait_recv()

        @pl.loop(0, part // 8)
        def _(i):
            outer_face(p_far, q_far, pl.multiple_of(n * part + i * 8, 8), has_far)

        there = pl.ds(OFF + n * part, part)
        f_far.append(remote(F.at[:, p_far, there], F.at[:, X + 1 - q_far, there], base + 5 + n, far))

        @pl.when(has_far)
        def _():
            f_far[n].start()

    base = base + 5 + PARTS

    Y2, Y3 = Y // 2, Y // 4
    shape2, shape3 = (Y2, Z), (Y3, Z)
    odd2 = (lanes(shape2) & 1) == 1

    def pairs(v):
        return v + jnp.where(odd2, roll(v, 1), roll(v, -1))

    def every_other(M, p, first):
        return M[p, pl.ds(first, Y2, stride=2), :]

    for m, M in enumerate((H, K)):
        for j in range(3):
            face = every_other(M, 2 * j, OFF) + every_other(M, 2 * j, OFF + 1)
            face = face + every_other(M, 2 * j + 1, OFF) + every_other(M, 2 * j + 1, OFF + 1)
            W2[m, j] = pairs(face)
        for j in range(2):
            r7, r8, r9, r10 = [
                every_other(M, 1 + 2 * j, OFF + d) + every_other(M, 2 + 2 * j, OFF + d) for d in (-1, 0, 1, 2)]
            W2[m, 3 + j] = pairs(r7 + r8)
            W2[m, 5 + j] = pairs(r9 + r10)
            cell = r8 + r9
            low = cell + from_below(cell, 1)
            high = cell + from_above(cell, 1)
            W2[m, 7 + j] = jnp.where(odd2, roll(low, 1), low)
            W2[m, 9 + j] = jnp.where(odd2, high, roll(high, -1))

    def kinds(c):
        return [1 if c == a else 0 for a in range(3)]

    for c in range(3):
        kx, ky, kz = kinds(c)
        for j in range(2):
            diag = W2[kx, j] + W2[kx, j + 1] + W2[ky, 3 + j] + W2[ky, 5 + j] + W2[kz, 7 + j] + W2[kz, 9 + j]
            inv = relaxation / diag
            I2[c, j] = inv
            res = R[c, j, pl.ds(0, Y2, stride=2), :] + R[c, j, pl.ds(1, Y2, stride=2), :]
            res = pairs(res)
            EX[c, j] = res
            F2[c, 1 + j, pl.ds(OFF, Y2), :] = res * inv

    quad = lanes(shape3) & 3
    high3 = quad >= 2

    def quads(v):
        return v + jnp.where(high3, roll(v, 2), roll(v, -2))

    def row_of(m, slot, first):
        return W2[m, slot, pl.ds(first, Y3, stride=2), :]

    w3 = {}
    for m in range(2):
        w3[m, "xl"] = quads(row_of(m, 0, 0) + row_of(m, 0, 1))
        w3[m, "xu"] = quads(row_of(m, 2, 0) + row_of(m, 2, 1))
        w3[m, "yl"] = quads(row_of(m, 3, 0) + row_of(m, 4, 0))
        w3[m, "yu"] = quads(row_of(m, 5, 1) + row_of(m, 6, 1))
        low = row_of(m, 7, 0) + row_of(m, 7, 1) + row_of(m, 8, 0) + row_of(m, 8, 1)
        high = row_of(m, 9, 0) + row_of(m, 9, 1) + row_of(m, 10, 0) + row_of(m, 10, 1)
        w3[m, "zl"] = jnp.where(high3, roll(low, 2), low)
        w3[m, "zu"] = jnp.where(high3, high, roll(high, -2))
    inv3 = []
    for c in range(3):
        kx, ky, kz = kinds(c)
        diag = w3[kx, "xl"] + w3[kx, "xu"] + w3[ky, "yl"] + w3[ky, "yu"] + w3[kz, "zl"] + w3[kz, "zu"]
        inv3.append(relaxation / diag)
        res = EX[c, 0, pl.ds(0, Y3, stride=2), :] + EX[c, 0, pl.ds(1, Y3, stride=2), :]
        res = res + EX[c, 1, pl.ds(0, Y3, stride=2), :] + EX[c, 1, pl.ds(1, Y3, stride=2), :]
        F3[c, 1, pl.ds(OFF, Y3), :] = quads(res) * inv3[c]

    half = Y2 // 2
    odd_half = odd2[:half]
    quad8 = quad[:8]
    for side, p2 in ((0, 2 - odd), (1, 1 + odd)):
        for c in range(3):
            a = F2[c, p2, pl.ds(OFF, half), :]
            b = F2[c, p2, pl.ds(OFF + half, half), :]
            PS[side, pl.ds(half * c, half), :] = jnp.where(odd_half, b, a)
            v = F3[c, 1, pl.ds(OFF, 8), :]
            for q in range(1, 4):
                v = jnp.where(quad8 == q, F3[c, 1, pl.ds(OFF + 8 * q, 8), :], v)
            PS[side, pl.ds(3 * half + 8 * c, 8), :] = v
    c_near = remote(PS.at[0], PR.at[0], base, near)
    c_far = remote(PS.at[1], PR.at[1], base + 1, far)

    @pl.when(has_far)
    def _():
        c_far.start()

    c_near.start()

    own2 = jnp.where(sec == 0, OFF + Y2 - 1, OFF)
    own3 = jnp.where(sec == 0, OFF + Y3 - 1, OFF)
    halo2 = jnp.where(sec == 0, OFF + Y2, OFF - 1)
    halo3 = jnp.where(sec == 0, OFF + Y3, OFF - 1)
    edge2 = jnp.where(sec == 0, OFF - 1, OFF + Y2)
    edge3 = jnp.where(sec == 0, OFF - 1, OFF + Y3)
    face_rows = []
    for c in range(3):
        for p in range(1, X + 1):
            face_rows.append((F, c, p, own_row, halo_row))
        for p in (1, 2):
            face_rows.append((F2, c, p, own2, halo2))
            F2[c, p, pl.ds(edge2, 1), :] = zero_row
        face_rows.append((F3, c, 1, own3, halo3))
        F3[c, 1, pl.ds(edge3, 1), :] = zero_row
    for r, (V, c, p, own, halo) in enumerate(face_rows):
        S2[pl.ds(r, 1), :] = V[c, p, pl.ds(own, 1), :]
    for r in range(21, 24):
        S2[pl.ds(r, 1), :] = zero_row
    cross2 = remote(S2, S2R, base + 2, across)
    cross2.start()

    def inner_sweep(y):
        here = pl.ds(y, 8)
        for p in range(1, X + 1):
            w = weights(p, y)
            for c in range(3):
                total, v = neighbours(F, c, p, y, w)
                E[c, p - 1, here, :] = (4.0 / 3.0) * v + INV[c, p - 1, here, :] * total

    def outer_sweep(p, q, y):
        here, there = pl.ds(y, 8), pl.ds(OFF + y, 8)
        s = H[q, there, :] + H[p, there, :]
        t = K[q, there, :] + K[p, there, :]
        for c in range(3):
            w = t if c == 0 else s
            E[c, p - 1, here, :] = E[c, p - 1, here, :] + INV[c, p - 1, here, :] * (w * F[c, q, there, :])

    f_near.wait_recv()

    @pl.loop(0, Y // 8 - 1)
    def _(i):
        y = pl.multiple_of((i + sec) * 8, 8)
        inner_sweep(y)
        outer_sweep(p_near, q_near, y)

    for n in range(PARTS):
        @pl.when(has_far)
        def _():
            f_far[n].wait_recv()

        @pl.loop(0, part // 8)
        def _(i):
            y = pl.multiple_of(n * part + i * 8, 8)

            @pl.when(y != halo_chunk)
            def _():
                outer_sweep(p_far, q_far, y)

    cross2.wait()
    for r, (V, c, p, own, halo) in enumerate(face_rows):
        V[c, p, pl.ds(halo, 1), :] = S2R[pl.ds(r, 1), :]
    inner_sweep(halo_chunk)
    outer_sweep(p_near, q_near, halo_chunk)
    outer_sweep(p_far, q_far, halo_chunk)

    c_near.wait_recv()

    @pl.when(has_far)
    def _():
        c_far.wait_recv()

    for side, p2, p3, present in ((0, 3 * (1 - odd), 2 * (1 - odd), True), (1, 3 * odd, 2 * odd, has_far)):
        for c in range(3):
            v = jnp.where(present, PR[side, pl.ds(half * c, half), :], 0.0)
            F2[c, p2, pl.ds(OFF, half), :] = jnp.where(odd_half, roll(v, 1), v)
            F2[c, p2, pl.ds(OFF + half, half), :] = jnp.where(odd_half, v, roll(v, -1))
            v = jnp.where(present, PR[side, pl.ds(3 * half + 8 * c, 8), :], 0.0)
            for q in range(4):
                spread = v
                for lane in range(4):
                    if lane != q:
                        spread = jnp.where(quad8 == lane, roll(v, lane - q), spread)
                F3[c, p3, pl.ds(OFF + 8 * q, 8), :] = spread

    for c in range(3):
        kx, ky, kz = kinds(c)
        v = F3[c, 1, pl.ds(OFF, Y3), :]
        total = w3[kx, "xl"] * F3[c, 0, pl.ds(OFF, Y3), :] + w3[kx, "xu"] * F3[c, 2, pl.ds(OFF, Y3), :]
        total = total + w3[ky, "yl"] * F3[c, 1, pl.ds(OFF - 1, Y3), :] + w3[ky, "yu"] * F3[c, 1, pl.ds(OFF + 1, Y3), :]
        total = total + w3[kz, "zl"] * from_below(v, 4) + w3[kz, "zu"] * from_above(v, 4)
        e3 = (4.0 / 3.0) * v + inv3[c] * total
        EX[c, 0, pl.ds(0, Y3, stride=2), :] = e3
        EX[c, 0, pl.ds(1, Y3, stride=2), :] = e3
        e3 = EX[c, 0]
        for j in range(2):
            p = 1 + j
            v = F2[c, p, pl.ds(OFF, Y2), :]
            total = W2[kx, j] * F2[c, p - 1, pl.ds(OFF, Y2), :] + W2[kx, j + 1] * F2[c, p + 1, pl.ds(OFF, Y2), :]
            total = total + W2[ky, 3 + j] * F2[c, p, pl.ds(OFF - 1, Y2), :]
            total = total + W2[ky, 5 + j] * F2[c, p, pl.ds(OFF + 1, Y2), :]
            total = total + W2[kz, 7 + j] * from_below(v, 2) + W2[kz, 9 + j] * from_above(v, 2)
            e2 = (4.0 / 3.0) * v + I2[c, j] * total + e3
            R[c, j, pl.ds(0, Y2, stride=2), :] = e2
            R[c, j, pl.ds(1, Y2, stride=2), :] = e2

    @pl.loop(0, Y // 8)
    def _(i):
        y = pl.multiple_of(i * 8, 8)
        here = pl.ds(y, 8)
        for p in range(X):
            for c in range(3):
                out[c, p, here, :] = E[c, p, here, :] + R[c, p // 2, here, :]

    for copy in near1 + [f_near, c_near]:
        copy.wait_send()

    @pl.when(has_far)
    def _():
        for copy in [copy for copies in far1 for copy in copies] + f_far + [c_far]:
            copy.wait_send()


def per_device(tiles, load_field, iterate, phase_label, damage):
    f32, i32 = jnp.float32, jnp.int32
    padded = Y + 2 * OFF
    return pl.pallas_call(
        functools.partial(kernel, tiles),
        out_shape=jax.ShapeDtypeStruct(load_field.shape, f32),
        in_specs=[pl.BlockSpec(memory_space=pltpu.HBM)] * 4,
        out_specs=pl.BlockSpec(memory_space=pltpu.VMEM),
        scratch_shapes=[
            pltpu.VMEM((3, X + 2, padded, Z), f32),
            pltpu.VMEM((3, X + 2, padded, Z), f32),
            pltpu.VMEM((3, X, Y, Z), f32),
            pltpu.VMEM((3, X, Y, Z), f32),
            pltpu.VMEM((3, X // 2, Y, Z), f32),
            pltpu.VMEM((3, X, Y, Z), f32),
            pltpu.VMEM((X + 2, padded, Z), f32),
            pltpu.VMEM((X + 2, padded, Z), f32),
            pltpu.VMEM((X + 2, Y, Z), i32),
            pltpu.VMEM((X + 2, Y, Z), i32),
            pltpu.VMEM((24, Z), f32),
            pltpu.VMEM((24, Z), f32),
            pltpu.VMEM((24, Z), f32),
            pltpu.VMEM((24, Z), f32),
            pltpu.VMEM((2, 120, Z), f32),
            pltpu.VMEM((2, 120, Z), f32),
            pltpu.VMEM((2, 11, Y // 2, Z), f32),
            pltpu.VMEM((3, 4, Y // 2 + 2 * OFF, Z), f32),
            pltpu.VMEM((3, 2, Y // 2, Z), f32),
            pltpu.VMEM((3, 3, Y // 4 + 2 * OFF, Z), f32),
            pltpu.VMEM((3, 2, Y // 2, Z), f32),
            pltpu.SemaphoreType.DMA((4,)),
            pltpu.SemaphoreType.DMA((4 * PARTS + 8,)),
            pltpu.SemaphoreType.DMA((4 * PARTS + 8,)),
        ],
        compiler_params=pltpu.CompilerParams(
            collective_id=0, has_side_effects=True, vmem_limit_bytes=48 * 1024 * 1024),
    )(*[pltpu.with_memory_space_constraint(a, pltpu.HBM) for a in (load_field, iterate, phase_label, damage)])


def solution(mesh):
    tiles = mesh.shape["tile"]
    in_specs = (
        P(None, "tile", "sec", None),
        P(None, "tile", "sec", None),
        P("tile", "sec", None),
        P("tile", "sec", None),
    )
    out_specs = P(None, "tile", "sec", None)
    return jax.shard_map(
        functools.partial(per_device, tiles), mesh=mesh, in_specs=in_specs, out_specs=out_specs, check_vma=False
    )
```

```python
import functools

import jax
import jax.numpy as jnp
from jax import lax
from jax.experimental import pallas as pl
from jax.experimental.pallas import tpu as pltpu
from jax.sharding import PartitionSpec as P

shear_table = (1.0, 0.6, 1.8, 0.35)
bulk_table = (1.2, 0.9, 2.5, 0.5)
damage_step = 0.25
damage_floor = 0.01
relaxation = 2.0 / 3.0

MESH = pl.DeviceIdType.MESH
X = 4
Y = 128
Z = 128
PARTS = 4
OFF = 8


def lanes(shape):
    return lax.broadcasted_iota(jnp.int32, shape, len(shape) - 1)


def roll(v, shift):
    return pltpu.roll(v, shift % Z, v.ndim - 1)


def from_above(v, step):
    return jnp.where(lanes(v.shape) < Z - step, roll(v, -step), 0.0)


def from_below(v, step):
    return jnp.where(lanes(v.shape) >= step, roll(v, step), 0.0)


def moduli(phase, damage):
    soft = 1.0 - damage_step * damage.astype(jnp.float32)
    degrade = soft * soft + damage_floor

    def table(values):
        picked = jnp.full(phase.shape, values[3], jnp.float32)
        for label in (2, 1, 0):
            picked = jnp.where(phase == label, values[label], picked)
        return picked

    half = table([0.5 * s for s in shear_table])
    normal = table([0.5 * b + s for s, b in zip(shear_table, bulk_table)])
    return half * degrade, normal * degrade


def kernel(tiles, load_hbm, u_hbm, lab_hbm, dam_hbm, out, U, F, L, INV, R, E, H, K, LAB, DAM, S1, S1R, S2, S2R,
           PN, QN, PF, QF, W2, F2, I2, W3, F3, I3, EX, local_sem, send_sem, recv_sem):
    me = lax.axis_index("tile")
    sec = lax.axis_index("sec")
    odd = lax.rem(me, 2)
    has_far = jnp.logical_and(me > 0, me < tiles - 1)
    near = {"tile": me + 1 - 2 * odd}
    far = {"tile": jnp.clip(me - 1 + 2 * odd, 0, tiles - 1)}
    across = {"sec": 1 - sec}
    p_near, q_near = X - (X - 1) * odd, (X + 1) * (1 - odd)
    p_far, q_far = 1 + (X - 1) * odd, (X + 1) * odd

    barrier = pltpu.get_barrier_semaphore()
    pl.semaphore_signal(barrier, inc=1, device_id=near, device_id_type=MESH)

    @pl.when(has_far)
    def _():
        pl.semaphore_signal(barrier, inc=1, device_id=far, device_id_type=MESH)

    pl.semaphore_signal(barrier, inc=1, device_id=across, device_id_type=MESH)

    loads = [
        pltpu.make_async_copy(lab_hbm, LAB.at[pl.ds(1, X)], local_sem.at[0]),
        pltpu.make_async_copy(dam_hbm, DAM.at[pl.ds(1, X)], local_sem.at[1]),
        pltpu.make_async_copy(u_hbm, U.at[:, pl.ds(1, X), pl.ds(OFF, Y)], local_sem.at[2]),
        pltpu.make_async_copy(load_hbm, L, local_sem.at[3]),
    ]
    for copy in loads:
        copy.start()

    own_row = jnp.where(sec == 0, OFF + Y - 1, OFF)
    halo_row = jnp.where(sec == 0, OFF + Y, OFF - 1)
    edge_row = jnp.where(sec == 0, OFF - 1, OFF + Y)
    faces = [H.at[pl.ds(1, X)], K.at[pl.ds(1, X)]] + [U.at[c, pl.ds(1, X)] for c in range(3)]
    zero_row = jnp.zeros((1, Z), jnp.float32)
    for r in range(20, 24):
        S1[pl.ds(r, 1), :] = zero_row
    for copy in loads[:2]:
        copy.wait()
    for p in range(X):
        h, k = moduli(LAB[1 + p, pl.ds(own_row - OFF, 1), :], DAM[1 + p, pl.ds(own_row - OFF, 1), :])
        S1[pl.ds(p, 1), :] = h
        S1[pl.ds(X + p, 1), :] = k
    loads[2].wait()
    for f in range(2, 5):
        for p in range(X):
            S1[pl.ds(X * f + p, 1), :] = faces[f][p, pl.ds(own_row, 1), :]
    pl.semaphore_wait(barrier, 2 + has_far.astype(jnp.int32))

    def remote(src, dst, index, device):
        return pltpu.make_async_remote_copy(
            src_ref=src, dst_ref=dst, send_sem=send_sem.at[index], recv_sem=recv_sem.at[index],
            device_id=device, device_id_type=MESH)

    rows = pl.ds(OFF, Y)
    part = Y // PARTS
    base = 5 * PARTS

    def part_of(k):
        n = k + (1 - sec) * (PARTS - 1 - 2 * k)
        return pl.multiple_of(n * part, part)

    def far1(k):
        y = part_of(k)
        here, there = pl.ds(y, part), pl.ds(OFF + y, part)
        return [
            remote(lab_hbm.at[p_far - 1, here], LAB.at[X + 1 - q_far, here], 3 * k, far),
            remote(dam_hbm.at[p_far - 1, here], DAM.at[X + 1 - q_far, here], 3 * k + 1, far),
            remote(u_hbm.at[:, p_far - 1, here], U.at[:, X + 1 - q_far, there], 3 * k + 2, far),
        ]

    def f_far(k):
        there = pl.ds(OFF + part_of(k), part)
        return remote(F.at[:, p_far, there], F.at[:, X + 1 - q_far, there], 3 * PARTS + k, far)

    def c_far(k):
        return remote(PF.at[k], QF.at[k], 4 * PARTS + k, far)

    near1 = [
        remote(lab_hbm.at[p_near - 1], LAB.at[X + 1 - q_near], base, near),
        remote(dam_hbm.at[p_near - 1], DAM.at[X + 1 - q_near], base + 1, near),
        remote(u_hbm.at[:, p_near - 1], U.at[:, X + 1 - q_near, rows], base + 2, near),
    ]
    cross1 = remote(S1, S1R, base + 3, across)
    cross1.start()

    @pl.when(has_far)
    def _():
        for k in range(PARTS):
            for copy in far1(k):
                copy.start()

    for copy in near1:
        copy.start()

    @pl.loop(0, Y // 8)
    def _(i):
        y = pl.multiple_of(i * 8, 8)
        for p in range(1, X + 1):
            h, k = moduli(LAB[p, pl.ds(y, 8), :], DAM[p, pl.ds(y, 8), :])
            H[p, pl.ds(OFF + y, 8), :] = h
            K[p, pl.ds(OFF + y, 8), :] = k

    for ref in faces:
        for p in range(X):
            ref[p, pl.ds(edge_row, 1), :] = zero_row
    for c in range(3):
        for p in range(1, X + 1):
            F[c, p, pl.ds(edge_row, 1), :] = zero_row

    @pl.when(jnp.logical_not(has_far))
    def _():
        for ref in (H, K):
            ref[q_far] = jnp.zeros(H.shape[1:], jnp.float32)
        for c in range(3):
            U[c, q_far] = jnp.zeros(U.shape[2:], jnp.float32)
            F[c, q_far] = jnp.zeros(F.shape[2:], jnp.float32)

    def weights(p, y):
        result = {}
        for name, M in (("s", H), ("t", K)):
            m = M[p, pl.ds(OFF + y, 8), :]
            if p > 1:
                result[name, "xl"] = m + M[p - 1, pl.ds(OFF + y, 8), :]
            if p < X:
                result[name, "xu"] = m + M[p + 1, pl.ds(OFF + y, 8), :]
            result[name, "yl"] = m + M[p, pl.ds(OFF + y - 1, 8), :]
            result[name, "yu"] = m + M[p, pl.ds(OFF + y + 1, 8), :]
            result[name, "zl"] = m + from_below(m, 1)
            result[name, "zu"] = m + from_above(m, 1)
        return result

    def neighbours(V, c, p, y, w):
        v = V[c, p, pl.ds(OFF + y, 8), :]
        kind = ["t" if c == a else "s" for a in range(3)]
        total = w[kind[1], "yl"] * V[c, p, pl.ds(OFF + y - 1, 8), :]
        total = total + w[kind[1], "yu"] * V[c, p, pl.ds(OFF + y + 1, 8), :]
        total = total + w[kind[2], "zl"] * from_below(v, 1)
        total = total + w[kind[2], "zu"] * from_above(v, 1)
        if p > 1:
            total = total + w[kind[0], "xl"] * V[c, p - 1, pl.ds(OFF + y, 8), :]
        if p < X:
            total = total + w[kind[0], "xu"] * V[c, p + 1, pl.ds(OFF + y, 8), :]
        return total, v

    def inner_residual(y):
        here = pl.ds(y, 8)
        for p in range(1, X + 1):
            w = weights(p, y)
            sides = {}
            for name in ("s", "t"):
                xs = [w[name, side] for side in ("xl", "xu") if (name, side) in w]
                sides[name, 0] = xs[0] if len(xs) == 1 else xs[0] + xs[1]
                sides[name, 1] = w[name, "yl"] + w[name, "yu"]
                sides[name, 2] = w[name, "zl"] + w[name, "zu"]
            for c in range(3):
                total, v = neighbours(U, c, p, y, w)
                others = [a for a in range(3) if a != c]
                diag = sides["t", c] + sides["s", others[0]] + sides["s", others[1]]
                acc = L[c, p - 1, here, :] + total
                if 1 < p < X:
                    r = acc - diag * v
                    inv = relaxation / diag
                    R[c, p - 2, here, :] = r
                    INV[c, p - 1, here, :] = inv
                    F[c, p, pl.ds(OFF + y, 8), :] = r * inv
                else:
                    L[c, p - 1, here, :] = acc
                    INV[c, p - 1, here, :] = diag

    halo_chunk = pl.multiple_of((1 - sec) * (Y - 8), 8)
    loads[3].wait()

    @pl.loop(0, Y // 8 - 1)
    def _(i):
        inner_residual(pl.multiple_of((i + sec) * 8, 8))

    cross1.wait()
    for f, ref in enumerate(faces):
        for p in range(X):
            ref[p, pl.ds(halo_row, 1), :] = S1R[pl.ds(X * f + p, 1), :]
    inner_residual(halo_chunk)

    def outer_face(p, q, y, present):
        here, there = pl.ds(y, 8), pl.ds(OFF + y, 8)
        h, k = moduli(LAB[q, here, :], DAM[q, here, :])
        if present is not None:
            h = jnp.where(present, h, 0.0)
            k = jnp.where(present, k, 0.0)
        H[q, there, :] = h
        K[q, there, :] = k
        s = h + H[p, there, :]
        t = k + K[p, there, :]
        j = (p - 1) // 2
        for c in range(3):
            w = t if c == 0 else s
            diag = INV[c, p - 1, here, :] + w
            r = L[c, p - 1, here, :] + w * U[c, q, there, :] - diag * U[c, p, there, :]
            inv = relaxation / diag
            INV[c, p - 1, here, :] = inv
            F[c, p, there, :] = r * inv
            R[c, j, here, :] = R[c, j, here, :] + r

    for copy in near1:
        copy.wait_recv()

    @pl.loop(0, Y // 8)
    def _(i):
        outer_face(p_near, q_near, pl.multiple_of(i * 8, 8), None)

    f_near = remote(F.at[:, p_near, rows], F.at[:, X + 1 - q_near, rows], base + 4, near)
    f_near.start()

    Y2, Y3 = Y // 2, Y // 4
    part2, part3 = part // 2, part // 4
    shape2, shape3 = (part2, Z), (part3, Z)
    odd2 = (lanes(shape2) & 1) == 1
    quad = lanes(shape3) & 3
    high3 = quad >= 2
    j_near, j_far = 1 - odd, odd

    def pairs(v):
        return v + jnp.where(odd2, roll(v, 1), roll(v, -1))

    def quads(v):
        return v + jnp.where(high3, roll(v, 2), roll(v, -2))

    def fine_rows(M, p, first):
        return M[p, pl.ds(first, part2, stride=2), :]

    def coarse_rows(m, slot, y2, first):
        return W2[m, slot, pl.ds(y2 + first, part3, stride=2), :]

    def kinds(c):
        return [1 if c == a else 0 for a in range(3)]

    def x_face(M, p, q, y):
        face = fine_rows(M, p, OFF + y) + fine_rows(M, p, OFF + y + 1)
        return pairs(face + fine_rows(M, q, OFF + y) + fine_rows(M, q, OFF + y + 1))

    def residual_two(c, j, y):
        return pairs(fine_rows(R.at[c], j, y) + fine_rows(R.at[c], j, y + 1))

    @pl.loop(0, PARTS)
    def _(n):
        y = pl.multiple_of(n * part, part)
        y2 = pl.multiple_of(n * part2, part2)
        y3 = pl.multiple_of(n * part3, part3)
        at2, at3 = pl.ds(y2, part2), pl.ds(y3, part3)
        sides = {}
        for m, M in enumerate((H, K)):
            mid = x_face(M, 2, 3, y)
            close = x_face(M, p_near, q_near, y)
            W2[m, 1, at2, :] = mid
            W2[m, 2 - 2 * odd, at2, :] = close
            W3[m, 1 - odd, at3, :] = quads(
                coarse_rows(m, 2 - 2 * odd, y2, 0) + coarse_rows(m, 2 - 2 * odd, y2, 1))
            for j in range(2):
                r7, r8, r9, r10 = [
                    fine_rows(M, 1 + 2 * j, OFF + y + d) + fine_rows(M, 2 + 2 * j, OFF + y + d) for d in (-1, 0, 1, 2)]
                yl, yu = pairs(r7 + r8), pairs(r9 + r10)
                cell = r8 + r9
                low = cell + from_below(cell, 1)
                high = cell + from_above(cell, 1)
                zl = jnp.where(odd2, roll(low, 1), low)
                zu = jnp.where(odd2, high, roll(high, -1))
                for slot, value in ((3, yl), (5, yu), (7, zl), (9, zu)):
                    W2[m, slot + j, at2, :] = value
                sides[m, j, 0] = mid
                sides[m, j, 1] = yl + yu
                sides[m, j, 2] = zl + zu
            W3[m, 2, at3, :] = quads(coarse_rows(m, 3, y2, 0) + coarse_rows(m, 4, y2, 0))
            W3[m, 3, at3, :] = quads(coarse_rows(m, 5, y2, 1) + coarse_rows(m, 6, y2, 1))
            low = coarse_rows(m, 7, y2, 0) + coarse_rows(m, 7, y2, 1)
            low = low + coarse_rows(m, 8, y2, 0) + coarse_rows(m, 8, y2, 1)
            high = coarse_rows(m, 9, y2, 0) + coarse_rows(m, 9, y2, 1)
            high = high + coarse_rows(m, 10, y2, 0) + coarse_rows(m, 10, y2, 1)
            W3[m, 4, at3, :] = jnp.where(high3, roll(low, 2), low)
            W3[m, 5, at3, :] = jnp.where(high3, high, roll(high, -2))
        for c in range(3):
            kx, ky, kz = kinds(c)
            for j in range(2):
                I2[c, j, at2, :] = sides[kx, j, 0] + sides[ky, j, 1] + sides[kz, j, 2]
            inv = relaxation / (I2[c, j_near, at2, :] + W2[kx, 2 - 2 * odd, at2, :])
            I2[c, j_near, at2, :] = inv
            res = residual_two(c, j_near, y)
            EX[c, j_near, at2, :] = res
            F2[c, 1 + j_near, pl.ds(OFF + y2, part2), :] = res * inv
            I3[c, at3, :] = (W3[kx, 1 - odd, at3, :] + W3[ky, 2, at3, :] + W3[ky, 3, at3, :]
                             + W3[kz, 4, at3, :] + W3[kz, 5, at3, :])

    half = part2 // 2
    odd_half = odd2[:half]

    def packed(V, c, p, y2):
        return jnp.where(odd_half, V[c, p, pl.ds(OFF + y2 + half, half), :], V[c, p, pl.ds(OFF + y2, half), :])

    own2 = jnp.where(sec == 0, OFF + Y2 - 1, OFF)
    own3 = jnp.where(sec == 0, OFF + Y3 - 1, OFF)
    halo2 = jnp.where(sec == 0, OFF + Y2, OFF - 1)
    halo3 = jnp.where(sec == 0, OFF + Y3, OFF - 1)
    edge2 = jnp.where(sec == 0, OFF - 1, OFF + Y2)
    edge3 = jnp.where(sec == 0, OFF - 1, OFF + Y3)
    face_rows = []
    for c in range(3):
        for p in range(1, X + 1):
            face_rows.append((F, c, p, own_row, halo_row))
        for p in (1, 2):
            face_rows.append((F2, c, p, own2, halo2))
            F2[c, p, pl.ds(edge2, 1), :] = zero_row
        face_rows.append((F3, c, 1, own3, halo3))
        F3[c, 1, pl.ds(edge3, 1), :] = zero_row
    for r in range(21, 24):
        S2[pl.ds(r, 1), :] = zero_row
    cross2 = remote(S2, S2R, base + 5, across)

    @pl.loop(0, PARTS)
    def _(k):
        y = part_of(k)

        @pl.when(has_far)
        def _():
            for copy in far1(k):
                copy.wait_recv()

        for i in range(part // 8):
            outer_face(p_far, q_far, pl.multiple_of(y + i * 8, 8), has_far)

        @pl.when(has_far)
        def _():
            f_far(k).start()

        y2, y3 = pl.multiple_of(y // 2, part2), pl.multiple_of(y // 4, part3)
        at2, at3 = pl.ds(y2, part2), pl.ds(y3, part3)
        for m, M in enumerate((H, K)):
            W2[m, 2 * odd, at2, :] = x_face(M, p_far, q_far, y)
            W3[m, odd, at3, :] = quads(coarse_rows(m, 2 * odd, y2, 0) + coarse_rows(m, 2 * odd, y2, 1))
        deep = jnp.zeros(shape3, jnp.float32)
        for c in range(3):
            kx = kinds(c)[0]
            inv = relaxation / (I2[c, j_far, at2, :] + W2[kx, 2 * odd, at2, :])
            I2[c, j_far, at2, :] = inv
            res = residual_two(c, j_far, y)
            EX[c, j_far, at2, :] = res
            F2[c, 1 + j_far, pl.ds(OFF + y2, part2), :] = res * inv
            inv = relaxation / (I3[c, at3, :] + W3[kx, odd, at3, :])
            I3[c, at3, :] = inv
            res = EX[c, 0, pl.ds(y2, part3, stride=2), :] + EX[c, 0, pl.ds(y2 + 1, part3, stride=2), :]
            res = res + EX[c, 1, pl.ds(y2, part3, stride=2), :] + EX[c, 1, pl.ds(y2 + 1, part3, stride=2), :]
            first = quads(res) * inv
            F3[c, 1, pl.ds(OFF + y3, part3), :] = first
            deep = jnp.where(quad == c, first, deep)
            PF[k, pl.ds(half * c, half), :] = packed(F2, c, 1 + j_far, y2)
            PN[k, pl.ds(half * c, half), :] = packed(F2, c, 1 + j_near, y2)
        PF[k, pl.ds(3 * half, part3), :] = deep
        PN[k, pl.ds(3 * half, part3), :] = deep

        @pl.when(has_far)
        def _():
            c_far(k).start()

        @pl.when(k == 0)
        def _():
            for r, (V, c, p, own, halo) in enumerate(face_rows):
                S2[pl.ds(r, 1), :] = V[c, p, pl.ds(own, 1), :]
            cross2.start()

    c_near = remote(PN, QN, base + 6, near)
    c_near.start()

    def inner_sweep(y):
        here = pl.ds(y, 8)
        for p in range(1, X + 1):
            w = weights(p, y)
            for c in range(3):
                total, v = neighbours(F, c, p, y, w)
                E[c, p - 1, here, :] = (4.0 / 3.0) * v + INV[c, p - 1, here, :] * total

    def outer_sweep(p, q, y):
        here, there = pl.ds(y, 8), pl.ds(OFF + y, 8)
        s = H[q, there, :] + H[p, there, :]
        t = K[q, there, :] + K[p, there, :]
        for c in range(3):
            w = t if c == 0 else s
            E[c, p - 1, here, :] = E[c, p - 1, here, :] + INV[c, p - 1, here, :] * (w * F[c, q, there, :])

    f_near.wait_recv()

    @pl.loop(0, Y // 8 - 1)
    def _(i):
        y = pl.multiple_of((i + sec) * 8, 8)
        inner_sweep(y)
        outer_sweep(p_near, q_near, y)

    cross2.wait()
    for r, (V, c, p, own, halo) in enumerate(face_rows):
        V[c, p, pl.ds(halo, 1), :] = S2R[pl.ds(r, 1), :]
    inner_sweep(halo_chunk)
    outer_sweep(p_near, q_near, halo_chunk)

    def unpack(Q, k, q2, q3, present):
        y = part_of(k)
        y2, y3 = y // 2, y // 4
        for c in range(3):
            v = Q[k, pl.ds(half * c, half), :]
            if present is not None:
                v = jnp.where(present, v, 0.0)
            F2[c, q2, pl.ds(OFF + y2, half), :] = jnp.where(odd_half, roll(v, 1), v)
            F2[c, q2, pl.ds(OFF + y2 + half, half), :] = jnp.where(odd_half, v, roll(v, -1))
        v = Q[k, pl.ds(3 * half, part3), :]
        if present is not None:
            v = jnp.where(present, v, 0.0)
        for c in range(3):
            spread = v
            for lane in range(4):
                if lane != c:
                    spread = jnp.where(quad == lane, roll(v, lane - c), spread)
            F3[c, q3, pl.ds(OFF + y3, part3), :] = spread

    c_near.wait_recv()
    for k in range(PARTS):
        unpack(QN, k, 3 * (1 - odd), 2 * (1 - odd), None)

    @pl.loop(0, PARTS)
    def _(k):
        y = part_of(k)
        y2, y3 = pl.multiple_of(y // 2, part2), pl.multiple_of(y // 4, part3)
        at2, at3 = pl.ds(y2, part2), pl.ds(y3, part3)

        @pl.when(has_far)
        def _():
            f_far(k).wait_recv()

        for i in range(part // 8):
            outer_sweep(p_far, q_far, pl.multiple_of(y + i * 8, 8))

        @pl.when(has_far)
        def _():
            c_far(k).wait_recv()

        unpack(QF, k, 3 * odd, 2 * odd, has_far)
        for c in range(3):
            kx, ky, kz = kinds(c)

            def f3(p, d):
                return F3[c, p, pl.ds(OFF + y3 + d, part3), :]

            v = f3(1, 0)
            total = W3[kx, 0, at3, :] * f3(0, 0) + W3[kx, 1, at3, :] * f3(2, 0)
            total = total + W3[ky, 2, at3, :] * f3(1, -1) + W3[ky, 3, at3, :] * f3(1, 1)
            total = total + W3[kz, 4, at3, :] * from_below(v, 4) + W3[kz, 5, at3, :] * from_above(v, 4)
            e3 = (4.0 / 3.0) * v + I3[c, at3, :] * total
            EX[c, 0, pl.ds(y2, part3, stride=2), :] = e3
            EX[c, 0, pl.ds(y2 + 1, part3, stride=2), :] = e3
            e3 = EX[c, 0, at2, :]

            def f2(p, d):
                return F2[c, p, pl.ds(OFF + y2 + d, part2), :]

            for j in range(2):
                p = 1 + j
                v = f2(p, 0)
                total = W2[kx, j, at2, :] * f2(p - 1, 0) + W2[kx, j + 1, at2, :] * f2(p + 1, 0)
                total = total + W2[ky, 3 + j, at2, :] * f2(p, -1) + W2[ky, 5 + j, at2, :] * f2(p, 1)
                total = total + W2[kz, 7 + j, at2, :] * from_below(v, 2) + W2[kz, 9 + j, at2, :] * from_above(v, 2)
                e2 = (4.0 / 3.0) * v + I2[c, j, at2, :] * total + e3
                R[c, j, pl.ds(y, part2, stride=2), :] = e2
                R[c, j, pl.ds(y + 1, part2, stride=2), :] = e2
        for i in range(part // 8):
            here = pl.ds(pl.multiple_of(y + i * 8, 8), 8)
            for p in range(X):
                for c in range(3):
                    out[c, p, here, :] = E[c, p, here, :] + R[c, p // 2, here, :]

    for copy in near1 + [f_near, c_near]:
        copy.wait_send()

    @pl.when(has_far)
    def _():
        for k in range(PARTS):
            for copy in far1(k) + [f_far(k), c_far(k)]:
                copy.wait_send()


def per_device(tiles, load_field, iterate, phase_label, damage):
    f32, i32 = jnp.float32, jnp.int32
    padded = Y + 2 * OFF
    return pl.pallas_call(
        functools.partial(kernel, tiles),
        out_shape=jax.ShapeDtypeStruct(load_field.shape, f32),
        in_specs=[pl.BlockSpec(memory_space=pltpu.HBM)] * 4,
        out_specs=pl.BlockSpec(memory_space=pltpu.VMEM),
        scratch_shapes=[
            pltpu.VMEM((3, X + 2, padded, Z), f32),
            pltpu.VMEM((3, X + 2, padded, Z), f32),
            pltpu.VMEM((3, X, Y, Z), f32),
            pltpu.VMEM((3, X, Y, Z), f32),
            pltpu.VMEM((3, X // 2, Y, Z), f32),
            pltpu.VMEM((3, X, Y, Z), f32),
            pltpu.VMEM((X + 2, padded, Z), f32),
            pltpu.VMEM((X + 2, padded, Z), f32),
            pltpu.VMEM((X + 2, Y, Z), i32),
            pltpu.VMEM((X + 2, Y, Z), i32),
            pltpu.VMEM((24, Z), f32),
            pltpu.VMEM((24, Z), f32),
            pltpu.VMEM((24, Z), f32),
            pltpu.VMEM((24, Z), f32),
            pltpu.VMEM((PARTS, Y // PARTS, Z), f32),
            pltpu.VMEM((PARTS, Y // PARTS, Z), f32),
            pltpu.VMEM((PARTS, Y // PARTS, Z), f32),
            pltpu.VMEM((PARTS, Y // PARTS, Z), f32),
            pltpu.VMEM((2, 11, Y // 2, Z), f32),
            pltpu.VMEM((3, 4, Y // 2 + 2 * OFF, Z), f32),
            pltpu.VMEM((3, 2, Y // 2, Z), f32),
            pltpu.VMEM((2, 6, Y // 4, Z), f32),
            pltpu.VMEM((3, 3, Y // 4 + 2 * OFF, Z), f32),
            pltpu.VMEM((3, Y // 4, Z), f32),
            pltpu.VMEM((3, 2, Y // 2, Z), f32),
            pltpu.SemaphoreType.DMA((4,)),
            pltpu.SemaphoreType.DMA((5 * PARTS + 7,)),
            pltpu.SemaphoreType.DMA((5 * PARTS + 7,)),
        ],
        compiler_params=pltpu.CompilerParams(
            collective_id=0, has_side_effects=True, vmem_limit_bytes=48 * 1024 * 1024),
    )(*[pltpu.with_memory_space_constraint(a, pltpu.HBM) for a in (load_field, iterate, phase_label, damage)])


def solution(mesh):
    tiles = mesh.shape["tile"]
    in_specs = (
        P(None, "tile", "sec", None),
        P(None, "tile", "sec", None),
        P("tile", "sec", None),
        P("tile", "sec", None),
    )
    out_specs = P(None, "tile", "sec", None)
    return jax.shard_map(
        functools.partial(per_device, tiles), mesh=mesh, in_specs=in_specs, out_specs=out_specs, check_vma=False
    )
```

```python
import functools

import jax
import jax.numpy as jnp
from jax import lax
from jax.experimental import pallas as pl
from jax.experimental.pallas import tpu as pltpu
from jax.sharding import PartitionSpec as P

shear_table = (1.0, 0.6, 1.8, 0.35)
bulk_table = (1.2, 0.9, 2.5, 0.5)
damage_step = 0.25
damage_floor = 0.01
relaxation = 2.0 / 3.0

MESH = pl.DeviceIdType.MESH
X = 4
Y = 128
Z = 128
PARTS = 2
OFF = 8


def lanes(shape):
    return lax.broadcasted_iota(jnp.int32, shape, len(shape) - 1)


def roll(v, shift):
    return pltpu.roll(v, shift % Z, v.ndim - 1)


def from_above(v, step):
    return jnp.where(lanes(v.shape) < Z - step, roll(v, -step), 0.0)


def from_below(v, step):
    return jnp.where(lanes(v.shape) >= step, roll(v, step), 0.0)


def moduli(phase, damage):
    soft = 1.0 - damage_step * damage.astype(jnp.float32)
    degrade = soft * soft + damage_floor

    def table(values):
        picked = jnp.full(phase.shape, values[3], jnp.float32)
        for label in (2, 1, 0):
            picked = jnp.where(phase == label, values[label], picked)
        return picked

    half = table([0.5 * s for s in shear_table])
    normal = table([0.5 * b + s for s, b in zip(shear_table, bulk_table)])
    return half * degrade, normal * degrade


def kernel(tiles, load_hbm, u_hbm, lab_hbm, dam_hbm, out, U, F, L, INV, R, E, H, K, LAB, DAM, S1, S1R, S2, S2R,
           PN, QN, PF, QF, W2, F2, I2, W3, F3, I3, EX, local_sem, send_sem, recv_sem):
    me = lax.axis_index("tile")
    sec = lax.axis_index("sec")
    odd = lax.rem(me, 2)
    has_far = jnp.logical_and(me > 0, me < tiles - 1)
    near = {"tile": me + 1 - 2 * odd}
    far = {"tile": jnp.clip(me - 1 + 2 * odd, 0, tiles - 1)}
    across = {"sec": 1 - sec}
    p_near, q_near = X - (X - 1) * odd, (X + 1) * (1 - odd)
    p_far, q_far = 1 + (X - 1) * odd, (X + 1) * odd

    barrier = pltpu.get_barrier_semaphore()
    pl.semaphore_signal(barrier, inc=1, device_id=near, device_id_type=MESH)

    @pl.when(has_far)
    def _():
        pl.semaphore_signal(barrier, inc=1, device_id=far, device_id_type=MESH)

    pl.semaphore_signal(barrier, inc=1, device_id=across, device_id_type=MESH)

    loads = [
        pltpu.make_async_copy(lab_hbm, LAB.at[pl.ds(1, X)], local_sem.at[0]),
        pltpu.make_async_copy(dam_hbm, DAM.at[pl.ds(1, X)], local_sem.at[1]),
        pltpu.make_async_copy(u_hbm, U.at[:, pl.ds(1, X), pl.ds(OFF, Y)], local_sem.at[2]),
        pltpu.make_async_copy(load_hbm, L, local_sem.at[3]),
    ]
    for copy in loads:
        copy.start()

    own_row = jnp.where(sec == 0, OFF + Y - 1, OFF)
    halo_row = jnp.where(sec == 0, OFF + Y, OFF - 1)
    edge_row = jnp.where(sec == 0, OFF - 1, OFF + Y)
    faces = [H.at[pl.ds(1, X)], K.at[pl.ds(1, X)]] + [U.at[c, pl.ds(1, X)] for c in range(3)]
    zero_row = jnp.zeros((1, Z), jnp.float32)
    for copy in loads[:2]:
        copy.wait()
    for p in range(X):
        h, k = moduli(LAB[1 + p, pl.ds(own_row - OFF, 1), :], DAM[1 + p, pl.ds(own_row - OFF, 1), :])
        S1[pl.ds(p, 1), :] = h
        S1[pl.ds(X + p, 1), :] = k
    loads[2].wait()
    for f in range(2, 5):
        for p in range(X):
            S1[pl.ds(X * f + p, 1), :] = faces[f][p, pl.ds(own_row, 1), :]
    pl.semaphore_wait(barrier, 2 + has_far.astype(jnp.int32))

    def remote(src, dst, index, device):
        return pltpu.make_async_remote_copy(
            src_ref=src, dst_ref=dst, send_sem=send_sem.at[index], recv_sem=recv_sem.at[index],
            device_id=device, device_id_type=MESH)

    rows = pl.ds(OFF, Y)
    part = Y // PARTS
    base = 5 * PARTS

    def part_of(k):
        n = k + (1 - sec) * (PARTS - 1 - 2 * k)
        return pl.multiple_of(n * part, part)

    def far1(k):
        y = part_of(k)
        here, there = pl.ds(y, part), pl.ds(OFF + y, part)
        return [
            remote(lab_hbm.at[p_far - 1, here], LAB.at[X + 1 - q_far, here], 3 * k, far),
            remote(dam_hbm.at[p_far - 1, here], DAM.at[X + 1 - q_far, here], 3 * k + 1, far),
            remote(u_hbm.at[:, p_far - 1, here], U.at[:, X + 1 - q_far, there], 3 * k + 2, far),
        ]

    def f_far(k):
        there = pl.ds(OFF + part_of(k), part)
        return remote(F.at[:, p_far, there], F.at[:, X + 1 - q_far, there], 3 * PARTS + k, far)

    def c_far(k):
        return remote(PF.at[k], QF.at[k], 4 * PARTS + k, far)

    near1 = [
        remote(lab_hbm.at[p_near - 1], LAB.at[X + 1 - q_near], base, near),
        remote(dam_hbm.at[p_near - 1], DAM.at[X + 1 - q_near], base + 1, near),
        remote(u_hbm.at[:, p_near - 1], U.at[:, X + 1 - q_near, rows], base + 2, near),
    ]
    cross1 = remote(S1, S1R, base + 3, across)
    cross1.start()

    @pl.when(has_far)
    def _():
        for k in range(PARTS):
            for copy in far1(k):
                copy.start()

    for copy in near1:
        copy.start()

    @pl.loop(0, Y // 8)
    def _(i):
        y = pl.multiple_of(i * 8, 8)
        for p in range(1, X + 1):
            h, k = moduli(LAB[p, pl.ds(y, 8), :], DAM[p, pl.ds(y, 8), :])
            H[p, pl.ds(OFF + y, 8), :] = h
            K[p, pl.ds(OFF + y, 8), :] = k

    for ref in faces:
        for p in range(X):
            ref[p, pl.ds(edge_row, 1), :] = zero_row
    for c in range(3):
        for p in range(1, X + 1):
            F[c, p, pl.ds(edge_row, 1), :] = zero_row

    @pl.when(jnp.logical_not(has_far))
    def _():
        for ref in (H, K):
            ref[q_far] = jnp.zeros(H.shape[1:], jnp.float32)
        for c in range(3):
            U[c, q_far] = jnp.zeros(U.shape[2:], jnp.float32)
            F[c, q_far] = jnp.zeros(F.shape[2:], jnp.float32)

    def weights(p, y):
        result = {}
        for name, M in (("s", H), ("t", K)):
            m = M[p, pl.ds(OFF + y, 8), :]
            if p > 1:
                result[name, "xl"] = m + M[p - 1, pl.ds(OFF + y, 8), :]
            if p < X:
                result[name, "xu"] = m + M[p + 1, pl.ds(OFF + y, 8), :]
            result[name, "yl"] = m + M[p, pl.ds(OFF + y - 1, 8), :]
            result[name, "yu"] = m + M[p, pl.ds(OFF + y + 1, 8), :]
            result[name, "zl"] = m + from_below(m, 1)
            result[name, "zu"] = m + from_above(m, 1)
        return result

    def neighbours(V, c, p, y, w):
        v = V[c, p, pl.ds(OFF + y, 8), :]
        kind = ["t" if c == a else "s" for a in range(3)]
        total = w[kind[1], "yl"] * V[c, p, pl.ds(OFF + y - 1, 8), :]
        total = total + w[kind[1], "yu"] * V[c, p, pl.ds(OFF + y + 1, 8), :]
        total = total + w[kind[2], "zl"] * from_below(v, 1)
        total = total + w[kind[2], "zu"] * from_above(v, 1)
        if p > 1:
            total = total + w[kind[0], "xl"] * V[c, p - 1, pl.ds(OFF + y, 8), :]
        if p < X:
            total = total + w[kind[0], "xu"] * V[c, p + 1, pl.ds(OFF + y, 8), :]
        return total, v

    def inner_residual(y):
        here = pl.ds(y, 8)
        for p in range(1, X + 1):
            w = weights(p, y)
            sides = {}
            for name in ("s", "t"):
                xs = [w[name, side] for side in ("xl", "xu") if (name, side) in w]
                sides[name, 0] = xs[0] if len(xs) == 1 else xs[0] + xs[1]
                sides[name, 1] = w[name, "yl"] + w[name, "yu"]
                sides[name, 2] = w[name, "zl"] + w[name, "zu"]
            for c in range(3):
                total, v = neighbours(U, c, p, y, w)
                others = [a for a in range(3) if a != c]
                diag = sides["t", c] + sides["s", others[0]] + sides["s", others[1]]
                acc = L[c, p - 1, here, :] + total
                if 1 < p < X:
                    r = acc - diag * v
                    inv = relaxation / diag
                    R[c, p - 2, here, :] = r
                    INV[c, p - 1, here, :] = inv
                    F[c, p, pl.ds(OFF + y, 8), :] = r * inv
                else:
                    L[c, p - 1, here, :] = acc
                    INV[c, p - 1, here, :] = diag

    halo_chunk = pl.multiple_of((1 - sec) * (Y - 8), 8)
    loads[3].wait()

    @pl.loop(0, Y // 8 - 1)
    def _(i):
        inner_residual(pl.multiple_of((i + sec) * 8, 8))

    cross1.wait()
    for f, ref in enumerate(faces):
        for p in range(X):
            ref[p, pl.ds(halo_row, 1), :] = S1R[pl.ds(X * f + p, 1), :]
    inner_residual(halo_chunk)

    def outer_face(p, q, y, present):
        here, there = pl.ds(y, 8), pl.ds(OFF + y, 8)
        h, k = moduli(LAB[q, here, :], DAM[q, here, :])
        if present is not None:
            h = jnp.where(present, h, 0.0)
            k = jnp.where(present, k, 0.0)
        H[q, there, :] = h
        K[q, there, :] = k
        s = h + H[p, there, :]
        t = k + K[p, there, :]
        j = (p - 1) // 2
        for c in range(3):
            w = t if c == 0 else s
            diag = INV[c, p - 1, here, :] + w
            r = L[c, p - 1, here, :] + w * U[c, q, there, :] - diag * U[c, p, there, :]
            inv = relaxation / diag
            INV[c, p - 1, here, :] = inv
            F[c, p, there, :] = r * inv
            R[c, j, here, :] = R[c, j, here, :] + r

    for copy in near1:
        copy.wait_recv()

    @pl.loop(0, Y // 8)
    def _(i):
        outer_face(p_near, q_near, pl.multiple_of(i * 8, 8), None)

    f_near = remote(F.at[:, p_near, rows], F.at[:, X + 1 - q_near, rows], base + 4, near)
    f_near.start()

    Y2, Y3 = Y // 2, Y // 4
    part2, part3 = part // 2, part // 4
    shape2, shape3 = (part2, Z), (part3, Z)
    odd2 = (lanes(shape2) & 1) == 1
    quad = lanes(shape3) & 3
    high3 = quad >= 2
    j_near, j_far = 1 - odd, odd

    def pairs(v):
        return v + jnp.where(odd2, roll(v, 1), roll(v, -1))

    def quads(v):
        return v + jnp.where(high3, roll(v, 2), roll(v, -2))

    def fine_rows(M, p, first):
        return M[p, pl.ds(first, part2, stride=2), :]

    def coarse_rows(m, slot, y2, first):
        return W2[m, slot, pl.ds(y2 + first, part3, stride=2), :]

    def kinds(c):
        return [1 if c == a else 0 for a in range(3)]

    def x_face(M, p, q, y):
        face = fine_rows(M, p, OFF + y) + fine_rows(M, p, OFF + y + 1)
        return pairs(face + fine_rows(M, q, OFF + y) + fine_rows(M, q, OFF + y + 1))

    def residual_two(c, j, y):
        return pairs(fine_rows(R.at[c], j, y) + fine_rows(R.at[c], j, y + 1))

    @pl.loop(0, PARTS)
    def _(n):
        y = pl.multiple_of(n * part, part)
        y2 = pl.multiple_of(n * part2, part2)
        y3 = pl.multiple_of(n * part3, part3)
        at2, at3 = pl.ds(y2, part2), pl.ds(y3, part3)
        sides = {}
        for m, M in enumerate((H, K)):
            mid = x_face(M, 2, 3, y)
            close = x_face(M, p_near, q_near, y)
            W2[m, 1, at2, :] = mid
            W2[m, 2 - 2 * odd, at2, :] = close
            W3[m, 1 - odd, at3, :] = quads(
                coarse_rows(m, 2 - 2 * odd, y2, 0) + coarse_rows(m, 2 - 2 * odd, y2, 1))
            for j in range(2):
                r7, r8, r9, r10 = [
                    fine_rows(M, 1 + 2 * j, OFF + y + d) + fine_rows(M, 2 + 2 * j, OFF + y + d) for d in (-1, 0, 1, 2)]
                yl, yu = pairs(r7 + r8), pairs(r9 + r10)
                cell = r8 + r9
                low = cell + from_below(cell, 1)
                high = cell + from_above(cell, 1)
                zl = jnp.where(odd2, roll(low, 1), low)
                zu = jnp.where(odd2, high, roll(high, -1))
                for slot, value in ((3, yl), (5, yu), (7, zl), (9, zu)):
                    W2[m, slot + j, at2, :] = value
                sides[m, j, 0] = mid
                sides[m, j, 1] = yl + yu
                sides[m, j, 2] = zl + zu
            W3[m, 2, at3, :] = quads(coarse_rows(m, 3, y2, 0) + coarse_rows(m, 4, y2, 0))
            W3[m, 3, at3, :] = quads(coarse_rows(m, 5, y2, 1) + coarse_rows(m, 6, y2, 1))
            low = coarse_rows(m, 7, y2, 0) + coarse_rows(m, 7, y2, 1)
            low = low + coarse_rows(m, 8, y2, 0) + coarse_rows(m, 8, y2, 1)
            high = coarse_rows(m, 9, y2, 0) + coarse_rows(m, 9, y2, 1)
            high = high + coarse_rows(m, 10, y2, 0) + coarse_rows(m, 10, y2, 1)
            W3[m, 4, at3, :] = jnp.where(high3, roll(low, 2), low)
            W3[m, 5, at3, :] = jnp.where(high3, high, roll(high, -2))
        for c in range(3):
            kx, ky, kz = kinds(c)
            for j in range(2):
                I2[c, j, at2, :] = sides[kx, j, 0] + sides[ky, j, 1] + sides[kz, j, 2]
            inv = relaxation / (I2[c, j_near, at2, :] + W2[kx, 2 - 2 * odd, at2, :])
            I2[c, j_near, at2, :] = inv
            res = residual_two(c, j_near, y)
            EX[c, j_near, at2, :] = res
            F2[c, 1 + j_near, pl.ds(OFF + y2, part2), :] = res * inv
            I3[c, at3, :] = (W3[kx, 1 - odd, at3, :] + W3[ky, 2, at3, :] + W3[ky, 3, at3, :]
                             + W3[kz, 4, at3, :] + W3[kz, 5, at3, :])

    half = part2 // 2
    odd_half = odd2[:half]

    def packed(V, c, p, y2):
        return jnp.where(odd_half, V[c, p, pl.ds(OFF + y2 + half, half), :], V[c, p, pl.ds(OFF + y2, half), :])

    own2 = jnp.where(sec == 0, OFF + Y2 - 1, OFF)
    own3 = jnp.where(sec == 0, OFF + Y3 - 1, OFF)
    halo2 = jnp.where(sec == 0, OFF + Y2, OFF - 1)
    halo3 = jnp.where(sec == 0, OFF + Y3, OFF - 1)
    edge2 = jnp.where(sec == 0, OFF - 1, OFF + Y2)
    edge3 = jnp.where(sec == 0, OFF - 1, OFF + Y3)
    quad_row = lanes((1, Z)) & 3
    odd_row = (quad_row & 1) == 1
    fine_faces = [(c, p) for c in range(3) for p in range(1, X + 1)]
    for c in range(3):
        F2[c, 1, pl.ds(edge2, 1), :] = zero_row
        F2[c, 2, pl.ds(edge2, 1), :] = zero_row
        F3[c, 1, pl.ds(edge3, 1), :] = zero_row

    def pack_rows():
        for r, (c, p) in enumerate(fine_faces):
            S2[pl.ds(r, 1), :] = F[c, p, pl.ds(own_row, 1), :]
        deep = zero_row
        for c in range(3):
            S2[pl.ds(12 + c, 1), :] = jnp.where(odd_row, F2[c, 2, pl.ds(own2, 1), :], F2[c, 1, pl.ds(own2, 1), :])
            deep = jnp.where(quad_row == c, F3[c, 1, pl.ds(own3, 1), :], deep)
        S2[pl.ds(15, 1), :] = deep

    def unpack_rows():
        for r, (c, p) in enumerate(fine_faces):
            F[c, p, pl.ds(halo_row, 1), :] = S2R[pl.ds(r, 1), :]
        deep = S2R[pl.ds(15, 1), :]
        for c in range(3):
            v = S2R[pl.ds(12 + c, 1), :]
            F2[c, 1, pl.ds(halo2, 1), :] = jnp.where(odd_row, roll(v, 1), v)
            F2[c, 2, pl.ds(halo2, 1), :] = jnp.where(odd_row, v, roll(v, -1))
            F3[c, 1, pl.ds(halo3, 1), :] = spread_quad(deep, c, quad_row)

    def spread_quad(v, c, quad):
        spread = v
        for lane in range(4):
            if lane != c:
                spread = jnp.where(quad == lane, roll(v, lane - c), spread)
        return spread

    cross2 = remote(S2, S2R, base + 5, across)

    @pl.loop(0, PARTS)
    def _(k):
        y = part_of(k)

        @pl.when(has_far)
        def _():
            for copy in far1(k):
                copy.wait_recv()

        for i in range(part // 8):
            outer_face(p_far, q_far, pl.multiple_of(y + i * 8, 8), has_far)

        @pl.when(has_far)
        def _():
            f_far(k).start()

        y2, y3 = pl.multiple_of(y // 2, part2), pl.multiple_of(y // 4, part3)
        at2, at3 = pl.ds(y2, part2), pl.ds(y3, part3)
        for m, M in enumerate((H, K)):
            W2[m, 2 * odd, at2, :] = x_face(M, p_far, q_far, y)
            W3[m, odd, at3, :] = quads(coarse_rows(m, 2 * odd, y2, 0) + coarse_rows(m, 2 * odd, y2, 1))
        deep = jnp.zeros(shape3, jnp.float32)
        for c in range(3):
            kx = kinds(c)[0]
            inv = relaxation / (I2[c, j_far, at2, :] + W2[kx, 2 * odd, at2, :])
            I2[c, j_far, at2, :] = inv
            res = residual_two(c, j_far, y)
            EX[c, j_far, at2, :] = res
            F2[c, 1 + j_far, pl.ds(OFF + y2, part2), :] = res * inv
            inv = relaxation / (I3[c, at3, :] + W3[kx, odd, at3, :])
            I3[c, at3, :] = inv
            res = EX[c, 0, pl.ds(y2, part3, stride=2), :] + EX[c, 0, pl.ds(y2 + 1, part3, stride=2), :]
            res = res + EX[c, 1, pl.ds(y2, part3, stride=2), :] + EX[c, 1, pl.ds(y2 + 1, part3, stride=2), :]
            first = quads(res) * inv
            F3[c, 1, pl.ds(OFF + y3, part3), :] = first
            deep = jnp.where(quad == c, first, deep)
            PF[k, pl.ds(half * c, half), :] = packed(F2, c, 1 + j_far, y2)
            PN[k, pl.ds(half * c, half), :] = packed(F2, c, 1 + j_near, y2)
        PF[k, pl.ds(3 * half, part3), :] = deep
        PN[k, pl.ds(3 * half, part3), :] = deep

        @pl.when(has_far)
        def _():
            c_far(k).start()

        @pl.when(k == 0)
        def _():
            pack_rows()
            cross2.start()

    c_near = remote(PN, QN, base + 6, near)
    c_near.start()

    def inner_sweep(y):
        here = pl.ds(y, 8)
        for p in range(1, X + 1):
            w = weights(p, y)
            for c in range(3):
                total, v = neighbours(F, c, p, y, w)
                E[c, p - 1, here, :] = (4.0 / 3.0) * v + INV[c, p - 1, here, :] * total

    def outer_sweep(p, q, y):
        here, there = pl.ds(y, 8), pl.ds(OFF + y, 8)
        s = H[q, there, :] + H[p, there, :]
        t = K[q, there, :] + K[p, there, :]
        for c in range(3):
            w = t if c == 0 else s
            E[c, p - 1, here, :] = E[c, p - 1, here, :] + INV[c, p - 1, here, :] * (w * F[c, q, there, :])

    f_near.wait_recv()

    @pl.loop(0, Y // 8 - 1)
    def _(i):
        y = pl.multiple_of((i + sec) * 8, 8)
        inner_sweep(y)
        outer_sweep(p_near, q_near, y)

    cross2.wait()
    unpack_rows()
    inner_sweep(halo_chunk)
    outer_sweep(p_near, q_near, halo_chunk)

    def unpack(Q, k, q2, q3, present):
        y = part_of(k)
        y2, y3 = y // 2, y // 4
        for c in range(3):
            v = Q[k, pl.ds(half * c, half), :]
            if present is not None:
                v = jnp.where(present, v, 0.0)
            F2[c, q2, pl.ds(OFF + y2, half), :] = jnp.where(odd_half, roll(v, 1), v)
            F2[c, q2, pl.ds(OFF + y2 + half, half), :] = jnp.where(odd_half, v, roll(v, -1))
        v = Q[k, pl.ds(3 * half, part3), :]
        if present is not None:
            v = jnp.where(present, v, 0.0)
        for c in range(3):
            F3[c, q3, pl.ds(OFF + y3, part3), :] = spread_quad(v, c, quad)

    c_near.wait_recv()
    for k in range(PARTS):
        unpack(QN, k, 3 * (1 - odd), 2 * (1 - odd), None)

    @pl.loop(0, PARTS)
    def _(k):
        y = part_of(k)
        y2, y3 = pl.multiple_of(y // 2, part2), pl.multiple_of(y // 4, part3)
        at2, at3 = pl.ds(y2, part2), pl.ds(y3, part3)

        @pl.when(has_far)
        def _():
            f_far(k).wait_recv()

        for i in range(part // 8):
            outer_sweep(p_far, q_far, pl.multiple_of(y + i * 8, 8))

        @pl.when(has_far)
        def _():
            c_far(k).wait_recv()

        unpack(QF, k, 3 * odd, 2 * odd, has_far)
        for c in range(3):
            kx, ky, kz = kinds(c)

            def f3(p, d):
                return F3[c, p, pl.ds(OFF + y3 + d, part3), :]

            v = f3(1, 0)
            total = W3[kx, 0, at3, :] * f3(0, 0) + W3[kx, 1, at3, :] * f3(2, 0)
            total = total + W3[ky, 2, at3, :] * f3(1, -1) + W3[ky, 3, at3, :] * f3(1, 1)
            total = total + W3[kz, 4, at3, :] * from_below(v, 4) + W3[kz, 5, at3, :] * from_above(v, 4)
            e3 = (4.0 / 3.0) * v + I3[c, at3, :] * total
            EX[c, 0, pl.ds(y2, part3, stride=2), :] = e3
            EX[c, 0, pl.ds(y2 + 1, part3, stride=2), :] = e3
            e3 = EX[c, 0, at2, :]

            def f2(p, d):
                return F2[c, p, pl.ds(OFF + y2 + d, part2), :]

            for j in range(2):
                p = 1 + j
                v = f2(p, 0)
                total = W2[kx, j, at2, :] * f2(p - 1, 0) + W2[kx, j + 1, at2, :] * f2(p + 1, 0)
                total = total + W2[ky, 3 + j, at2, :] * f2(p, -1) + W2[ky, 5 + j, at2, :] * f2(p, 1)
                total = total + W2[kz, 7 + j, at2, :] * from_below(v, 2) + W2[kz, 9 + j, at2, :] * from_above(v, 2)
                e2 = (4.0 / 3.0) * v + I2[c, j, at2, :] * total + e3
                R[c, j, pl.ds(y, part2, stride=2), :] = e2
                R[c, j, pl.ds(y + 1, part2, stride=2), :] = e2
        for i in range(part // 8):
            here = pl.ds(pl.multiple_of(y + i * 8, 8), 8)
            for p in range(X):
                for c in range(3):
                    out[c, p, here, :] = E[c, p, here, :] + R[c, p // 2, here, :]

    for copy in near1 + [f_near, c_near]:
        copy.wait_send()

    @pl.when(has_far)
    def _():
        for k in range(PARTS):
            for copy in far1(k) + [f_far(k), c_far(k)]:
                copy.wait_send()


def per_device(tiles, load_field, iterate, phase_label, damage):
    f32, i32 = jnp.float32, jnp.int32
    padded = Y + 2 * OFF
    return pl.pallas_call(
        functools.partial(kernel, tiles),
        out_shape=jax.ShapeDtypeStruct(load_field.shape, f32),
        in_specs=[pl.BlockSpec(memory_space=pltpu.HBM)] * 4,
        out_specs=pl.BlockSpec(memory_space=pltpu.VMEM),
        scratch_shapes=[
            pltpu.VMEM((3, X + 2, padded, Z), f32),
            pltpu.VMEM((3, X + 2, padded, Z), f32),
            pltpu.VMEM((3, X, Y, Z), f32),
            pltpu.VMEM((3, X, Y, Z), f32),
            pltpu.VMEM((3, X // 2, Y, Z), f32),
            pltpu.VMEM((3, X, Y, Z), f32),
            pltpu.VMEM((X + 2, padded, Z), f32),
            pltpu.VMEM((X + 2, padded, Z), f32),
            pltpu.VMEM((X + 2, Y, Z), i32),
            pltpu.VMEM((X + 2, Y, Z), i32),
            pltpu.VMEM((20, Z), f32),
            pltpu.VMEM((20, Z), f32),
            pltpu.VMEM((16, Z), f32),
            pltpu.VMEM((16, Z), f32),
            pltpu.VMEM((PARTS, Y // PARTS, Z), f32),
            pltpu.VMEM((PARTS, Y // PARTS, Z), f32),
            pltpu.VMEM((PARTS, Y // PARTS, Z), f32),
            pltpu.VMEM((PARTS, Y // PARTS, Z), f32),
            pltpu.VMEM((2, 11, Y // 2, Z), f32),
            pltpu.VMEM((3, 4, Y // 2 + 2 * OFF, Z), f32),
            pltpu.VMEM((3, 2, Y // 2, Z), f32),
            pltpu.VMEM((2, 6, Y // 4, Z), f32),
            pltpu.VMEM((3, 3, Y // 4 + 2 * OFF, Z), f32),
            pltpu.VMEM((3, Y // 4, Z), f32),
            pltpu.VMEM((3, 2, Y // 2, Z), f32),
            pltpu.SemaphoreType.DMA((4,)),
            pltpu.SemaphoreType.DMA((5 * PARTS + 7,)),
            pltpu.SemaphoreType.DMA((5 * PARTS + 7,)),
        ],
        compiler_params=pltpu.CompilerParams(
            collective_id=0, has_side_effects=True, vmem_limit_bytes=48 * 1024 * 1024),
    )(*[pltpu.with_memory_space_constraint(a, pltpu.HBM) for a in (load_field, iterate, phase_label, damage)])


def solution(mesh):
    tiles = mesh.shape["tile"]
    in_specs = (
        P(None, "tile", "sec", None),
        P(None, "tile", "sec", None),
        P("tile", "sec", None),
        P("tile", "sec", None),
    )
    out_specs = P(None, "tile", "sec", None)
    return jax.shard_map(
        functools.partial(per_device, tiles), mesh=mesh, in_specs=in_specs, out_specs=out_specs, check_vma=False
    )
```

```python
import functools

import jax
import jax.numpy as jnp
from jax import lax
from jax.experimental import pallas as pl
from jax.experimental.pallas import tpu as pltpu
from jax.sharding import PartitionSpec as P

shear_table = (1.0, 0.6, 1.8, 0.35)
bulk_table = (1.2, 0.9, 2.5, 0.5)
damage_step = 0.25
damage_floor = 0.01
relaxation = 2.0 / 3.0

MESH = pl.DeviceIdType.MESH
X = 4
Y = 128
Z = 128
PARTS = 2
OFF = 8


def lanes(shape):
    return lax.broadcasted_iota(jnp.int32, shape, len(shape) - 1)


def roll(v, shift):
    return pltpu.roll(v, shift % Z, v.ndim - 1)


def from_above(v, step):
    return jnp.where(lanes(v.shape) < Z - step, roll(v, -step), 0.0)


def from_below(v, step):
    return jnp.where(lanes(v.shape) >= step, roll(v, step), 0.0)


def moduli(phase, damage):
    soft = 1.0 - damage_step * damage.astype(jnp.float32)
    degrade = soft * soft + damage_floor

    def table(values):
        picked = jnp.full(phase.shape, values[3], jnp.float32)
        for label in (2, 1, 0):
            picked = jnp.where(phase == label, values[label], picked)
        return picked

    half = table([0.5 * s for s in shear_table])
    normal = table([0.5 * b + s for s, b in zip(shear_table, bulk_table)])
    return half * degrade, normal * degrade


def kernel(tiles, load_hbm, u_hbm, lab_hbm, dam_hbm, out, U, F, L, INV, R, E, H, K, LAB, DAM, S1, S1R, S2, S2R,
           PN, QN, PF, QF, W2, F2, I2, W3, F3, I3, EX, local_sem, send_sem, recv_sem):
    me = lax.axis_index("tile")
    sec = lax.axis_index("sec")
    odd = lax.rem(me, 2)
    has_far = jnp.logical_and(me > 0, me < tiles - 1)
    near = {"tile": me + 1 - 2 * odd}
    far = {"tile": jnp.clip(me - 1 + 2 * odd, 0, tiles - 1)}
    across = {"sec": 1 - sec}
    p_near, q_near = X - (X - 1) * odd, (X + 1) * (1 - odd)
    p_far, q_far = 1 + (X - 1) * odd, (X + 1) * odd

    barrier = pltpu.get_barrier_semaphore()
    pl.semaphore_signal(barrier, inc=1, device_id=near, device_id_type=MESH)

    @pl.when(has_far)
    def _():
        pl.semaphore_signal(barrier, inc=1, device_id=far, device_id_type=MESH)

    pl.semaphore_signal(barrier, inc=1, device_id=across, device_id_type=MESH)

    loads = [
        pltpu.make_async_copy(lab_hbm, LAB.at[pl.ds(1, X)], local_sem.at[0]),
        pltpu.make_async_copy(dam_hbm, DAM.at[pl.ds(1, X)], local_sem.at[1]),
        pltpu.make_async_copy(u_hbm, U.at[:, pl.ds(1, X), pl.ds(OFF, Y)], local_sem.at[2]),
        pltpu.make_async_copy(load_hbm, L, local_sem.at[3]),
    ]
    for copy in loads:
        copy.start()

    own_row = jnp.where(sec == 0, OFF + Y - 1, OFF)
    halo_row = jnp.where(sec == 0, OFF + Y, OFF - 1)
    edge_row = jnp.where(sec == 0, OFF - 1, OFF + Y)
    faces = [H.at[pl.ds(1, X)], K.at[pl.ds(1, X)]] + [U.at[c, pl.ds(1, X)] for c in range(3)]
    zero_row = jnp.zeros((1, Z), jnp.float32)
    for copy in loads[:2]:
        copy.wait()
    for p in range(X):
        h, k = moduli(LAB[1 + p, pl.ds(own_row - OFF, 1), :], DAM[1 + p, pl.ds(own_row - OFF, 1), :])
        S1[pl.ds(p, 1), :] = h
        S1[pl.ds(X + p, 1), :] = k
    loads[2].wait()
    for f in range(2, 5):
        for p in range(X):
            S1[pl.ds(X * f + p, 1), :] = faces[f][p, pl.ds(own_row, 1), :]
    pl.semaphore_wait(barrier, 2 + has_far.astype(jnp.int32))

    def remote(src, dst, index, device):
        return pltpu.make_async_remote_copy(
            src_ref=src, dst_ref=dst, send_sem=send_sem.at[index], recv_sem=recv_sem.at[index],
            device_id=device, device_id_type=MESH)

    rows = pl.ds(OFF, Y)
    part = Y // PARTS
    base = 5 * PARTS

    def part_of(k):
        n = k + (1 - sec) * (PARTS - 1 - 2 * k)
        return pl.multiple_of(n * part, part)

    def far1(k):
        y = part_of(k)
        here, there = pl.ds(y, part), pl.ds(OFF + y, part)
        return [
            remote(LAB.at[p_far, here], LAB.at[X + 1 - q_far, here], 3 * k, far),
            remote(DAM.at[p_far, here], DAM.at[X + 1 - q_far, here], 3 * k + 1, far),
            remote(U.at[:, p_far, there], U.at[:, X + 1 - q_far, there], 3 * k + 2, far),
        ]

    def f_far(k):
        there = pl.ds(OFF + part_of(k), part)
        return remote(F.at[:, p_far, there], F.at[:, X + 1 - q_far, there], 3 * PARTS + k, far)

    def c_far(k):
        return remote(PF.at[k], QF.at[k], 4 * PARTS + k, far)

    near1 = [
        remote(LAB.at[p_near], LAB.at[X + 1 - q_near], base, near),
        remote(DAM.at[p_near], DAM.at[X + 1 - q_near], base + 1, near),
        remote(U.at[:, p_near, rows], U.at[:, X + 1 - q_near, rows], base + 2, near),
    ]
    cross1 = remote(S1, S1R, base + 3, across)
    cross1.start()

    @pl.when(has_far)
    def _():
        for k in range(PARTS):
            for copy in far1(k):
                copy.start()

    for copy in near1:
        copy.start()

    @pl.loop(0, Y // 8)
    def _(i):
        y = pl.multiple_of(i * 8, 8)
        for p in range(1, X + 1):
            h, k = moduli(LAB[p, pl.ds(y, 8), :], DAM[p, pl.ds(y, 8), :])
            H[p, pl.ds(OFF + y, 8), :] = h
            K[p, pl.ds(OFF + y, 8), :] = k

    for ref in faces:
        for p in range(X):
            ref[p, pl.ds(edge_row, 1), :] = zero_row
    for c in range(3):
        for p in range(1, X + 1):
            F[c, p, pl.ds(edge_row, 1), :] = zero_row

    @pl.when(jnp.logical_not(has_far))
    def _():
        for ref in (H, K):
            ref[q_far] = jnp.zeros(H.shape[1:], jnp.float32)
        for c in range(3):
            U[c, q_far] = jnp.zeros(U.shape[2:], jnp.float32)
            F[c, q_far] = jnp.zeros(F.shape[2:], jnp.float32)

    def weights(p, y):
        result = {}
        for name, M in (("s", H), ("t", K)):
            m = M[p, pl.ds(OFF + y, 8), :]
            if p > 1:
                result[name, "xl"] = m + M[p - 1, pl.ds(OFF + y, 8), :]
            if p < X:
                result[name, "xu"] = m + M[p + 1, pl.ds(OFF + y, 8), :]
            result[name, "yl"] = m + M[p, pl.ds(OFF + y - 1, 8), :]
            result[name, "yu"] = m + M[p, pl.ds(OFF + y + 1, 8), :]
            result[name, "zl"] = m + from_below(m, 1)
            result[name, "zu"] = m + from_above(m, 1)
        return result

    def neighbours(V, c, p, y, w):
        v = V[c, p, pl.ds(OFF + y, 8), :]
        kind = ["t" if c == a else "s" for a in range(3)]
        total = w[kind[1], "yl"] * V[c, p, pl.ds(OFF + y - 1, 8), :]
        total = total + w[kind[1], "yu"] * V[c, p, pl.ds(OFF + y + 1, 8), :]
        total = total + w[kind[2], "zl"] * from_below(v, 1)
        total = total + w[kind[2], "zu"] * from_above(v, 1)
        if p > 1:
            total = total + w[kind[0], "xl"] * V[c, p - 1, pl.ds(OFF + y, 8), :]
        if p < X:
            total = total + w[kind[0], "xu"] * V[c, p + 1, pl.ds(OFF + y, 8), :]
        return total, v

    def inner_residual(y):
        here = pl.ds(y, 8)
        for p in range(1, X + 1):
            w = weights(p, y)
            sides = {}
            for name in ("s", "t"):
                xs = [w[name, side] for side in ("xl", "xu") if (name, side) in w]
                sides[name, 0] = xs[0] if len(xs) == 1 else xs[0] + xs[1]
                sides[name, 1] = w[name, "yl"] + w[name, "yu"]
                sides[name, 2] = w[name, "zl"] + w[name, "zu"]
            for c in range(3):
                total, v = neighbours(U, c, p, y, w)
                others = [a for a in range(3) if a != c]
                diag = sides["t", c] + sides["s", others[0]] + sides["s", others[1]]
                acc = L[c, p - 1, here, :] + total
                if 1 < p < X:
                    r = acc - diag * v
                    inv = relaxation / diag
                    R[c, p - 2, here, :] = r
                    INV[c, p - 1, here, :] = inv
                    F[c, p, pl.ds(OFF + y, 8), :] = r * inv
                else:
                    L[c, p - 1, here, :] = acc
                    INV[c, p - 1, here, :] = diag

    halo_chunk = pl.multiple_of((1 - sec) * (Y - 8), 8)
    loads[3].wait()

    @pl.loop(0, Y // 8 - 1)
    def _(i):
        inner_residual(pl.multiple_of((i + sec) * 8, 8))

    cross1.wait()
    for f, ref in enumerate(faces):
        for p in range(X):
            ref[p, pl.ds(halo_row, 1), :] = S1R[pl.ds(X * f + p, 1), :]
    inner_residual(halo_chunk)

    def outer_face(p, q, y, present):
        here, there = pl.ds(y, 8), pl.ds(OFF + y, 8)
        h, k = moduli(LAB[q, here, :], DAM[q, here, :])
        if present is not None:
            h = jnp.where(present, h, 0.0)
            k = jnp.where(present, k, 0.0)
        H[q, there, :] = h
        K[q, there, :] = k
        s = h + H[p, there, :]
        t = k + K[p, there, :]
        j = (p - 1) // 2
        for c in range(3):
            w = t if c == 0 else s
            diag = INV[c, p - 1, here, :] + w
            r = L[c, p - 1, here, :] + w * U[c, q, there, :] - diag * U[c, p, there, :]
            inv = relaxation / diag
            INV[c, p - 1, here, :] = inv
            F[c, p, there, :] = r * inv
            R[c, j, here, :] = R[c, j, here, :] + r

    for copy in near1:
        copy.wait_recv()

    @pl.loop(0, Y // 8)
    def _(i):
        outer_face(p_near, q_near, pl.multiple_of(i * 8, 8), None)

    f_near = remote(F.at[:, p_near, rows], F.at[:, X + 1 - q_near, rows], base + 4, near)
    f_near.start()

    Y2, Y3 = Y // 2, Y // 4
    part2, part3 = part // 2, part // 4
    shape2, shape3 = (part2, Z), (part3, Z)
    odd2 = (lanes(shape2) & 1) == 1
    quad = lanes(shape3) & 3
    high3 = quad >= 2
    j_near, j_far = 1 - odd, odd

    def pairs(v):
        return v + jnp.where(odd2, roll(v, 1), roll(v, -1))

    def quads(v):
        return v + jnp.where(high3, roll(v, 2), roll(v, -2))

    def fine_rows(M, p, first):
        return M[p, pl.ds(first, part2, stride=2), :]

    def coarse_rows(m, slot, y2, first):
        return W2[m, slot, pl.ds(y2 + first, part3, stride=2), :]

    def kinds(c):
        return [1 if c == a else 0 for a in range(3)]

    def x_face(M, p, q, y):
        face = fine_rows(M, p, OFF + y) + fine_rows(M, p, OFF + y + 1)
        return pairs(face + fine_rows(M, q, OFF + y) + fine_rows(M, q, OFF + y + 1))

    def residual_two(c, j, y):
        return pairs(fine_rows(R.at[c], j, y) + fine_rows(R.at[c], j, y + 1))

    @pl.loop(0, PARTS)
    def _(n):
        y = pl.multiple_of(n * part, part)
        y2 = pl.multiple_of(n * part2, part2)
        y3 = pl.multiple_of(n * part3, part3)
        at2, at3 = pl.ds(y2, part2), pl.ds(y3, part3)
        sides = {}
        for m, M in enumerate((H, K)):
            mid = x_face(M, 2, 3, y)
            close = x_face(M, p_near, q_near, y)
            W2[m, 1, at2, :] = mid
            W2[m, 2 - 2 * odd, at2, :] = close
            W3[m, 1 - odd, at3, :] = quads(
                coarse_rows(m, 2 - 2 * odd, y2, 0) + coarse_rows(m, 2 - 2 * odd, y2, 1))
            for j in range(2):
                r7, r8, r9, r10 = [
                    fine_rows(M, 1 + 2 * j, OFF + y + d) + fine_rows(M, 2 + 2 * j, OFF + y + d) for d in (-1, 0, 1, 2)]
                yl, yu = pairs(r7 + r8), pairs(r9 + r10)
                cell = r8 + r9
                low = cell + from_below(cell, 1)
                high = cell + from_above(cell, 1)
                zl = jnp.where(odd2, roll(low, 1), low)
                zu = jnp.where(odd2, high, roll(high, -1))
                for slot, value in ((3, yl), (5, yu), (7, zl), (9, zu)):
                    W2[m, slot + j, at2, :] = value
                sides[m, j, 0] = mid
                sides[m, j, 1] = yl + yu
                sides[m, j, 2] = zl + zu
            W3[m, 2, at3, :] = quads(coarse_rows(m, 3, y2, 0) + coarse_rows(m, 4, y2, 0))
            W3[m, 3, at3, :] = quads(coarse_rows(m, 5, y2, 1) + coarse_rows(m, 6, y2, 1))
            low = coarse_rows(m, 7, y2, 0) + coarse_rows(m, 7, y2, 1)
            low = low + coarse_rows(m, 8, y2, 0) + coarse_rows(m, 8, y2, 1)
            high = coarse_rows(m, 9, y2, 0) + coarse_rows(m, 9, y2, 1)
            high = high + coarse_rows(m, 10, y2, 0) + coarse_rows(m, 10, y2, 1)
            W3[m, 4, at3, :] = jnp.where(high3, roll(low, 2), low)
            W3[m, 5, at3, :] = jnp.where(high3, high, roll(high, -2))
        for c in range(3):
            kx, ky, kz = kinds(c)
            for j in range(2):
                I2[c, j, at2, :] = sides[kx, j, 0] + sides[ky, j, 1] + sides[kz, j, 2]
            inv = relaxation / (I2[c, j_near, at2, :] + W2[kx, 2 - 2 * odd, at2, :])
            I2[c, j_near, at2, :] = inv
            res = residual_two(c, j_near, y)
            EX[c, j_near, at2, :] = res
            F2[c, 1 + j_near, pl.ds(OFF + y2, part2), :] = res * inv
            I3[c, at3, :] = (W3[kx, 1 - odd, at3, :] + W3[ky, 2, at3, :] + W3[ky, 3, at3, :]
                             + W3[kz, 4, at3, :] + W3[kz, 5, at3, :])

    half = part2 // 2
    odd_half = odd2[:half]

    def packed(V, c, p, y2):
        return jnp.where(odd_half, V[c, p, pl.ds(OFF + y2 + half, half), :], V[c, p, pl.ds(OFF + y2, half), :])

    own2 = jnp.where(sec == 0, OFF + Y2 - 1, OFF)
    own3 = jnp.where(sec == 0, OFF + Y3 - 1, OFF)
    halo2 = jnp.where(sec == 0, OFF + Y2, OFF - 1)
    halo3 = jnp.where(sec == 0, OFF + Y3, OFF - 1)
    edge2 = jnp.where(sec == 0, OFF - 1, OFF + Y2)
    edge3 = jnp.where(sec == 0, OFF - 1, OFF + Y3)
    quad_row = lanes((1, Z)) & 3
    odd_row = (quad_row & 1) == 1
    fine_faces = [(c, p) for c in range(3) for p in range(1, X + 1)]
    for c in range(3):
        F2[c, 1, pl.ds(edge2, 1), :] = zero_row
        F2[c, 2, pl.ds(edge2, 1), :] = zero_row
        F3[c, 1, pl.ds(edge3, 1), :] = zero_row

    def pack_rows():
        for r, (c, p) in enumerate(fine_faces):
            S2[pl.ds(r, 1), :] = F[c, p, pl.ds(own_row, 1), :]
        deep = zero_row
        for c in range(3):
            S2[pl.ds(12 + c, 1), :] = jnp.where(odd_row, F2[c, 2, pl.ds(own2, 1), :], F2[c, 1, pl.ds(own2, 1), :])
            deep = jnp.where(quad_row == c, F3[c, 1, pl.ds(own3, 1), :], deep)
        S2[pl.ds(15, 1), :] = deep

    def unpack_rows():
        for r, (c, p) in enumerate(fine_faces):
            F[c, p, pl.ds(halo_row, 1), :] = S2R[pl.ds(r, 1), :]
        deep = S2R[pl.ds(15, 1), :]
        for c in range(3):
            v = S2R[pl.ds(12 + c, 1), :]
            F2[c, 1, pl.ds(halo2, 1), :] = jnp.where(odd_row, roll(v, 1), v)
            F2[c, 2, pl.ds(halo2, 1), :] = jnp.where(odd_row, v, roll(v, -1))
            F3[c, 1, pl.ds(halo3, 1), :] = spread_quad(deep, c, quad_row)

    def spread_quad(v, c, quad):
        spread = v
        for lane in range(4):
            if lane != c:
                spread = jnp.where(quad == lane, roll(v, lane - c), spread)
        return spread

    cross2 = remote(S2, S2R, base + 5, across)

    @pl.loop(0, PARTS)
    def _(k):
        y = part_of(k)

        @pl.when(has_far)
        def _():
            for copy in far1(k):
                copy.wait_recv()

        for i in range(part // 8):
            outer_face(p_far, q_far, pl.multiple_of(y + i * 8, 8), has_far)

        y2, y3 = pl.multiple_of(y // 2, part2), pl.multiple_of(y // 4, part3)
        at2, at3 = pl.ds(y2, part2), pl.ds(y3, part3)
        for m, M in enumerate((H, K)):
            W2[m, 2 * odd, at2, :] = x_face(M, p_far, q_far, y)
            W3[m, odd, at3, :] = quads(coarse_rows(m, 2 * odd, y2, 0) + coarse_rows(m, 2 * odd, y2, 1))
        deep = jnp.zeros(shape3, jnp.float32)
        for c in range(3):
            kx = kinds(c)[0]
            inv = relaxation / (I2[c, j_far, at2, :] + W2[kx, 2 * odd, at2, :])
            I2[c, j_far, at2, :] = inv
            res = residual_two(c, j_far, y)
            EX[c, j_far, at2, :] = res
            F2[c, 1 + j_far, pl.ds(OFF + y2, part2), :] = res * inv
            inv = relaxation / (I3[c, at3, :] + W3[kx, odd, at3, :])
            I3[c, at3, :] = inv
            res = EX[c, 0, pl.ds(y2, part3, stride=2), :] + EX[c, 0, pl.ds(y2 + 1, part3, stride=2), :]
            res = res + EX[c, 1, pl.ds(y2, part3, stride=2), :] + EX[c, 1, pl.ds(y2 + 1, part3, stride=2), :]
            first = quads(res) * inv
            F3[c, 1, pl.ds(OFF + y3, part3), :] = first
            deep = jnp.where(quad == c, first, deep)
            PF[k, pl.ds(half * c, half), :] = packed(F2, c, 1 + j_far, y2)
            PN[k, pl.ds(half * c, half), :] = packed(F2, c, 1 + j_near, y2)
        PF[k, pl.ds(3 * half, part3), :] = deep
        PN[k, pl.ds(3 * half, part3), :] = deep

        @pl.when(has_far)
        def _():
            c_far(k).start()
            f_far(k).start()

        @pl.when(k == 0)
        def _():
            pack_rows()
            cross2.start()

    c_near = remote(PN, QN, base + 6, near)
    c_near.start()

    def inner_sweep(y):
        here = pl.ds(y, 8)
        for p in range(1, X + 1):
            w = weights(p, y)
            for c in range(3):
                total, v = neighbours(F, c, p, y, w)
                E[c, p - 1, here, :] = (4.0 / 3.0) * v + INV[c, p - 1, here, :] * total

    def outer_sweep(target, p, q, y):
        here, there = pl.ds(y, 8), pl.ds(OFF + y, 8)
        s = H[q, there, :] + H[p, there, :]
        t = K[q, there, :] + K[p, there, :]
        for c in range(3):
            w = t if c == 0 else s
            target[c, p - 1, here, :] = target[c, p - 1, here, :] + INV[c, p - 1, here, :] * (w * F[c, q, there, :])

    f_near.wait_recv()

    @pl.loop(0, Y // 8 - 1)
    def _(i):
        y = pl.multiple_of((i + sec) * 8, 8)
        inner_sweep(y)
        outer_sweep(E, p_near, q_near, y)

    cross2.wait()
    unpack_rows()
    inner_sweep(halo_chunk)
    outer_sweep(E, p_near, q_near, halo_chunk)

    def unpack(Q, k, q2, q3, present):
        y = part_of(k)
        y2, y3 = y // 2, y // 4
        for c in range(3):
            v = Q[k, pl.ds(half * c, half), :]
            if present is not None:
                v = jnp.where(present, v, 0.0)
            F2[c, q2, pl.ds(OFF + y2, half), :] = jnp.where(odd_half, roll(v, 1), v)
            F2[c, q2, pl.ds(OFF + y2 + half, half), :] = jnp.where(odd_half, v, roll(v, -1))
        v = Q[k, pl.ds(3 * half, part3), :]
        if present is not None:
            v = jnp.where(present, v, 0.0)
        for c in range(3):
            F3[c, q3, pl.ds(OFF + y3, part3), :] = spread_quad(v, c, quad)

    c_near.wait_recv()
    for k in range(PARTS):
        unpack(QN, k, 3 * (1 - odd), 2 * (1 - odd), None)

    @pl.loop(0, PARTS)
    def _(k):
        y = part_of(k)
        y2, y3 = pl.multiple_of(y // 2, part2), pl.multiple_of(y // 4, part3)
        at2, at3 = pl.ds(y2, part2), pl.ds(y3, part3)

        @pl.when(has_far)
        def _():
            c_far(k).wait_recv()

        unpack(QF, k, 3 * odd, 2 * odd, has_far)
        for c in range(3):
            kx, ky, kz = kinds(c)

            def f3(p, d):
                return F3[c, p, pl.ds(OFF + y3 + d, part3), :]

            v = f3(1, 0)
            total = W3[kx, 0, at3, :] * f3(0, 0) + W3[kx, 1, at3, :] * f3(2, 0)
            total = total + W3[ky, 2, at3, :] * f3(1, -1) + W3[ky, 3, at3, :] * f3(1, 1)
            total = total + W3[kz, 4, at3, :] * from_below(v, 4) + W3[kz, 5, at3, :] * from_above(v, 4)
            e3 = (4.0 / 3.0) * v + I3[c, at3, :] * total
            EX[c, 0, pl.ds(y2, part3, stride=2), :] = e3
            EX[c, 0, pl.ds(y2 + 1, part3, stride=2), :] = e3
            e3 = EX[c, 0, at2, :]

            def f2(p, d):
                return F2[c, p, pl.ds(OFF + y2 + d, part2), :]

            for j in range(2):
                p = 1 + j
                v = f2(p, 0)
                total = W2[kx, j, at2, :] * f2(p - 1, 0) + W2[kx, j + 1, at2, :] * f2(p + 1, 0)
                total = total + W2[ky, 3 + j, at2, :] * f2(p, -1) + W2[ky, 5 + j, at2, :] * f2(p, 1)
                total = total + W2[kz, 7 + j, at2, :] * from_below(v, 2) + W2[kz, 9 + j, at2, :] * from_above(v, 2)
                e2 = (4.0 / 3.0) * v + I2[c, j, at2, :] * total + e3
                R[c, j, pl.ds(y, part2, stride=2), :] = e2
                R[c, j, pl.ds(y + 1, part2, stride=2), :] = e2
        for i in range(part // 8):
            here = pl.ds(pl.multiple_of(y + i * 8, 8), 8)
            for p in range(X):
                for c in range(3):
                    out[c, p, here, :] = E[c, p, here, :] + R[c, p // 2, here, :]

        @pl.when(has_far)
        def _():
            f_far(k).wait_recv()

        for i in range(part // 8):
            outer_sweep(out, p_far, q_far, pl.multiple_of(y + i * 8, 8))

    for copy in near1 + [f_near, c_near]:
        copy.wait_send()

    @pl.when(has_far)
    def _():
        for k in range(PARTS):
            for copy in far1(k) + [f_far(k), c_far(k)]:
                copy.wait_send()


def per_device(tiles, load_field, iterate, phase_label, damage):
    f32, i32 = jnp.float32, jnp.int32
    padded = Y + 2 * OFF
    return pl.pallas_call(
        functools.partial(kernel, tiles),
        out_shape=jax.ShapeDtypeStruct(load_field.shape, f32),
        in_specs=[pl.BlockSpec(memory_space=pltpu.HBM)] * 4,
        out_specs=pl.BlockSpec(memory_space=pltpu.VMEM),
        scratch_shapes=[
            pltpu.VMEM((3, X + 2, padded, Z), f32),
            pltpu.VMEM((3, X + 2, padded, Z), f32),
            pltpu.VMEM((3, X, Y, Z), f32),
            pltpu.VMEM((3, X, Y, Z), f32),
            pltpu.VMEM((3, X // 2, Y, Z), f32),
            pltpu.VMEM((3, X, Y, Z), f32),
            pltpu.VMEM((X + 2, padded, Z), f32),
            pltpu.VMEM((X + 2, padded, Z), f32),
            pltpu.VMEM((X + 2, Y, Z), i32),
            pltpu.VMEM((X + 2, Y, Z), i32),
            pltpu.VMEM((20, Z), f32),
            pltpu.VMEM((20, Z), f32),
            pltpu.VMEM((16, Z), f32),
            pltpu.VMEM((16, Z), f32),
            pltpu.VMEM((PARTS, Y // PARTS, Z), f32),
            pltpu.VMEM((PARTS, Y // PARTS, Z), f32),
            pltpu.VMEM((PARTS, Y // PARTS, Z), f32),
            pltpu.VMEM((PARTS, Y // PARTS, Z), f32),
            pltpu.VMEM((2, 11, Y // 2, Z), f32),
            pltpu.VMEM((3, 4, Y // 2 + 2 * OFF, Z), f32),
            pltpu.VMEM((3, 2, Y // 2, Z), f32),
            pltpu.VMEM((2, 6, Y // 4, Z), f32),
            pltpu.VMEM((3, 3, Y // 4 + 2 * OFF, Z), f32),
            pltpu.VMEM((3, Y // 4, Z), f32),
            pltpu.VMEM((3, 2, Y // 2, Z), f32),
            pltpu.SemaphoreType.DMA((4,)),
            pltpu.SemaphoreType.DMA((5 * PARTS + 7,)),
            pltpu.SemaphoreType.DMA((5 * PARTS + 7,)),
        ],
        compiler_params=pltpu.CompilerParams(
            collective_id=0, has_side_effects=True, vmem_limit_bytes=48 * 1024 * 1024),
    )(*[pltpu.with_memory_space_constraint(a, pltpu.HBM) for a in (load_field, iterate, phase_label, damage)])


def solution(mesh):
    tiles = mesh.shape["tile"]
    in_specs = (
        P(None, "tile", "sec", None),
        P(None, "tile", "sec", None),
        P("tile", "sec", None),
        P("tile", "sec", None),
    )
    out_specs = P(None, "tile", "sec", None)
    return jax.shard_map(
        functools.partial(per_device, tiles), mesh=mesh, in_specs=in_specs, out_specs=out_specs, check_vma=False
    )
```

```python
import functools

import jax
import jax.numpy as jnp
from jax import lax
from jax.experimental import pallas as pl
from jax.experimental.pallas import tpu as pltpu
from jax.sharding import PartitionSpec as P

shear_table = (1.0, 0.6, 1.8, 0.35)
bulk_table = (1.2, 0.9, 2.5, 0.5)
damage_step = 0.25
damage_floor = 0.01
relaxation = 2.0 / 3.0

MESH = pl.DeviceIdType.MESH
X = 4
Y = 128
Z = 128
PARTS = 2
OFF = 8


def lanes(shape):
    return lax.broadcasted_iota(jnp.int32, shape, len(shape) - 1)


def roll(v, shift):
    return pltpu.roll(v, shift % Z, v.ndim - 1)


def from_above(v, step):
    return jnp.where(lanes(v.shape) < Z - step, roll(v, -step), 0.0)


def from_below(v, step):
    return jnp.where(lanes(v.shape) >= step, roll(v, step), 0.0)


def moduli(phase, damage):
    soft = 1.0 - damage_step * damage.astype(jnp.float32)
    degrade = soft * soft + damage_floor

    def table(values):
        picked = jnp.full(phase.shape, values[3], jnp.float32)
        for label in (2, 1, 0):
            picked = jnp.where(phase == label, values[label], picked)
        return picked

    half = table([0.5 * s for s in shear_table])
    normal = table([0.5 * b + s for s, b in zip(shear_table, bulk_table)])
    return half * degrade, normal * degrade


def kernel(tiles, load_hbm, u_hbm, lab_hbm, dam_hbm, out, U, F, L, INV, R, E, H, K, CODE, S1, S1R, S2, S2R,
           PN, QN, PF, QF, W2, F2, I2, W3, F3, I3, EX, local_sem, send_sem, recv_sem):
    LAB, DAM = CODE.at[0], CODE.at[1]
    me = lax.axis_index("tile")
    sec = lax.axis_index("sec")
    odd = lax.rem(me, 2)
    has_far = jnp.logical_and(me > 0, me < tiles - 1)
    near = {"tile": me + 1 - 2 * odd}
    far = {"tile": jnp.clip(me - 1 + 2 * odd, 0, tiles - 1)}
    across = {"sec": 1 - sec}
    p_near, q_near = X - (X - 1) * odd, (X + 1) * (1 - odd)
    p_far, q_far = 1 + (X - 1) * odd, (X + 1) * odd

    barrier = pltpu.get_barrier_semaphore()
    pl.semaphore_signal(barrier, inc=1, device_id=near, device_id_type=MESH)

    @pl.when(has_far)
    def _():
        pl.semaphore_signal(barrier, inc=1, device_id=far, device_id_type=MESH)

    pl.semaphore_signal(barrier, inc=1, device_id=across, device_id_type=MESH)

    loads = [
        pltpu.make_async_copy(lab_hbm, LAB.at[pl.ds(1, X)], local_sem.at[0]),
        pltpu.make_async_copy(dam_hbm, DAM.at[pl.ds(1, X)], local_sem.at[1]),
        pltpu.make_async_copy(u_hbm, U.at[:, pl.ds(1, X), pl.ds(OFF, Y)], local_sem.at[2]),
        pltpu.make_async_copy(load_hbm, L, local_sem.at[3]),
    ]
    for copy in loads[:3]:
        copy.start()

    own_row = jnp.where(sec == 0, OFF + Y - 1, OFF)
    halo_row = jnp.where(sec == 0, OFF + Y, OFF - 1)
    edge_row = jnp.where(sec == 0, OFF - 1, OFF + Y)
    faces = [H.at[pl.ds(1, X)], K.at[pl.ds(1, X)]] + [U.at[c, pl.ds(1, X)] for c in range(3)]
    zero_row = jnp.zeros((1, Z), jnp.float32)
    for copy in loads[:2]:
        copy.wait()
    for p in range(X):
        h, k = moduli(LAB[1 + p, pl.ds(own_row - OFF, 1), :], DAM[1 + p, pl.ds(own_row - OFF, 1), :])
        S1[pl.ds(p, 1), :] = h
        S1[pl.ds(X + p, 1), :] = k
    loads[2].wait()
    for f in range(2, 5):
        for p in range(X):
            S1[pl.ds(X * f + p, 1), :] = faces[f][p, pl.ds(own_row, 1), :]
    pl.semaphore_wait(barrier, 2 + has_far.astype(jnp.int32))

    def remote(src, dst, index, device):
        return pltpu.make_async_remote_copy(
            src_ref=src, dst_ref=dst, send_sem=send_sem.at[index], recv_sem=recv_sem.at[index],
            device_id=device, device_id_type=MESH)

    rows = pl.ds(OFF, Y)
    part = Y // PARTS
    base = 5 * PARTS

    def part_of(k):
        n = k + (1 - sec) * (PARTS - 1 - 2 * k)
        return pl.multiple_of(n * part, part)

    def far1(k):
        y = part_of(k)
        here, there = pl.ds(y, part), pl.ds(OFF + y, part)
        return [
            remote(CODE.at[:, p_far, here], CODE.at[:, X + 1 - q_far, here], 3 * k, far),
            remote(U.at[:, p_far, there], U.at[:, X + 1 - q_far, there], 3 * k + 2, far),
        ]

    def f_far(k):
        there = pl.ds(OFF + part_of(k), part)
        return remote(F.at[:, p_far, there], F.at[:, X + 1 - q_far, there], 3 * PARTS + k, far)

    def c_far(k):
        return remote(PF.at[k], QF.at[k], 4 * PARTS + k, far)

    near1 = [
        remote(CODE.at[:, p_near], CODE.at[:, X + 1 - q_near], base, near),
        remote(U.at[:, p_near, rows], U.at[:, X + 1 - q_near, rows], base + 2, near),
    ]
    cross1 = remote(S1, S1R, base + 3, across)
    cross1.start()

    @pl.when(has_far)
    def _():
        for k in range(PARTS):
            for copy in far1(k):
                copy.start()

    for copy in near1:
        copy.start()

    loads[3].start()

    @pl.loop(0, Y // 8)
    def _(i):
        y = pl.multiple_of(i * 8, 8)
        for p in range(1, X + 1):
            h, k = moduli(LAB[p, pl.ds(y, 8), :], DAM[p, pl.ds(y, 8), :])
            H[p, pl.ds(OFF + y, 8), :] = h
            K[p, pl.ds(OFF + y, 8), :] = k

    for ref in faces:
        for p in range(X):
            ref[p, pl.ds(edge_row, 1), :] = zero_row
    for c in range(3):
        for p in range(1, X + 1):
            F[c, p, pl.ds(edge_row, 1), :] = zero_row

    @pl.when(jnp.logical_not(has_far))
    def _():
        for ref in (H, K):
            ref[q_far] = jnp.zeros(H.shape[1:], jnp.float32)
        for c in range(3):
            U[c, q_far] = jnp.zeros(U.shape[2:], jnp.float32)
            F[c, q_far] = jnp.zeros(F.shape[2:], jnp.float32)

    def weights(p, y):
        result = {}
        for name, M in (("s", H), ("t", K)):
            m = M[p, pl.ds(OFF + y, 8), :]
            if p > 1:
                result[name, "xl"] = m + M[p - 1, pl.ds(OFF + y, 8), :]
            if p < X:
                result[name, "xu"] = m + M[p + 1, pl.ds(OFF + y, 8), :]
            result[name, "yl"] = m + M[p, pl.ds(OFF + y - 1, 8), :]
            result[name, "yu"] = m + M[p, pl.ds(OFF + y + 1, 8), :]
            result[name, "zl"] = m + from_below(m, 1)
            result[name, "zu"] = m + from_above(m, 1)
        return result

    def neighbours(V, c, p, y, w):
        v = V[c, p, pl.ds(OFF + y, 8), :]
        kind = ["t" if c == a else "s" for a in range(3)]
        total = w[kind[1], "yl"] * V[c, p, pl.ds(OFF + y - 1, 8), :]
        total = total + w[kind[1], "yu"] * V[c, p, pl.ds(OFF + y + 1, 8), :]
        total = total + w[kind[2], "zl"] * from_below(v, 1)
        total = total + w[kind[2], "zu"] * from_above(v, 1)
        if p > 1:
            total = total + w[kind[0], "xl"] * V[c, p - 1, pl.ds(OFF + y, 8), :]
        if p < X:
            total = total + w[kind[0], "xu"] * V[c, p + 1, pl.ds(OFF + y, 8), :]
        return total, v

    def inner_residual(y):
        here = pl.ds(y, 8)
        for p in range(1, X + 1):
            w = weights(p, y)
            sides = {}
            for name in ("s", "t"):
                xs = [w[name, side] for side in ("xl", "xu") if (name, side) in w]
                sides[name, 0] = xs[0] if len(xs) == 1 else xs[0] + xs[1]
                sides[name, 1] = w[name, "yl"] + w[name, "yu"]
                sides[name, 2] = w[name, "zl"] + w[name, "zu"]
            for c in range(3):
                total, v = neighbours(U, c, p, y, w)
                others = [a for a in range(3) if a != c]
                diag = sides["t", c] + sides["s", others[0]] + sides["s", others[1]]
                acc = L[c, p - 1, here, :] + total
                if 1 < p < X:
                    r = acc - diag * v
                    inv = relaxation / diag
                    R[c, p - 2, here, :] = r
                    INV[c, p - 1, here, :] = inv
                    F[c, p, pl.ds(OFF + y, 8), :] = r * inv
                else:
                    L[c, p - 1, here, :] = acc
                    INV[c, p - 1, here, :] = diag

    halo_chunk = pl.multiple_of((1 - sec) * (Y - 8), 8)
    loads[3].wait()

    @pl.loop(0, Y // 8 - 1)
    def _(i):
        inner_residual(pl.multiple_of((i + sec) * 8, 8))

    cross1.wait()
    for f, ref in enumerate(faces):
        for p in range(X):
            ref[p, pl.ds(halo_row, 1), :] = S1R[pl.ds(X * f + p, 1), :]
    inner_residual(halo_chunk)

    def outer_face(p, q, y, present):
        here, there = pl.ds(y, 8), pl.ds(OFF + y, 8)
        h, k = moduli(LAB[q, here, :], DAM[q, here, :])
        if present is not None:
            h = jnp.where(present, h, 0.0)
            k = jnp.where(present, k, 0.0)
        H[q, there, :] = h
        K[q, there, :] = k
        s = h + H[p, there, :]
        t = k + K[p, there, :]
        j = (p - 1) // 2
        for c in range(3):
            w = t if c == 0 else s
            diag = INV[c, p - 1, here, :] + w
            r = L[c, p - 1, here, :] + w * U[c, q, there, :] - diag * U[c, p, there, :]
            inv = relaxation / diag
            INV[c, p - 1, here, :] = inv
            F[c, p, there, :] = r * inv
            R[c, j, here, :] = R[c, j, here, :] + r

    for copy in near1:
        copy.wait_recv()

    @pl.loop(0, Y // 8)
    def _(i):
        outer_face(p_near, q_near, pl.multiple_of(i * 8, 8), None)

    f_near = remote(F.at[:, p_near, rows], F.at[:, X + 1 - q_near, rows], base + 4, near)
    f_near.start()

    Y2, Y3 = Y // 2, Y // 4
    part2, part3 = part // 2, part // 4
    shape2, shape3 = (part2, Z), (part3, Z)
    odd2 = (lanes(shape2) & 1) == 1
    quad = lanes(shape3) & 3
    high3 = quad >= 2
    j_near, j_far = 1 - odd, odd

    def pairs(v):
        return v + jnp.where(odd2, roll(v, 1), roll(v, -1))

    def quads(v):
        return v + jnp.where(high3, roll(v, 2), roll(v, -2))

    def fine_rows(M, p, first):
        return M[p, pl.ds(first, part2, stride=2), :]

    def coarse_rows(m, slot, y2, first):
        return W2[m, slot, pl.ds(y2 + first, part3, stride=2), :]

    def kinds(c):
        return [1 if c == a else 0 for a in range(3)]

    def x_face(M, p, q, y):
        face = fine_rows(M, p, OFF + y) + fine_rows(M, p, OFF + y + 1)
        return pairs(face + fine_rows(M, q, OFF + y) + fine_rows(M, q, OFF + y + 1))

    def residual_two(c, j, y):
        return pairs(fine_rows(R.at[c], j, y) + fine_rows(R.at[c], j, y + 1))

    @pl.loop(0, PARTS)
    def _(n):
        y = pl.multiple_of(n * part, part)
        y2 = pl.multiple_of(n * part2, part2)
        y3 = pl.multiple_of(n * part3, part3)
        at2, at3 = pl.ds(y2, part2), pl.ds(y3, part3)
        sides = {}
        for m, M in enumerate((H, K)):
            mid = x_face(M, 2, 3, y)
            close = x_face(M, p_near, q_near, y)
            W2[m, 1, at2, :] = mid
            W2[m, 2 - 2 * odd, at2, :] = close
            W3[m, 1 - odd, at3, :] = quads(
                coarse_rows(m, 2 - 2 * odd, y2, 0) + coarse_rows(m, 2 - 2 * odd, y2, 1))
            for j in range(2):
                r7, r8, r9, r10 = [
                    fine_rows(M, 1 + 2 * j, OFF + y + d) + fine_rows(M, 2 + 2 * j, OFF + y + d) for d in (-1, 0, 1, 2)]
                yl, yu = pairs(r7 + r8), pairs(r9 + r10)
                cell = r8 + r9
                low = cell + from_below(cell, 1)
                high = cell + from_above(cell, 1)
                zl = jnp.where(odd2, roll(low, 1), low)
                zu = jnp.where(odd2, high, roll(high, -1))
                for slot, value in ((3, yl), (5, yu), (7, zl), (9, zu)):
                    W2[m, slot + j, at2, :] = value
                sides[m, j, 0] = mid
                sides[m, j, 1] = yl + yu
                sides[m, j, 2] = zl + zu
            W3[m, 2, at3, :] = quads(coarse_rows(m, 3, y2, 0) + coarse_rows(m, 4, y2, 0))
            W3[m, 3, at3, :] = quads(coarse_rows(m, 5, y2, 1) + coarse_rows(m, 6, y2, 1))
            low = coarse_rows(m, 7, y2, 0) + coarse_rows(m, 7, y2, 1)
            low = low + coarse_rows(m, 8, y2, 0) + coarse_rows(m, 8, y2, 1)
            high = coarse_rows(m, 9, y2, 0) + coarse_rows(m, 9, y2, 1)
            high = high + coarse_rows(m, 10, y2, 0) + coarse_rows(m, 10, y2, 1)
            W3[m, 4, at3, :] = jnp.where(high3, roll(low, 2), low)
            W3[m, 5, at3, :] = jnp.where(high3, high, roll(high, -2))
        for c in range(3):
            kx, ky, kz = kinds(c)
            for j in range(2):
                I2[c, j, at2, :] = sides[kx, j, 0] + sides[ky, j, 1] + sides[kz, j, 2]
            inv = relaxation / (I2[c, j_near, at2, :] + W2[kx, 2 - 2 * odd, at2, :])
            I2[c, j_near, at2, :] = inv
            res = residual_two(c, j_near, y)
            EX[c, j_near, at2, :] = res
            F2[c, 1 + j_near, pl.ds(OFF + y2, part2), :] = res * inv
            I3[c, at3, :] = (W3[kx, 1 - odd, at3, :] + W3[ky, 2, at3, :] + W3[ky, 3, at3, :]
                             + W3[kz, 4, at3, :] + W3[kz, 5, at3, :])

    half = part2 // 2
    odd_half = odd2[:half]

    deep_pieces = [
        (0, part3 // 2, [(0, 0), (0, part3 // 2), (1, 0), (1, part3 // 2)]),
        (part3 // 2, part3 // 4, [(2, n * (part3 // 4)) for n in range(4)]),
    ]

    def packed(V, c, p, y2):
        return jnp.where(odd_half, V[c, p, pl.ds(OFF + y2 + half, half), :], V[c, p, pl.ds(OFF + y2, half), :])

    own2 = jnp.where(sec == 0, OFF + Y2 - 1, OFF)
    own3 = jnp.where(sec == 0, OFF + Y3 - 1, OFF)
    halo2 = jnp.where(sec == 0, OFF + Y2, OFF - 1)
    halo3 = jnp.where(sec == 0, OFF + Y3, OFF - 1)
    edge2 = jnp.where(sec == 0, OFF - 1, OFF + Y2)
    edge3 = jnp.where(sec == 0, OFF - 1, OFF + Y3)
    quad_row = lanes((1, Z)) & 3
    odd_row = (quad_row & 1) == 1
    fine_faces = [(c, p) for c in range(3) for p in range(1, X + 1)]
    for c in range(3):
        F2[c, 1, pl.ds(edge2, 1), :] = zero_row
        F2[c, 2, pl.ds(edge2, 1), :] = zero_row
        F3[c, 1, pl.ds(edge3, 1), :] = zero_row

    def pack_rows():
        for r, (c, p) in enumerate(fine_faces):
            S2[pl.ds(r, 1), :] = F[c, p, pl.ds(own_row, 1), :]
        deep = zero_row
        for c in range(3):
            S2[pl.ds(12 + c, 1), :] = jnp.where(odd_row, F2[c, 2, pl.ds(own2, 1), :], F2[c, 1, pl.ds(own2, 1), :])
            deep = jnp.where(quad_row == c, F3[c, 1, pl.ds(own3, 1), :], deep)
        S2[pl.ds(15, 1), :] = deep

    def unpack_rows():
        for r, (c, p) in enumerate(fine_faces):
            F[c, p, pl.ds(halo_row, 1), :] = S2R[pl.ds(r, 1), :]
        deep = S2R[pl.ds(15, 1), :]
        for c in range(3):
            v = S2R[pl.ds(12 + c, 1), :]
            F2[c, 1, pl.ds(halo2, 1), :] = jnp.where(odd_row, roll(v, 1), v)
            F2[c, 2, pl.ds(halo2, 1), :] = jnp.where(odd_row, v, roll(v, -1))
            F3[c, 1, pl.ds(halo3, 1), :] = spread_quad(deep, c, quad_row)

    def spread_quad(v, c, quad):
        spread = v
        for lane in range(4):
            if lane != c:
                spread = jnp.where(quad == lane, roll(v, lane - c), spread)
        return spread

    cross2 = remote(S2, S2R, base + 5, across)

    @pl.loop(0, PARTS)
    def _(k):
        y = part_of(k)

        @pl.when(has_far)
        def _():
            for copy in far1(k):
                copy.wait_recv()

        for i in range(part // 8):
            outer_face(p_far, q_far, pl.multiple_of(y + i * 8, 8), has_far)

        y2, y3 = pl.multiple_of(y // 2, part2), pl.multiple_of(y // 4, part3)
        at2, at3 = pl.ds(y2, part2), pl.ds(y3, part3)
        for m, M in enumerate((H, K)):
            W2[m, 2 * odd, at2, :] = x_face(M, p_far, q_far, y)
            W3[m, odd, at3, :] = quads(coarse_rows(m, 2 * odd, y2, 0) + coarse_rows(m, 2 * odd, y2, 1))
        for c in range(3):
            kx = kinds(c)[0]
            inv = relaxation / (I2[c, j_far, at2, :] + W2[kx, 2 * odd, at2, :])
            I2[c, j_far, at2, :] = inv
            res = residual_two(c, j_far, y)
            EX[c, j_far, at2, :] = res
            F2[c, 1 + j_far, pl.ds(OFF + y2, part2), :] = res * inv
            inv = relaxation / (I3[c, at3, :] + W3[kx, odd, at3, :])
            I3[c, at3, :] = inv
            res = EX[c, 0, pl.ds(y2, part3, stride=2), :] + EX[c, 0, pl.ds(y2 + 1, part3, stride=2), :]
            res = res + EX[c, 1, pl.ds(y2, part3, stride=2), :] + EX[c, 1, pl.ds(y2 + 1, part3, stride=2), :]
            first = quads(res) * inv
            F3[c, 1, pl.ds(OFF + y3, part3), :] = first
            PF[k, pl.ds(half * c, half), :] = packed(F2, c, 1 + j_far, y2)
            PN[k, pl.ds(half * c, half), :] = packed(F2, c, 1 + j_near, y2)
        for first_row, count, pieces in deep_pieces:
            quad_now = quad[:count]
            deep = F3[pieces[0][0], 1, pl.ds(OFF + y3 + pieces[0][1], count), :]
            for slot in range(1, 4):
                c, row = pieces[slot]
                deep = jnp.where(quad_now == slot, F3[c, 1, pl.ds(OFF + y3 + row, count), :], deep)
            PF[k, pl.ds(3 * half + first_row, count), :] = deep
            PN[k, pl.ds(3 * half + first_row, count), :] = deep

        @pl.when(has_far)
        def _():
            c_far(k).start()
            f_far(k).start()

        @pl.when(k == 0)
        def _():
            pack_rows()
            cross2.start()

    c_near = remote(PN, QN, base + 6, near)
    c_near.start()

    def inner_sweep(y):
        here = pl.ds(y, 8)
        for p in range(1, X + 1):
            w = weights(p, y)
            for c in range(3):
                total, v = neighbours(F, c, p, y, w)
                E[c, p - 1, here, :] = (4.0 / 3.0) * v + INV[c, p - 1, here, :] * total

    def outer_sweep(target, p, q, y):
        here, there = pl.ds(y, 8), pl.ds(OFF + y, 8)
        s = H[q, there, :] + H[p, there, :]
        t = K[q, there, :] + K[p, there, :]
        for c in range(3):
            w = t if c == 0 else s
            target[c, p - 1, here, :] = target[c, p - 1, here, :] + INV[c, p - 1, here, :] * (w * F[c, q, there, :])

    f_near.wait_recv()

    @pl.loop(0, Y // 8 - 1)
    def _(i):
        y = pl.multiple_of((i + sec) * 8, 8)
        inner_sweep(y)
        outer_sweep(E, p_near, q_near, y)

    cross2.wait()
    unpack_rows()
    inner_sweep(halo_chunk)
    outer_sweep(E, p_near, q_near, halo_chunk)

    def unpack(Q, k, q2, q3, present):
        y = part_of(k)
        y2, y3 = y // 2, y // 4
        for c in range(3):
            v = Q[k, pl.ds(half * c, half), :]
            if present is not None:
                v = jnp.where(present, v, 0.0)
            F2[c, q2, pl.ds(OFF + y2, half), :] = jnp.where(odd_half, roll(v, 1), v)
            F2[c, q2, pl.ds(OFF + y2 + half, half), :] = jnp.where(odd_half, v, roll(v, -1))
        for first_row, count, pieces in deep_pieces:
            v = Q[k, pl.ds(3 * half + first_row, count), :]
            if present is not None:
                v = jnp.where(present, v, 0.0)
            for slot, (c, row) in enumerate(pieces):
                F3[c, q3, pl.ds(OFF + y3 + row, count), :] = spread_quad(v, slot, quad[:count])

    c_near.wait_recv()
    for k in range(PARTS):
        unpack(QN, k, 3 * (1 - odd), 2 * (1 - odd), None)

    @pl.loop(0, PARTS)
    def _(k):
        y = part_of(k)
        y2, y3 = pl.multiple_of(y // 2, part2), pl.multiple_of(y // 4, part3)
        at2, at3 = pl.ds(y2, part2), pl.ds(y3, part3)

        @pl.when(has_far)
        def _():
            c_far(k).wait_recv()

        unpack(QF, k, 3 * odd, 2 * odd, has_far)
        for c in range(3):
            kx, ky, kz = kinds(c)

            def f3(p, d):
                return F3[c, p, pl.ds(OFF + y3 + d, part3), :]

            v = f3(1, 0)
            total = W3[kx, 0, at3, :] * f3(0, 0) + W3[kx, 1, at3, :] * f3(2, 0)
            total = total + W3[ky, 2, at3, :] * f3(1, -1) + W3[ky, 3, at3, :] * f3(1, 1)
            total = total + W3[kz, 4, at3, :] * from_below(v, 4) + W3[kz, 5, at3, :] * from_above(v, 4)
            e3 = (4.0 / 3.0) * v + I3[c, at3, :] * total
            EX[c, 0, pl.ds(y2, part3, stride=2), :] = e3
            EX[c, 0, pl.ds(y2 + 1, part3, stride=2), :] = e3
            e3 = EX[c, 0, at2, :]

            def f2(p, d):
                return F2[c, p, pl.ds(OFF + y2 + d, part2), :]

            for j in range(2):
                p = 1 + j
                v = f2(p, 0)
                total = W2[kx, j, at2, :] * f2(p - 1, 0) + W2[kx, j + 1, at2, :] * f2(p + 1, 0)
                total = total + W2[ky, 3 + j, at2, :] * f2(p, -1) + W2[ky, 5 + j, at2, :] * f2(p, 1)
                total = total + W2[kz, 7 + j, at2, :] * from_below(v, 2) + W2[kz, 9 + j, at2, :] * from_above(v, 2)
                e2 = (4.0 / 3.0) * v + I2[c, j, at2, :] * total + e3
                R[c, j, pl.ds(y, part2, stride=2), :] = e2
                R[c, j, pl.ds(y + 1, part2, stride=2), :] = e2
        for i in range(part // 8):
            here = pl.ds(pl.multiple_of(y + i * 8, 8), 8)
            for p in range(X):
                for c in range(3):
                    out[c, p, here, :] = E[c, p, here, :] + R[c, p // 2, here, :]

        @pl.when(has_far)
        def _():
            f_far(k).wait_recv()

        for i in range(part // 8):
            outer_sweep(out, p_far, q_far, pl.multiple_of(y + i * 8, 8))

    for copy in near1 + [f_near, c_near]:
        copy.wait_send()

    @pl.when(has_far)
    def _():
        for k in range(PARTS):
            for copy in far1(k) + [f_far(k), c_far(k)]:
                copy.wait_send()


def per_device(tiles, load_field, iterate, phase_label, damage):
    f32, i32 = jnp.float32, jnp.int32
    padded = Y + 2 * OFF
    return pl.pallas_call(
        functools.partial(kernel, tiles),
        out_shape=jax.ShapeDtypeStruct(load_field.shape, f32),
        in_specs=[pl.BlockSpec(memory_space=pltpu.HBM)] * 4,
        out_specs=pl.BlockSpec(memory_space=pltpu.VMEM),
        scratch_shapes=[
            pltpu.VMEM((3, X + 2, padded, Z), f32),
            pltpu.VMEM((3, X + 2, padded, Z), f32),
            pltpu.VMEM((3, X, Y, Z), f32),
            pltpu.VMEM((3, X, Y, Z), f32),
            pltpu.VMEM((3, X // 2, Y, Z), f32),
            pltpu.VMEM((3, X, Y, Z), f32),
            pltpu.VMEM((X + 2, padded, Z), f32),
            pltpu.VMEM((X + 2, padded, Z), f32),
            pltpu.VMEM((2, X + 2, Y, Z), i32),
            pltpu.VMEM((20, Z), f32),
            pltpu.VMEM((20, Z), f32),
            pltpu.VMEM((16, Z), f32),
            pltpu.VMEM((16, Z), f32),
            pltpu.VMEM((PARTS, Y * 15 // (16 * PARTS), Z), f32),
            pltpu.VMEM((PARTS, Y * 15 // (16 * PARTS), Z), f32),
            pltpu.VMEM((PARTS, Y * 15 // (16 * PARTS), Z), f32),
            pltpu.VMEM((PARTS, Y * 15 // (16 * PARTS), Z), f32),
            pltpu.VMEM((2, 11, Y // 2, Z), f32),
            pltpu.VMEM((3, 4, Y // 2 + 2 * OFF, Z), f32),
            pltpu.VMEM((3, 2, Y // 2, Z), f32),
            pltpu.VMEM((2, 6, Y // 4, Z), f32),
            pltpu.VMEM((3, 3, Y // 4 + 2 * OFF, Z), f32),
            pltpu.VMEM((3, Y // 4, Z), f32),
            pltpu.VMEM((3, 2, Y // 2, Z), f32),
            pltpu.SemaphoreType.DMA((4,)),
            pltpu.SemaphoreType.DMA((5 * PARTS + 7,)),
            pltpu.SemaphoreType.DMA((5 * PARTS + 7,)),
        ],
        compiler_params=pltpu.CompilerParams(
            collective_id=0, has_side_effects=True, vmem_limit_bytes=48 * 1024 * 1024),
    )(*[pltpu.with_memory_space_constraint(a, pltpu.HBM) for a in (load_field, iterate, phase_label, damage)])


def solution(mesh):
    tiles = mesh.shape["tile"]
    in_specs = (
        P(None, "tile", "sec", None),
        P(None, "tile", "sec", None),
        P("tile", "sec", None),
        P("tile", "sec", None),
    )
    out_specs = P(None, "tile", "sec", None)
    return jax.shard_map(
        functools.partial(per_device, tiles), mesh=mesh, in_specs=in_specs, out_specs=out_specs, check_vma=False
    )
```

```python
import functools

import jax
import jax.numpy as jnp
from jax import lax
from jax.experimental import pallas as pl
from jax.experimental.pallas import tpu as pltpu
from jax.sharding import PartitionSpec as P

shear_table = (1.0, 0.6, 1.8, 0.35)
bulk_table = (1.2, 0.9, 2.5, 0.5)
damage_step = 0.25
damage_floor = 0.01
relaxation = 2.0 / 3.0

MESH = pl.DeviceIdType.MESH
X = 4
Y = 128
Z = 128
PARTS = 2
OFF = 8


def lanes(shape):
    return lax.broadcasted_iota(jnp.int32, shape, len(shape) - 1)


def roll(v, shift):
    return pltpu.roll(v, shift % Z, v.ndim - 1)


def from_above(v, step):
    return jnp.where(lanes(v.shape) < Z - step, roll(v, -step), 0.0)


def from_below(v, step):
    return jnp.where(lanes(v.shape) >= step, roll(v, step), 0.0)


def moduli(phase, damage):
    soft = 1.0 - damage_step * damage.astype(jnp.float32)
    degrade = soft * soft + damage_floor

    def table(values):
        picked = jnp.full(phase.shape, values[3], jnp.float32)
        for label in (2, 1, 0):
            picked = jnp.where(phase == label, values[label], picked)
        return picked

    half = table([0.5 * s for s in shear_table])
    normal = table([0.5 * b + s for s, b in zip(shear_table, bulk_table)])
    return half * degrade, normal * degrade


def kernel(tiles, load_hbm, u_hbm, lab_hbm, dam_hbm, out, U, F, L, INV, R, E, CODE, S1, S1R, S2, S2R,
           PN, QN, PF, QF, W2, F2, I2, W3, F3, I3, EX, local_sem, send_sem, recv_sem):
    LAB, DAM = CODE.at[0], CODE.at[1]
    H, K = U.at[3], U.at[4]
    me = lax.axis_index("tile")
    sec = lax.axis_index("sec")
    odd = lax.rem(me, 2)
    has_far = jnp.logical_and(me > 0, me < tiles - 1)
    near = {"tile": me + 1 - 2 * odd}
    far = {"tile": jnp.clip(me - 1 + 2 * odd, 0, tiles - 1)}
    across = {"sec": 1 - sec}
    p_near, q_near = X - (X - 1) * odd, (X + 1) * (1 - odd)
    p_far, q_far = 1 + (X - 1) * odd, (X + 1) * odd

    barrier = pltpu.get_barrier_semaphore()
    pl.semaphore_signal(barrier, inc=1, device_id=near, device_id_type=MESH)

    @pl.when(has_far)
    def _():
        pl.semaphore_signal(barrier, inc=1, device_id=far, device_id_type=MESH)

    pl.semaphore_signal(barrier, inc=1, device_id=across, device_id_type=MESH)

    loads = [
        pltpu.make_async_copy(lab_hbm, LAB.at[pl.ds(1, X)], local_sem.at[0]),
        pltpu.make_async_copy(dam_hbm, DAM.at[pl.ds(1, X)], local_sem.at[1]),
        pltpu.make_async_copy(u_hbm, U.at[pl.ds(0, 3), pl.ds(1, X), pl.ds(OFF, Y)], local_sem.at[2]),
        pltpu.make_async_copy(load_hbm, L, local_sem.at[3]),
    ]
    for copy in loads[:3]:
        copy.start()

    own_row = jnp.where(sec == 0, OFF + Y - 1, OFF)
    halo_row = jnp.where(sec == 0, OFF + Y, OFF - 1)
    edge_row = jnp.where(sec == 0, OFF - 1, OFF + Y)
    faces = [H.at[pl.ds(1, X)], K.at[pl.ds(1, X)]] + [U.at[c, pl.ds(1, X)] for c in range(3)]
    zero_row = jnp.zeros((1, Z), jnp.float32)
    for copy in loads[:2]:
        copy.wait()
    for p in range(X):
        h, k = moduli(LAB[1 + p, pl.ds(own_row - OFF, 1), :], DAM[1 + p, pl.ds(own_row - OFF, 1), :])
        S1[pl.ds(p, 1), :] = h
        S1[pl.ds(X + p, 1), :] = k

    def own_moduli(planes):
        @pl.loop(0, Y // 8)
        def _(i):
            y = pl.multiple_of(i * 8, 8)
            for p in planes:
                h, k = moduli(LAB[p, pl.ds(y, 8), :], DAM[p, pl.ds(y, 8), :])
                H[p, pl.ds(OFF + y, 8), :] = h
                K[p, pl.ds(OFF + y, 8), :] = k

    own_moduli((1, X))
    loads[2].wait()
    for f in range(2, 5):
        for p in range(X):
            S1[pl.ds(X * f + p, 1), :] = faces[f][p, pl.ds(own_row, 1), :]
    pl.semaphore_wait(barrier, 2 + has_far.astype(jnp.int32))

    def remote(src, dst, index, device):
        return pltpu.make_async_remote_copy(
            src_ref=src, dst_ref=dst, send_sem=send_sem.at[index], recv_sem=recv_sem.at[index],
            device_id=device, device_id_type=MESH)

    rows = pl.ds(OFF, Y)
    part = Y // PARTS
    base = 5 * PARTS

    def part_of(k):
        n = k + (1 - sec) * (PARTS - 1 - 2 * k)
        return pl.multiple_of(n * part, part)

    def far1(k):
        y = part_of(k)
        here, there = pl.ds(y, part), pl.ds(OFF + y, part)
        return [
            remote(U.at[:, p_far, there], U.at[:, X + 1 - q_far, there], 3 * k + 2, far),
        ]

    def f_far(k):
        there = pl.ds(OFF + part_of(k), part)
        return remote(F.at[:, p_far, there], F.at[:, X + 1 - q_far, there], 3 * PARTS + k, far)

    def c_far(k):
        return remote(PF.at[k], QF.at[k], 4 * PARTS + k, far)

    near1 = [
        remote(U.at[:, p_near, rows], U.at[:, X + 1 - q_near, rows], base + 2, near),
    ]
    cross1 = remote(S1, S1R, base + 3, across)
    cross1.start()

    @pl.when(has_far)
    def _():
        for k in range(PARTS):
            for copy in far1(k):
                copy.start()

    for copy in near1:
        copy.start()

    loads[3].start()

    own_moduli(range(2, X))
    for ref in faces:
        for p in range(X):
            ref[p, pl.ds(edge_row, 1), :] = zero_row
    for c in range(3):
        for p in range(1, X + 1):
            F[c, p, pl.ds(edge_row, 1), :] = zero_row

    @pl.when(jnp.logical_not(has_far))
    def _():
        for ref in (H, K):
            ref[q_far] = jnp.zeros(H.shape[1:], jnp.float32)
        for c in range(3):
            U[c, q_far] = jnp.zeros(U.shape[2:], jnp.float32)
            F[c, q_far] = jnp.zeros(F.shape[2:], jnp.float32)

    def weights(p, y):
        result = {}
        for name, M in (("s", H), ("t", K)):
            m = M[p, pl.ds(OFF + y, 8), :]
            if p > 1:
                result[name, "xl"] = m + M[p - 1, pl.ds(OFF + y, 8), :]
            if p < X:
                result[name, "xu"] = m + M[p + 1, pl.ds(OFF + y, 8), :]
            result[name, "yl"] = m + M[p, pl.ds(OFF + y - 1, 8), :]
            result[name, "yu"] = m + M[p, pl.ds(OFF + y + 1, 8), :]
            result[name, "zl"] = m + from_below(m, 1)
            result[name, "zu"] = m + from_above(m, 1)
        return result

    def neighbours(V, c, p, y, w):
        v = V[c, p, pl.ds(OFF + y, 8), :]
        kind = ["t" if c == a else "s" for a in range(3)]
        total = w[kind[1], "yl"] * V[c, p, pl.ds(OFF + y - 1, 8), :]
        total = total + w[kind[1], "yu"] * V[c, p, pl.ds(OFF + y + 1, 8), :]
        total = total + w[kind[2], "zl"] * from_below(v, 1)
        total = total + w[kind[2], "zu"] * from_above(v, 1)
        if p > 1:
            total = total + w[kind[0], "xl"] * V[c, p - 1, pl.ds(OFF + y, 8), :]
        if p < X:
            total = total + w[kind[0], "xu"] * V[c, p + 1, pl.ds(OFF + y, 8), :]
        return total, v

    def inner_residual(y):
        here = pl.ds(y, 8)
        for p in range(1, X + 1):
            w = weights(p, y)
            sides = {}
            for name in ("s", "t"):
                xs = [w[name, side] for side in ("xl", "xu") if (name, side) in w]
                sides[name, 0] = xs[0] if len(xs) == 1 else xs[0] + xs[1]
                sides[name, 1] = w[name, "yl"] + w[name, "yu"]
                sides[name, 2] = w[name, "zl"] + w[name, "zu"]
            for c in range(3):
                total, v = neighbours(U, c, p, y, w)
                others = [a for a in range(3) if a != c]
                diag = sides["t", c] + sides["s", others[0]] + sides["s", others[1]]
                acc = L[c, p - 1, here, :] + total
                if 1 < p < X:
                    r = acc - diag * v
                    inv = relaxation / diag
                    R[c, p - 2, here, :] = r
                    INV[c, p - 1, here, :] = inv
                    F[c, p, pl.ds(OFF + y, 8), :] = r * inv
                else:
                    L[c, p - 1, here, :] = acc
                    INV[c, p - 1, here, :] = diag

    halo_chunk = pl.multiple_of((1 - sec) * (Y - 8), 8)
    loads[3].wait()

    @pl.loop(0, Y // 8 - 1)
    def _(i):
        inner_residual(pl.multiple_of((i + sec) * 8, 8))

    cross1.wait()
    for f, ref in enumerate(faces):
        for p in range(X):
            ref[p, pl.ds(halo_row, 1), :] = S1R[pl.ds(X * f + p, 1), :]
    inner_residual(halo_chunk)

    def outer_face(p, q, y, present):
        here, there = pl.ds(y, 8), pl.ds(OFF + y, 8)
        h, k = H[q, there, :], K[q, there, :]
        s = h + H[p, there, :]
        t = k + K[p, there, :]
        j = (p - 1) // 2
        for c in range(3):
            w = t if c == 0 else s
            diag = INV[c, p - 1, here, :] + w
            r = L[c, p - 1, here, :] + w * U[c, q, there, :] - diag * U[c, p, there, :]
            inv = relaxation / diag
            INV[c, p - 1, here, :] = inv
            F[c, p, there, :] = r * inv
            R[c, j, here, :] = R[c, j, here, :] + r

    for copy in near1:
        copy.wait_recv()

    @pl.loop(0, Y // 8)
    def _(i):
        outer_face(p_near, q_near, pl.multiple_of(i * 8, 8), None)

    f_near = remote(F.at[:, p_near, rows], F.at[:, X + 1 - q_near, rows], base + 4, near)
    f_near.start()

    Y2, Y3 = Y // 2, Y // 4
    part2, part3 = part // 2, part // 4
    shape2, shape3 = (part2, Z), (part3, Z)
    odd2 = (lanes(shape2) & 1) == 1
    quad = lanes(shape3) & 3
    high3 = quad >= 2
    j_near, j_far = 1 - odd, odd

    def pairs(v):
        return v + jnp.where(odd2, roll(v, 1), roll(v, -1))

    def quads(v):
        return v + jnp.where(high3, roll(v, 2), roll(v, -2))

    def fine_rows(M, p, first):
        return M[p, pl.ds(first, part2, stride=2), :]

    def coarse_rows(m, slot, y2, first):
        return W2[m, slot, pl.ds(y2 + first, part3, stride=2), :]

    def kinds(c):
        return [1 if c == a else 0 for a in range(3)]

    def x_face(M, p, q, y):
        face = fine_rows(M, p, OFF + y) + fine_rows(M, p, OFF + y + 1)
        return pairs(face + fine_rows(M, q, OFF + y) + fine_rows(M, q, OFF + y + 1))

    def residual_two(c, j, y):
        return pairs(fine_rows(R.at[c], j, y) + fine_rows(R.at[c], j, y + 1))

    @pl.loop(0, PARTS)
    def _(n):
        y = pl.multiple_of(n * part, part)
        y2 = pl.multiple_of(n * part2, part2)
        y3 = pl.multiple_of(n * part3, part3)
        at2, at3 = pl.ds(y2, part2), pl.ds(y3, part3)
        sides = {}
        for m, M in enumerate((H, K)):
            mid = x_face(M, 2, 3, y)
            close = x_face(M, p_near, q_near, y)
            W2[m, 1, at2, :] = mid
            W2[m, 2 - 2 * odd, at2, :] = close
            W3[m, 1 - odd, at3, :] = quads(
                coarse_rows(m, 2 - 2 * odd, y2, 0) + coarse_rows(m, 2 - 2 * odd, y2, 1))
            for j in range(2):
                r7, r8, r9, r10 = [
                    fine_rows(M, 1 + 2 * j, OFF + y + d) + fine_rows(M, 2 + 2 * j, OFF + y + d) for d in (-1, 0, 1, 2)]
                yl, yu = pairs(r7 + r8), pairs(r9 + r10)
                cell = r8 + r9
                low = cell + from_below(cell, 1)
                high = cell + from_above(cell, 1)
                zl = jnp.where(odd2, roll(low, 1), low)
                zu = jnp.where(odd2, high, roll(high, -1))
                for slot, value in ((3, yl), (5, yu), (7, zl), (9, zu)):
                    W2[m, slot + j, at2, :] = value
                sides[m, j, 0] = mid
                sides[m, j, 1] = yl + yu
                sides[m, j, 2] = zl + zu
            W3[m, 2, at3, :] = quads(coarse_rows(m, 3, y2, 0) + coarse_rows(m, 4, y2, 0))
            W3[m, 3, at3, :] = quads(coarse_rows(m, 5, y2, 1) + coarse_rows(m, 6, y2, 1))
            low = coarse_rows(m, 7, y2, 0) + coarse_rows(m, 7, y2, 1)
            low = low + coarse_rows(m, 8, y2, 0) + coarse_rows(m, 8, y2, 1)
            high = coarse_rows(m, 9, y2, 0) + coarse_rows(m, 9, y2, 1)
            high = high + coarse_rows(m, 10, y2, 0) + coarse_rows(m, 10, y2, 1)
            W3[m, 4, at3, :] = jnp.where(high3, roll(low, 2), low)
            W3[m, 5, at3, :] = jnp.where(high3, high, roll(high, -2))
        for c in range(3):
            kx, ky, kz = kinds(c)
            for j in range(2):
                I2[c, j, at2, :] = sides[kx, j, 0] + sides[ky, j, 1] + sides[kz, j, 2]
            inv = relaxation / (I2[c, j_near, at2, :] + W2[kx, 2 - 2 * odd, at2, :])
            I2[c, j_near, at2, :] = inv
            res = residual_two(c, j_near, y)
            EX[c, j_near, at2, :] = res
            F2[c, 1 + j_near, pl.ds(OFF + y2, part2), :] = res * inv
            I3[c, at3, :] = (W3[kx, 1 - odd, at3, :] + W3[ky, 2, at3, :] + W3[ky, 3, at3, :]
                             + W3[kz, 4, at3, :] + W3[kz, 5, at3, :])

    half = part2 // 2
    odd_half = odd2[:half]

    deep_pieces = [
        (0, part3 // 2, [(0, 0), (0, part3 // 2), (1, 0), (1, part3 // 2)]),
        (part3 // 2, part3 // 4, [(2, n * (part3 // 4)) for n in range(4)]),
    ]

    def packed(V, c, p, y2):
        return jnp.where(odd_half, V[c, p, pl.ds(OFF + y2 + half, half), :], V[c, p, pl.ds(OFF + y2, half), :])

    own2 = jnp.where(sec == 0, OFF + Y2 - 1, OFF)
    own3 = jnp.where(sec == 0, OFF + Y3 - 1, OFF)
    halo2 = jnp.where(sec == 0, OFF + Y2, OFF - 1)
    halo3 = jnp.where(sec == 0, OFF + Y3, OFF - 1)
    edge2 = jnp.where(sec == 0, OFF - 1, OFF + Y2)
    edge3 = jnp.where(sec == 0, OFF - 1, OFF + Y3)
    quad_row = lanes((1, Z)) & 3
    odd_row = (quad_row & 1) == 1
    fine_faces = [(c, p) for c in range(3) for p in range(1, X + 1)]
    for c in range(3):
        F2[c, 1, pl.ds(edge2, 1), :] = zero_row
        F2[c, 2, pl.ds(edge2, 1), :] = zero_row
        F3[c, 1, pl.ds(edge3, 1), :] = zero_row

    def pack_rows():
        for r, (c, p) in enumerate(fine_faces):
            S2[pl.ds(r, 1), :] = F[c, p, pl.ds(own_row, 1), :]
        deep = zero_row
        for c in range(3):
            S2[pl.ds(12 + c, 1), :] = jnp.where(odd_row, F2[c, 2, pl.ds(own2, 1), :], F2[c, 1, pl.ds(own2, 1), :])
            deep = jnp.where(quad_row == c, F3[c, 1, pl.ds(own3, 1), :], deep)
        S2[pl.ds(15, 1), :] = deep

    def unpack_rows():
        for r, (c, p) in enumerate(fine_faces):
            F[c, p, pl.ds(halo_row, 1), :] = S2R[pl.ds(r, 1), :]
        deep = S2R[pl.ds(15, 1), :]
        for c in range(3):
            v = S2R[pl.ds(12 + c, 1), :]
            F2[c, 1, pl.ds(halo2, 1), :] = jnp.where(odd_row, roll(v, 1), v)
            F2[c, 2, pl.ds(halo2, 1), :] = jnp.where(odd_row, v, roll(v, -1))
            F3[c, 1, pl.ds(halo3, 1), :] = spread_quad(deep, c, quad_row)

    def spread_quad(v, c, quad):
        spread = v
        for lane in range(4):
            if lane != c:
                spread = jnp.where(quad == lane, roll(v, lane - c), spread)
        return spread

    cross2 = remote(S2, S2R, base + 5, across)

    @pl.loop(0, PARTS)
    def _(k):
        y = part_of(k)

        @pl.when(has_far)
        def _():
            for copy in far1(k):
                copy.wait_recv()

        for i in range(part // 8):
            outer_face(p_far, q_far, pl.multiple_of(y + i * 8, 8), has_far)

        y2, y3 = pl.multiple_of(y // 2, part2), pl.multiple_of(y // 4, part3)
        at2, at3 = pl.ds(y2, part2), pl.ds(y3, part3)
        for m, M in enumerate((H, K)):
            W2[m, 2 * odd, at2, :] = x_face(M, p_far, q_far, y)
            W3[m, odd, at3, :] = quads(coarse_rows(m, 2 * odd, y2, 0) + coarse_rows(m, 2 * odd, y2, 1))
        for c in range(3):
            kx = kinds(c)[0]
            inv = relaxation / (I2[c, j_far, at2, :] + W2[kx, 2 * odd, at2, :])
            I2[c, j_far, at2, :] = inv
            res = residual_two(c, j_far, y)
            EX[c, j_far, at2, :] = res
            F2[c, 1 + j_far, pl.ds(OFF + y2, part2), :] = res * inv
            inv = relaxation / (I3[c, at3, :] + W3[kx, odd, at3, :])
            I3[c, at3, :] = inv
            res = EX[c, 0, pl.ds(y2, part3, stride=2), :] + EX[c, 0, pl.ds(y2 + 1, part3, stride=2), :]
            res = res + EX[c, 1, pl.ds(y2, part3, stride=2), :] + EX[c, 1, pl.ds(y2 + 1, part3, stride=2), :]
            first = quads(res) * inv
            F3[c, 1, pl.ds(OFF + y3, part3), :] = first
            PF[k, pl.ds(half * c, half), :] = packed(F2, c, 1 + j_far, y2)
            PN[k, pl.ds(half * c, half), :] = packed(F2, c, 1 + j_near, y2)
        for first_row, count, pieces in deep_pieces:
            quad_now = quad[:count]
            deep = F3[pieces[0][0], 1, pl.ds(OFF + y3 + pieces[0][1], count), :]
            for slot in range(1, 4):
                c, row = pieces[slot]
                deep = jnp.where(quad_now == slot, F3[c, 1, pl.ds(OFF + y3 + row, count), :], deep)
            PF[k, pl.ds(3 * half + first_row, count), :] = deep
            PN[k, pl.ds(3 * half + first_row, count), :] = deep

        @pl.when(has_far)
        def _():
            c_far(k).start()
            f_far(k).start()

        @pl.when(k == 0)
        def _():
            pack_rows()
            cross2.start()

    c_near = remote(PN, QN, base + 6, near)
    c_near.start()

    def inner_sweep(y):
        here = pl.ds(y, 8)
        for p in range(1, X + 1):
            w = weights(p, y)
            for c in range(3):
                total, v = neighbours(F, c, p, y, w)
                E[c, p - 1, here, :] = (4.0 / 3.0) * v + INV[c, p - 1, here, :] * total

    def outer_sweep(target, p, q, y):
        here, there = pl.ds(y, 8), pl.ds(OFF + y, 8)
        s = H[q, there, :] + H[p, there, :]
        t = K[q, there, :] + K[p, there, :]
        for c in range(3):
            w = t if c == 0 else s
            target[c, p - 1, here, :] = target[c, p - 1, here, :] + INV[c, p - 1, here, :] * (w * F[c, q, there, :])

    f_near.wait_recv()

    @pl.loop(0, Y // 8 - 1)
    def _(i):
        y = pl.multiple_of((i + sec) * 8, 8)
        inner_sweep(y)
        outer_sweep(E, p_near, q_near, y)

    cross2.wait()
    unpack_rows()
    inner_sweep(halo_chunk)
    outer_sweep(E, p_near, q_near, halo_chunk)

    def unpack(Q, k, q2, q3, present):
        y = part_of(k)
        y2, y3 = y // 2, y // 4
        for c in range(3):
            v = Q[k, pl.ds(half * c, half), :]
            if present is not None:
                v = jnp.where(present, v, 0.0)
            F2[c, q2, pl.ds(OFF + y2, half), :] = jnp.where(odd_half, roll(v, 1), v)
            F2[c, q2, pl.ds(OFF + y2 + half, half), :] = jnp.where(odd_half, v, roll(v, -1))
        for first_row, count, pieces in deep_pieces:
            v = Q[k, pl.ds(3 * half + first_row, count), :]
            if present is not None:
                v = jnp.where(present, v, 0.0)
            for slot, (c, row) in enumerate(pieces):
                F3[c, q3, pl.ds(OFF + y3 + row, count), :] = spread_quad(v, slot, quad[:count])

    c_near.wait_recv()
    for k in range(PARTS):
        unpack(QN, k, 3 * (1 - odd), 2 * (1 - odd), None)

    @pl.loop(0, PARTS)
    def _(k):
        y = part_of(k)
        y2, y3 = pl.multiple_of(y // 2, part2), pl.multiple_of(y // 4, part3)
        at2, at3 = pl.ds(y2, part2), pl.ds(y3, part3)

        @pl.when(has_far)
        def _():
            c_far(k).wait_recv()

        unpack(QF, k, 3 * odd, 2 * odd, has_far)
        for c in range(3):
            kx, ky, kz = kinds(c)

            def f3(p, d):
                return F3[c, p, pl.ds(OFF + y3 + d, part3), :]

            v = f3(1, 0)
            total = W3[kx, 0, at3, :] * f3(0, 0) + W3[kx, 1, at3, :] * f3(2, 0)
            total = total + W3[ky, 2, at3, :] * f3(1, -1) + W3[ky, 3, at3, :] * f3(1, 1)
            total = total + W3[kz, 4, at3, :] * from_below(v, 4) + W3[kz, 5, at3, :] * from_above(v, 4)
            e3 = (4.0 / 3.0) * v + I3[c, at3, :] * total
            EX[c, 0, pl.ds(y2, part3, stride=2), :] = e3
            EX[c, 0, pl.ds(y2 + 1, part3, stride=2), :] = e3
            e3 = EX[c, 0, at2, :]

            def f2(p, d):
                return F2[c, p, pl.ds(OFF + y2 + d, part2), :]

            for j in range(2):
                p = 1 + j
                v = f2(p, 0)
                total = W2[kx, j, at2, :] * f2(p - 1, 0) + W2[kx, j + 1, at2, :] * f2(p + 1, 0)
                total = total + W2[ky, 3 + j, at2, :] * f2(p, -1) + W2[ky, 5 + j, at2, :] * f2(p, 1)
                total = total + W2[kz, 7 + j, at2, :] * from_below(v, 2) + W2[kz, 9 + j, at2, :] * from_above(v, 2)
                e2 = (4.0 / 3.0) * v + I2[c, j, at2, :] * total + e3
                R[c, j, pl.ds(y, part2, stride=2), :] = e2
                R[c, j, pl.ds(y + 1, part2, stride=2), :] = e2
        for i in range(part // 8):
            here = pl.ds(pl.multiple_of(y + i * 8, 8), 8)
            for p in range(X):
                for c in range(3):
                    out[c, p, here, :] = E[c, p, here, :] + R[c, p // 2, here, :]

        @pl.when(has_far)
        def _():
            f_far(k).wait_recv()

        for i in range(part // 8):
            outer_sweep(out, p_far, q_far, pl.multiple_of(y + i * 8, 8))

    for copy in near1 + [f_near, c_near]:
        copy.wait_send()

    @pl.when(has_far)
    def _():
        for k in range(PARTS):
            for copy in far1(k) + [f_far(k), c_far(k)]:
                copy.wait_send()


def per_device(tiles, load_field, iterate, phase_label, damage):
    f32, i32 = jnp.float32, jnp.int32
    padded = Y + 2 * OFF
    return pl.pallas_call(
        functools.partial(kernel, tiles),
        out_shape=jax.ShapeDtypeStruct(load_field.shape, f32),
        in_specs=[pl.BlockSpec(memory_space=pltpu.HBM)] * 4,
        out_specs=pl.BlockSpec(memory_space=pltpu.VMEM),
        scratch_shapes=[
            pltpu.VMEM((5, X + 2, padded, Z), f32),
            pltpu.VMEM((3, X + 2, padded, Z), f32),
            pltpu.VMEM((3, X, Y, Z), f32),
            pltpu.VMEM((3, X, Y, Z), f32),
            pltpu.VMEM((3, X // 2, Y, Z), f32),
            pltpu.VMEM((3, X, Y, Z), f32),
            pltpu.VMEM((2, X + 2, Y, Z), i32),
            pltpu.VMEM((20, Z), f32),
            pltpu.VMEM((20, Z), f32),
            pltpu.VMEM((16, Z), f32),
            pltpu.VMEM((16, Z), f32),
            pltpu.VMEM((PARTS, Y * 15 // (16 * PARTS), Z), f32),
            pltpu.VMEM((PARTS, Y * 15 // (16 * PARTS), Z), f32),
            pltpu.VMEM((PARTS, Y * 15 // (16 * PARTS), Z), f32),
            pltpu.VMEM((PARTS, Y * 15 // (16 * PARTS), Z), f32),
            pltpu.VMEM((2, 11, Y // 2, Z), f32),
            pltpu.VMEM((3, 4, Y // 2 + 2 * OFF, Z), f32),
            pltpu.VMEM((3, 2, Y // 2, Z), f32),
            pltpu.VMEM((2, 6, Y // 4, Z), f32),
            pltpu.VMEM((3, 3, Y // 4 + 2 * OFF, Z), f32),
            pltpu.VMEM((3, Y // 4, Z), f32),
            pltpu.VMEM((3, 2, Y // 2, Z), f32),
            pltpu.SemaphoreType.DMA((4,)),
            pltpu.SemaphoreType.DMA((5 * PARTS + 7,)),
            pltpu.SemaphoreType.DMA((5 * PARTS + 7,)),
        ],
        compiler_params=pltpu.CompilerParams(
            collective_id=0, has_side_effects=True, vmem_limit_bytes=48 * 1024 * 1024),
    )(*[pltpu.with_memory_space_constraint(a, pltpu.HBM) for a in (load_field, iterate, phase_label, damage)])


def solution(mesh):
    tiles = mesh.shape["tile"]
    in_specs = (
        P(None, "tile", "sec", None),
        P(None, "tile", "sec", None),
        P("tile", "sec", None),
        P("tile", "sec", None),
    )
    out_specs = P(None, "tile", "sec", None)
    return jax.shard_map(
        functools.partial(per_device, tiles), mesh=mesh, in_specs=in_specs, out_specs=out_specs, check_vma=False
    )
```

```python
import functools

import jax
import jax.numpy as jnp
from jax import lax
from jax.experimental import pallas as pl
from jax.experimental.pallas import tpu as pltpu
from jax.sharding import PartitionSpec as P

shear_table = (1.0, 0.6, 1.8, 0.35)
bulk_table = (1.2, 0.9, 2.5, 0.5)
damage_step = 0.25
damage_floor = 0.01
relaxation = 2.0 / 3.0

MESH = pl.DeviceIdType.MESH
X = 4
Y = 128
Z = 128
PARTS = 2
OFF = 8


def lanes(shape):
    return lax.broadcasted_iota(jnp.int32, shape, len(shape) - 1)


def roll(v, shift):
    return pltpu.roll(v, shift % Z, v.ndim - 1)


def from_above(v, step):
    return jnp.where(lanes(v.shape) < Z - step, roll(v, -step), 0.0)


def from_below(v, step):
    return jnp.where(lanes(v.shape) >= step, roll(v, step), 0.0)


def moduli(phase, damage):
    soft = 1.0 - damage_step * damage.astype(jnp.float32)
    degrade = soft * soft + damage_floor

    def table(values):
        picked = jnp.full(phase.shape, values[3], jnp.float32)
        for label in (2, 1, 0):
            picked = jnp.where(phase == label, values[label], picked)
        return picked

    half = table([0.5 * s for s in shear_table])
    normal = table([0.5 * b + s for s, b in zip(shear_table, bulk_table)])
    return half * degrade, normal * degrade


def kernel(tiles, load_hbm, u_hbm, lab_hbm, dam_hbm, out, U, F, L, INV, R, E, CODE, S1, S1R, S2, S2R,
           PN, QN, PF, QF, W2, F2, I2, W3, F3, I3, EX, local_sem, send_sem, recv_sem):
    LAB, DAM = CODE.at[0], CODE.at[1]
    H, K = U.at[3], U.at[4]
    me = lax.axis_index("tile")
    sec = lax.axis_index("sec")
    odd = lax.rem(me, 2)
    has_far = jnp.logical_and(me > 0, me < tiles - 1)
    near = {"tile": me + 1 - 2 * odd}
    far = {"tile": jnp.clip(me - 1 + 2 * odd, 0, tiles - 1)}
    across = {"sec": 1 - sec}
    p_near, q_near = X - (X - 1) * odd, (X + 1) * (1 - odd)
    p_far, q_far = 1 + (X - 1) * odd, (X + 1) * odd

    barrier = pltpu.get_barrier_semaphore()
    pl.semaphore_signal(barrier, inc=1, device_id=near, device_id_type=MESH)

    @pl.when(has_far)
    def _():
        pl.semaphore_signal(barrier, inc=1, device_id=far, device_id_type=MESH)

    pl.semaphore_signal(barrier, inc=1, device_id=across, device_id_type=MESH)

    loads = [
        pltpu.make_async_copy(lab_hbm, LAB.at[pl.ds(1, X)], local_sem.at[0]),
        pltpu.make_async_copy(dam_hbm, DAM.at[pl.ds(1, X)], local_sem.at[1]),
        pltpu.make_async_copy(u_hbm, U.at[pl.ds(0, 3), pl.ds(1, X), pl.ds(OFF, Y)], local_sem.at[2]),
        pltpu.make_async_copy(load_hbm, L, local_sem.at[3]),
    ]
    for copy in loads[:3]:
        copy.start()

    own_row = jnp.where(sec == 0, OFF + Y - 1, OFF)
    halo_row = jnp.where(sec == 0, OFF + Y, OFF - 1)
    edge_row = jnp.where(sec == 0, OFF - 1, OFF + Y)
    faces = [H.at[pl.ds(1, X)], K.at[pl.ds(1, X)]] + [U.at[c, pl.ds(1, X)] for c in range(3)]
    zero_row = jnp.zeros((1, Z), jnp.float32)
    for copy in loads[:2]:
        copy.wait()
    for p in range(X):
        h, k = moduli(LAB[1 + p, pl.ds(own_row - OFF, 1), :], DAM[1 + p, pl.ds(own_row - OFF, 1), :])
        S1[pl.ds(p, 1), :] = h
        S1[pl.ds(X + p, 1), :] = k

    def own_moduli(planes):
        @pl.loop(0, Y // 8)
        def _(i):
            y = pl.multiple_of(i * 8, 8)
            for p in planes:
                h, k = moduli(LAB[p, pl.ds(y, 8), :], DAM[p, pl.ds(y, 8), :])
                H[p, pl.ds(OFF + y, 8), :] = h
                K[p, pl.ds(OFF + y, 8), :] = k

    own_moduli((1, X))
    loads[2].wait()
    for f in range(2, 5):
        for p in range(X):
            S1[pl.ds(X * f + p, 1), :] = faces[f][p, pl.ds(own_row, 1), :]
    pl.semaphore_wait(barrier, 2 + has_far.astype(jnp.int32))

    def remote(src, dst, index, device):
        return pltpu.make_async_remote_copy(
            src_ref=src, dst_ref=dst, send_sem=send_sem.at[index], recv_sem=recv_sem.at[index],
            device_id=device, device_id_type=MESH)

    rows = pl.ds(OFF, Y)
    part = Y // PARTS
    base = 5 * PARTS

    def part_of(k):
        n = k + (1 - sec) * (PARTS - 1 - 2 * k)
        return pl.multiple_of(n * part, part)

    def far1(k):
        y = part_of(k)
        here, there = pl.ds(y, part), pl.ds(OFF + y, part)
        return [
            remote(U.at[:, p_far, there], U.at[:, X + 1 - q_far, there], 3 * k + 2, far),
        ]

    def f_far(k):
        there = pl.ds(OFF + part_of(k), part)
        return remote(F.at[:, p_far, there], F.at[:, X + 1 - q_far, there], 3 * PARTS + k, far)

    def c_far(k):
        return remote(PF.at[k], QF.at[k], 4 * PARTS + k, far)

    near1 = [
        remote(U.at[:, p_near, rows], U.at[:, X + 1 - q_near, rows], base + 2, near),
    ]
    cross1 = remote(S1, S1R, base + 3, across)
    cross1.start()

    @pl.when(has_far)
    def _():
        for k in range(PARTS):
            for copy in far1(k):
                copy.start()

    for copy in near1:
        copy.start()

    loads[3].start()

    own_moduli(range(2, X))
    for ref in faces:
        for p in range(X):
            ref[p, pl.ds(edge_row, 1), :] = zero_row
    for c in range(3):
        for p in range(1, X + 1):
            F[c, p, pl.ds(edge_row, 1), :] = zero_row

    @pl.when(jnp.logical_not(has_far))
    def _():
        for ref in (H, K):
            ref[q_far] = jnp.zeros(H.shape[1:], jnp.float32)
        for c in range(3):
            U[c, q_far] = jnp.zeros(U.shape[2:], jnp.float32)
            F[c, q_far] = jnp.zeros(F.shape[2:], jnp.float32)

    def weights(p, y):
        result = {}
        for name, M in (("s", H), ("t", K)):
            m = M[p, pl.ds(OFF + y, 8), :]
            if p > 1:
                result[name, "xl"] = m + M[p - 1, pl.ds(OFF + y, 8), :]
            if p < X:
                result[name, "xu"] = m + M[p + 1, pl.ds(OFF + y, 8), :]
            result[name, "yl"] = m + M[p, pl.ds(OFF + y - 1, 8), :]
            result[name, "yu"] = m + M[p, pl.ds(OFF + y + 1, 8), :]
            result[name, "zl"] = m + from_below(m, 1)
            result[name, "zu"] = m + from_above(m, 1)
        return result

    def neighbours(V, c, p, y, w):
        v = V[c, p, pl.ds(OFF + y, 8), :]
        kind = ["t" if c == a else "s" for a in range(3)]
        total = w[kind[1], "yl"] * V[c, p, pl.ds(OFF + y - 1, 8), :]
        total = total + w[kind[1], "yu"] * V[c, p, pl.ds(OFF + y + 1, 8), :]
        total = total + w[kind[2], "zl"] * from_below(v, 1)
        total = total + w[kind[2], "zu"] * from_above(v, 1)
        if p > 1:
            total = total + w[kind[0], "xl"] * V[c, p - 1, pl.ds(OFF + y, 8), :]
        if p < X:
            total = total + w[kind[0], "xu"] * V[c, p + 1, pl.ds(OFF + y, 8), :]
        return total, v

    def inner_residual(y):
        here = pl.ds(y, 8)
        for p in range(1, X + 1):
            w = weights(p, y)
            sides = {}
            for name in ("s", "t"):
                xs = [w[name, side] for side in ("xl", "xu") if (name, side) in w]
                sides[name, 0] = xs[0] if len(xs) == 1 else xs[0] + xs[1]
                sides[name, 1] = w[name, "yl"] + w[name, "yu"]
                sides[name, 2] = w[name, "zl"] + w[name, "zu"]
            for c in range(3):
                total, v = neighbours(U, c, p, y, w)
                others = [a for a in range(3) if a != c]
                diag = sides["t", c] + sides["s", others[0]] + sides["s", others[1]]
                acc = L[c, p - 1, here, :] + total
                if 1 < p < X:
                    r = acc - diag * v
                    inv = relaxation / diag
                    R[c, p - 2, here, :] = r
                    INV[c, p - 1, here, :] = inv
                    F[c, p, pl.ds(OFF + y, 8), :] = r * inv
                else:
                    L[c, p - 1, here, :] = acc
                    INV[c, p - 1, here, :] = diag

    halo_chunk = pl.multiple_of((1 - sec) * (Y - 8), 8)
    loads[3].wait()

    @pl.loop(0, Y // 8 - 1)
    def _(i):
        inner_residual(pl.multiple_of((i + sec) * 8, 8))

    cross1.wait()
    for f, ref in enumerate(faces):
        for p in range(X):
            ref[p, pl.ds(halo_row, 1), :] = S1R[pl.ds(X * f + p, 1), :]
    inner_residual(halo_chunk)

    def outer_face(p, q, y, present):
        here, there = pl.ds(y, 8), pl.ds(OFF + y, 8)
        h, k = H[q, there, :], K[q, there, :]
        s = h + H[p, there, :]
        t = k + K[p, there, :]
        j = (p - 1) // 2
        for c in range(3):
            w = t if c == 0 else s
            diag = INV[c, p - 1, here, :] + w
            r = L[c, p - 1, here, :] + w * U[c, q, there, :] - diag * U[c, p, there, :]
            inv = relaxation / diag
            INV[c, p - 1, here, :] = inv
            F[c, p, there, :] = r * inv
            R[c, j, here, :] = R[c, j, here, :] + r

    for copy in near1:
        copy.wait_recv()

    @pl.loop(0, Y // 8)
    def _(i):
        outer_face(p_near, q_near, pl.multiple_of(i * 8, 8), None)

    f_near = remote(F.at[:, p_near, rows], F.at[:, X + 1 - q_near, rows], base + 4, near)
    f_near.start()

    Y2, Y3 = Y // 2, Y // 4
    part2, part3 = part // 2, part // 4
    shape2, shape3 = (part2, Z), (part3, Z)
    odd2 = (lanes(shape2) & 1) == 1
    quad = lanes(shape3) & 3
    high3 = quad >= 2
    j_near, j_far = 1 - odd, odd

    def pairs(v):
        return v + jnp.where(odd2, roll(v, 1), roll(v, -1))

    def quads(v):
        return v + jnp.where(high3, roll(v, 2), roll(v, -2))

    def fine_rows(M, p, first):
        return M[p, pl.ds(first, part2, stride=2), :]

    def coarse_rows(m, slot, y2, first):
        return W2[m, slot, pl.ds(y2 + first, part3, stride=2), :]

    def kinds(c):
        return [1 if c == a else 0 for a in range(3)]

    def x_face(M, p, q, y):
        face = fine_rows(M, p, OFF + y) + fine_rows(M, p, OFF + y + 1)
        return pairs(face + fine_rows(M, q, OFF + y) + fine_rows(M, q, OFF + y + 1))

    def residual_two(c, j, y):
        return pairs(fine_rows(R.at[c], j, y) + fine_rows(R.at[c], j, y + 1))

    @pl.loop(0, PARTS)
    def _(n):
        y = pl.multiple_of(n * part, part)
        y2 = pl.multiple_of(n * part2, part2)
        y3 = pl.multiple_of(n * part3, part3)
        at2, at3 = pl.ds(y2, part2), pl.ds(y3, part3)
        sides = {}
        for m, M in enumerate((H, K)):
            mid = x_face(M, 2, 3, y)
            close = x_face(M, p_near, q_near, y)
            W2[m, 1, at2, :] = mid
            W2[m, 2 - 2 * odd, at2, :] = close
            W3[m, 1 - odd, at3, :] = quads(
                coarse_rows(m, 2 - 2 * odd, y2, 0) + coarse_rows(m, 2 - 2 * odd, y2, 1))
            for j in range(2):
                r7, r8, r9, r10 = [
                    fine_rows(M, 1 + 2 * j, OFF + y + d) + fine_rows(M, 2 + 2 * j, OFF + y + d) for d in (-1, 0, 1, 2)]
                yl, yu = pairs(r7 + r8), pairs(r9 + r10)
                cell = r8 + r9
                low = cell + from_below(cell, 1)
                high = cell + from_above(cell, 1)
                zl = jnp.where(odd2, roll(low, 1), low)
                zu = jnp.where(odd2, high, roll(high, -1))
                for slot, value in ((3, yl), (5, yu), (7, zl), (9, zu)):
                    W2[m, slot + j, at2, :] = value
                sides[m, j, 0] = mid
                sides[m, j, 1] = yl + yu
                sides[m, j, 2] = zl + zu
            W3[m, 2, at3, :] = quads(coarse_rows(m, 3, y2, 0) + coarse_rows(m, 4, y2, 0))
            W3[m, 3, at3, :] = quads(coarse_rows(m, 5, y2, 1) + coarse_rows(m, 6, y2, 1))
            low = coarse_rows(m, 7, y2, 0) + coarse_rows(m, 7, y2, 1)
            low = low + coarse_rows(m, 8, y2, 0) + coarse_rows(m, 8, y2, 1)
            high = coarse_rows(m, 9, y2, 0) + coarse_rows(m, 9, y2, 1)
            high = high + coarse_rows(m, 10, y2, 0) + coarse_rows(m, 10, y2, 1)
            W3[m, 4, at3, :] = jnp.where(high3, roll(low, 2), low)
            W3[m, 5, at3, :] = jnp.where(high3, high, roll(high, -2))
        for c in range(3):
            kx, ky, kz = kinds(c)
            for j in range(2):
                I2[c, j, at2, :] = sides[kx, j, 0] + sides[ky, j, 1] + sides[kz, j, 2]
            inv = relaxation / (I2[c, j_near, at2, :] + W2[kx, 2 - 2 * odd, at2, :])
            I2[c, j_near, at2, :] = inv
            res = residual_two(c, j_near, y)
            EX[c, j_near, at2, :] = res
            F2[c, 1 + j_near, pl.ds(OFF + y2, part2), :] = res * inv
            I3[c, at3, :] = (W3[kx, 1 - odd, at3, :] + W3[ky, 2, at3, :] + W3[ky, 3, at3, :]
                             + W3[kz, 4, at3, :] + W3[kz, 5, at3, :])

    half = part2 // 2
    odd_half = odd2[:half]

    deep_pieces = [
        (0, part3 // 2, [(0, 0), (0, part3 // 2), (1, 0), (1, part3 // 2)]),
        (part3 // 2, part3 // 4, [(2, n * (part3 // 4)) for n in range(4)]),
    ]

    def packed(V, c, p, y2):
        return jnp.where(odd_half, V[c, p, pl.ds(OFF + y2 + half, half), :], V[c, p, pl.ds(OFF + y2, half), :])

    own2 = jnp.where(sec == 0, OFF + Y2 - 1, OFF)
    own3 = jnp.where(sec == 0, OFF + Y3 - 1, OFF)
    halo2 = jnp.where(sec == 0, OFF + Y2, OFF - 1)
    halo3 = jnp.where(sec == 0, OFF + Y3, OFF - 1)
    edge2 = jnp.where(sec == 0, OFF - 1, OFF + Y2)
    edge3 = jnp.where(sec == 0, OFF - 1, OFF + Y3)
    quad_row = lanes((1, Z)) & 3
    odd_row = (quad_row & 1) == 1
    fine_faces = [(c, p) for c in range(3) for p in range(1, X + 1)]
    for c in range(3):
        F2[c, 1, pl.ds(edge2, 1), :] = zero_row
        F2[c, 2, pl.ds(edge2, 1), :] = zero_row
        F3[c, 1, pl.ds(edge3, 1), :] = zero_row

    def pack_rows():
        for r, (c, p) in enumerate(fine_faces):
            S2[pl.ds(r, 1), :] = F[c, p, pl.ds(own_row, 1), :]
        deep = zero_row
        for c in range(3):
            S2[pl.ds(12 + c, 1), :] = jnp.where(odd_row, F2[c, 2, pl.ds(own2, 1), :], F2[c, 1, pl.ds(own2, 1), :])
            deep = jnp.where(quad_row == c, F3[c, 1, pl.ds(own3, 1), :], deep)
        S2[pl.ds(15, 1), :] = deep

    def unpack_rows():
        for r, (c, p) in enumerate(fine_faces):
            F[c, p, pl.ds(halo_row, 1), :] = S2R[pl.ds(r, 1), :]
        deep = S2R[pl.ds(15, 1), :]
        for c in range(3):
            v = S2R[pl.ds(12 + c, 1), :]
            F2[c, 1, pl.ds(halo2, 1), :] = jnp.where(odd_row, roll(v, 1), v)
            F2[c, 2, pl.ds(halo2, 1), :] = jnp.where(odd_row, v, roll(v, -1))
            F3[c, 1, pl.ds(halo3, 1), :] = spread_quad(deep, c, quad_row)

    def spread_quad(v, c, quad):
        spread = v
        for lane in range(4):
            if lane != c:
                spread = jnp.where(quad == lane, roll(v, lane - c), spread)
        return spread

    cross2 = remote(S2, S2R, base + 5, across)

    @pl.loop(0, PARTS)
    def _(k):
        y = part_of(k)

        @pl.when(has_far)
        def _():
            for copy in far1(k):
                copy.wait_recv()

        for i in range(part // 8):
            outer_face(p_far, q_far, pl.multiple_of(y + i * 8, 8), has_far)

        y2, y3 = pl.multiple_of(y // 2, part2), pl.multiple_of(y // 4, part3)
        at2, at3 = pl.ds(y2, part2), pl.ds(y3, part3)
        for m, M in enumerate((H, K)):
            W2[m, 2 * odd, at2, :] = x_face(M, p_far, q_far, y)
            W3[m, odd, at3, :] = quads(coarse_rows(m, 2 * odd, y2, 0) + coarse_rows(m, 2 * odd, y2, 1))
        for c in range(3):
            kx = kinds(c)[0]
            inv = relaxation / (I2[c, j_far, at2, :] + W2[kx, 2 * odd, at2, :])
            I2[c, j_far, at2, :] = inv
            res = residual_two(c, j_far, y)
            EX[c, j_far, at2, :] = res
            F2[c, 1 + j_far, pl.ds(OFF + y2, part2), :] = res * inv
            inv = relaxation / (I3[c, at3, :] + W3[kx, odd, at3, :])
            I3[c, at3, :] = inv
            res = EX[c, 0, pl.ds(y2, part3, stride=2), :] + EX[c, 0, pl.ds(y2 + 1, part3, stride=2), :]
            res = res + EX[c, 1, pl.ds(y2, part3, stride=2), :] + EX[c, 1, pl.ds(y2 + 1, part3, stride=2), :]
            first = quads(res) * inv
            F3[c, 1, pl.ds(OFF + y3, part3), :] = first
            PF[k, pl.ds(half * c, half), :] = packed(F2, c, 1 + j_far, y2)
            PN[k, pl.ds(half * c, half), :] = packed(F2, c, 1 + j_near, y2)
        for first_row, count, pieces in deep_pieces:
            quad_now = quad[:count]
            deep = F3[pieces[0][0], 1, pl.ds(OFF + y3 + pieces[0][1], count), :]
            for slot in range(1, 4):
                c, row = pieces[slot]
                deep = jnp.where(quad_now == slot, F3[c, 1, pl.ds(OFF + y3 + row, count), :], deep)
            PF[k, pl.ds(3 * half + first_row, count), :] = deep
            PN[k, pl.ds(3 * half + first_row, count), :] = deep

        @pl.when(k == 0)
        def _():
            pack_rows()
            cross2.start()

        @pl.when(has_far)
        def _():
            c_far(k).start()
            f_far(k).start()

    c_near = remote(PN, QN, base + 6, near)
    c_near.start()

    def inner_sweep(y):
        here = pl.ds(y, 8)
        for p in range(1, X + 1):
            w = weights(p, y)
            for c in range(3):
                total, v = neighbours(F, c, p, y, w)
                E[c, p - 1, here, :] = (4.0 / 3.0) * v + INV[c, p - 1, here, :] * total

    def outer_sweep(target, p, q, y):
        here, there = pl.ds(y, 8), pl.ds(OFF + y, 8)
        s = H[q, there, :] + H[p, there, :]
        t = K[q, there, :] + K[p, there, :]
        for c in range(3):
            w = t if c == 0 else s
            target[c, p - 1, here, :] = target[c, p - 1, here, :] + INV[c, p - 1, here, :] * (w * F[c, q, there, :])

    f_near.wait_recv()

    @pl.loop(0, Y // 8 - 1)
    def _(i):
        y = pl.multiple_of((i + sec) * 8, 8)
        inner_sweep(y)
        outer_sweep(E, p_near, q_near, y)

    cross2.wait()
    unpack_rows()
    inner_sweep(halo_chunk)
    outer_sweep(E, p_near, q_near, halo_chunk)

    def unpack(Q, k, q2, q3, present):
        y = part_of(k)
        y2, y3 = y // 2, y // 4
        for c in range(3):
            v = Q[k, pl.ds(half * c, half), :]
            if present is not None:
                v = jnp.where(present, v, 0.0)
            F2[c, q2, pl.ds(OFF + y2, half), :] = jnp.where(odd_half, roll(v, 1), v)
            F2[c, q2, pl.ds(OFF + y2 + half, half), :] = jnp.where(odd_half, v, roll(v, -1))
        for first_row, count, pieces in deep_pieces:
            v = Q[k, pl.ds(3 * half + first_row, count), :]
            if present is not None:
                v = jnp.where(present, v, 0.0)
            for slot, (c, row) in enumerate(pieces):
                F3[c, q3, pl.ds(OFF + y3 + row, count), :] = spread_quad(v, slot, quad[:count])

    c_near.wait_recv()
    for k in range(PARTS):
        unpack(QN, k, 3 * (1 - odd), 2 * (1 - odd), None)

    @pl.loop(0, PARTS)
    def _(k):
        y = part_of(k)
        y2, y3 = pl.multiple_of(y // 2, part2), pl.multiple_of(y // 4, part3)
        at2, at3 = pl.ds(y2, part2), pl.ds(y3, part3)

        @pl.when(has_far)
        def _():
            c_far(k).wait_recv()

        unpack(QF, k, 3 * odd, 2 * odd, has_far)
        for c in range(3):
            kx, ky, kz = kinds(c)

            def f3(p, d):
                return F3[c, p, pl.ds(OFF + y3 + d, part3), :]

            v = f3(1, 0)
            total = W3[kx, 0, at3, :] * f3(0, 0) + W3[kx, 1, at3, :] * f3(2, 0)
            total = total + W3[ky, 2, at3, :] * f3(1, -1) + W3[ky, 3, at3, :] * f3(1, 1)
            total = total + W3[kz, 4, at3, :] * from_below(v, 4) + W3[kz, 5, at3, :] * from_above(v, 4)
            e3 = (4.0 / 3.0) * v + I3[c, at3, :] * total
            EX[c, 0, pl.ds(y2, part3, stride=2), :] = e3
            EX[c, 0, pl.ds(y2 + 1, part3, stride=2), :] = e3
            e3 = EX[c, 0, at2, :]

            def f2(p, d):
                return F2[c, p, pl.ds(OFF + y2 + d, part2), :]

            for j in range(2):
                p = 1 + j
                v = f2(p, 0)
                total = W2[kx, j, at2, :] * f2(p - 1, 0) + W2[kx, j + 1, at2, :] * f2(p + 1, 0)
                total = total + W2[ky, 3 + j, at2, :] * f2(p, -1) + W2[ky, 5 + j, at2, :] * f2(p, 1)
                total = total + W2[kz, 7 + j, at2, :] * from_below(v, 2) + W2[kz, 9 + j, at2, :] * from_above(v, 2)
                e2 = (4.0 / 3.0) * v + I2[c, j, at2, :] * total + e3
                R[c, j, pl.ds(y, part2, stride=2), :] = e2
                R[c, j, pl.ds(y + 1, part2, stride=2), :] = e2
        for i in range(part // 8):
            here = pl.ds(pl.multiple_of(y + i * 8, 8), 8)
            for p in range(X):
                for c in range(3):
                    out[c, p, here, :] = E[c, p, here, :] + R[c, p // 2, here, :]

        @pl.when(has_far)
        def _():
            f_far(k).wait_recv()

        for i in range(part // 8):
            outer_sweep(out, p_far, q_far, pl.multiple_of(y + i * 8, 8))

    for copy in near1 + [f_near, c_near]:
        copy.wait_send()

    @pl.when(has_far)
    def _():
        for k in range(PARTS):
            for copy in far1(k) + [f_far(k), c_far(k)]:
                copy.wait_send()


def per_device(tiles, load_field, iterate, phase_label, damage):
    f32, i32 = jnp.float32, jnp.int32
    padded = Y + 2 * OFF
    return pl.pallas_call(
        functools.partial(kernel, tiles),
        out_shape=jax.ShapeDtypeStruct(load_field.shape, f32),
        in_specs=[pl.BlockSpec(memory_space=pltpu.HBM)] * 4,
        out_specs=pl.BlockSpec(memory_space=pltpu.VMEM),
        scratch_shapes=[
            pltpu.VMEM((5, X + 2, padded, Z), f32),
            pltpu.VMEM((3, X + 2, padded, Z), f32),
            pltpu.VMEM((3, X, Y, Z), f32),
            pltpu.VMEM((3, X, Y, Z), f32),
            pltpu.VMEM((3, X // 2, Y, Z), f32),
            pltpu.VMEM((3, X, Y, Z), f32),
            pltpu.VMEM((2, X + 2, Y, Z), i32),
            pltpu.VMEM((20, Z), f32),
            pltpu.VMEM((20, Z), f32),
            pltpu.VMEM((16, Z), f32),
            pltpu.VMEM((16, Z), f32),
            pltpu.VMEM((PARTS, Y * 15 // (16 * PARTS), Z), f32),
            pltpu.VMEM((PARTS, Y * 15 // (16 * PARTS), Z), f32),
            pltpu.VMEM((PARTS, Y * 15 // (16 * PARTS), Z), f32),
            pltpu.VMEM((PARTS, Y * 15 // (16 * PARTS), Z), f32),
            pltpu.VMEM((2, 11, Y // 2, Z), f32),
            pltpu.VMEM((3, 4, Y // 2 + 2 * OFF, Z), f32),
            pltpu.VMEM((3, 2, Y // 2, Z), f32),
            pltpu.VMEM((2, 6, Y // 4, Z), f32),
            pltpu.VMEM((3, 3, Y // 4 + 2 * OFF, Z), f32),
            pltpu.VMEM((3, Y // 4, Z), f32),
            pltpu.VMEM((3, 2, Y // 2, Z), f32),
            pltpu.SemaphoreType.DMA((4,)),
            pltpu.SemaphoreType.DMA((5 * PARTS + 7,)),
            pltpu.SemaphoreType.DMA((5 * PARTS + 7,)),
        ],
        compiler_params=pltpu.CompilerParams(
            collective_id=0, has_side_effects=True, vmem_limit_bytes=48 * 1024 * 1024),
    )(*[pltpu.with_memory_space_constraint(a, pltpu.HBM) for a in (load_field, iterate, phase_label, damage)])


def solution(mesh):
    tiles = mesh.shape["tile"]
    in_specs = (
        P(None, "tile", "sec", None),
        P(None, "tile", "sec", None),
        P("tile", "sec", None),
        P("tile", "sec", None),
    )
    out_specs = P(None, "tile", "sec", None)
    return jax.shard_map(
        functools.partial(per_device, tiles), mesh=mesh, in_specs=in_specs, out_specs=out_specs, check_vma=False
    )
```

```python
import functools

import jax
import jax.numpy as jnp
from jax import lax
from jax.experimental import pallas as pl
from jax.experimental.pallas import tpu as pltpu
from jax.sharding import PartitionSpec as P

shear_table = (1.0, 0.6, 1.8, 0.35)
bulk_table = (1.2, 0.9, 2.5, 0.5)
damage_step = 0.25
damage_floor = 0.01
relaxation = 2.0 / 3.0

MESH = pl.DeviceIdType.MESH
X = 4
Y = 128
Z = 128
PARTS = 2
OFF = 8


def lanes(shape):
    return lax.broadcasted_iota(jnp.int32, shape, len(shape) - 1)


def roll(v, shift):
    return pltpu.roll(v, shift % Z, v.ndim - 1)


def from_above(v, step):
    return jnp.where(lanes(v.shape) < Z - step, roll(v, -step), 0.0)


def from_below(v, step):
    return jnp.where(lanes(v.shape) >= step, roll(v, step), 0.0)


def moduli(phase, damage):
    soft = 1.0 - damage_step * damage.astype(jnp.float32)
    degrade = soft * soft + damage_floor

    def table(values):
        picked = jnp.full(phase.shape, values[3], jnp.float32)
        for label in (2, 1, 0):
            picked = jnp.where(phase == label, values[label], picked)
        return picked

    half = table([0.5 * s for s in shear_table])
    normal = table([0.5 * b + s for s, b in zip(shear_table, bulk_table)])
    return half * degrade, normal * degrade


def kernel(tiles, load_hbm, u_hbm, lab_hbm, dam_hbm, out, U, F, L, INV, R, E, H, K, CODE, S1, S1R, S2, S2R,
           PN, QN, PF, QF, W2, F2, I2, W3, F3, I3, EX, local_sem, send_sem, recv_sem):
    LAB, DAM = CODE.at[0], CODE.at[1]
    me = lax.axis_index("tile")
    sec = lax.axis_index("sec")
    odd = lax.rem(me, 2)
    has_far = jnp.logical_and(me > 0, me < tiles - 1)
    near = {"tile": me + 1 - 2 * odd}
    far = {"tile": jnp.clip(me - 1 + 2 * odd, 0, tiles - 1)}
    across = {"sec": 1 - sec}
    p_near, q_near = X - (X - 1) * odd, (X + 1) * (1 - odd)
    p_far, q_far = 1 + (X - 1) * odd, (X + 1) * odd

    barrier = pltpu.get_barrier_semaphore()
    pl.semaphore_signal(barrier, inc=1, device_id=near, device_id_type=MESH)

    @pl.when(has_far)
    def _():
        pl.semaphore_signal(barrier, inc=1, device_id=far, device_id_type=MESH)

    pl.semaphore_signal(barrier, inc=1, device_id=across, device_id_type=MESH)

    loads = [
        pltpu.make_async_copy(lab_hbm, LAB.at[pl.ds(1, X)], local_sem.at[0]),
        pltpu.make_async_copy(dam_hbm, DAM.at[pl.ds(1, X)], local_sem.at[1]),
        pltpu.make_async_copy(u_hbm, U.at[:, pl.ds(1, X), pl.ds(OFF, Y)], local_sem.at[2]),
        pltpu.make_async_copy(load_hbm, L, local_sem.at[3]),
    ]
    for copy in loads[:3]:
        copy.start()

    own_row = jnp.where(sec == 0, OFF + Y - 1, OFF)
    halo_row = jnp.where(sec == 0, OFF + Y, OFF - 1)
    edge_row = jnp.where(sec == 0, OFF - 1, OFF + Y)
    faces = [H.at[pl.ds(1, X)], K.at[pl.ds(1, X)]] + [U.at[c, pl.ds(1, X)] for c in range(3)]
    zero_row = jnp.zeros((1, Z), jnp.float32)
    for copy in loads[:2]:
        copy.wait()
    for p in range(X):
        h, k = moduli(LAB[1 + p, pl.ds(own_row - OFF, 1), :], DAM[1 + p, pl.ds(own_row - OFF, 1), :])
        S1[pl.ds(p, 1), :] = h
        S1[pl.ds(X + p, 1), :] = k
    loads[2].wait()
    for f in range(2, 5):
        for p in range(X):
            S1[pl.ds(X * f + p, 1), :] = faces[f][p, pl.ds(own_row, 1), :]
    pl.semaphore_wait(barrier, 2 + has_far.astype(jnp.int32))

    def remote(src, dst, index, device):
        return pltpu.make_async_remote_copy(
            src_ref=src, dst_ref=dst, send_sem=send_sem.at[index], recv_sem=recv_sem.at[index],
            device_id=device, device_id_type=MESH)

    rows = pl.ds(OFF, Y)
    part = Y // PARTS
    base = 5 * PARTS

    def part_of(k):
        n = k + (1 - sec) * (PARTS - 1 - 2 * k)
        return pl.multiple_of(n * part, part)

    def far1(k):
        y = part_of(k)
        here, there = pl.ds(y, part), pl.ds(OFF + y, part)
        return [
            remote(CODE.at[:, p_far, here], CODE.at[:, X + 1 - q_far, here], 3 * k, far),
            remote(U.at[:, p_far, there], U.at[:, X + 1 - q_far, there], 3 * k + 2, far),
        ]

    def f_far(k):
        there = pl.ds(OFF + part_of(k), part)
        return remote(F.at[:, p_far, there], F.at[:, X + 1 - q_far, there], 3 * PARTS + k, far)

    def c_far(k):
        return remote(PF.at[k], QF.at[k], 4 * PARTS + k, far)

    near1 = [
        remote(CODE.at[:, p_near], CODE.at[:, X + 1 - q_near], base, near),
        remote(U.at[:, p_near, rows], U.at[:, X + 1 - q_near, rows], base + 2, near),
    ]
    cross1 = remote(S1, S1R, base + 3, across)
    cross1.start()

    @pl.when(has_far)
    def _():
        for k in range(PARTS):
            for copy in far1(k):
                copy.start()

    for copy in near1:
        copy.start()

    loads[3].start()

    @pl.loop(0, Y // 8)
    def _(i):
        y = pl.multiple_of(i * 8, 8)
        for p in range(1, X + 1):
            h, k = moduli(LAB[p, pl.ds(y, 8), :], DAM[p, pl.ds(y, 8), :])
            H[p, pl.ds(OFF + y, 8), :] = h
            K[p, pl.ds(OFF + y, 8), :] = k

    for ref in faces:
        for p in range(X):
            ref[p, pl.ds(edge_row, 1), :] = zero_row
    for c in range(3):
        for p in range(1, X + 1):
            F[c, p, pl.ds(edge_row, 1), :] = zero_row

    @pl.when(jnp.logical_not(has_far))
    def _():
        for ref in (H, K):
            ref[q_far] = jnp.zeros(H.shape[1:], jnp.float32)
        for c in range(3):
            U[c, q_far] = jnp.zeros(U.shape[2:], jnp.float32)
            F[c, q_far] = jnp.zeros(F.shape[2:], jnp.float32)

    def weights(p, y):
        result = {}
        for name, M in (("s", H), ("t", K)):
            m = M[p, pl.ds(OFF + y, 8), :]
            if p > 1:
                result[name, "xl"] = m + M[p - 1, pl.ds(OFF + y, 8), :]
            if p < X:
                result[name, "xu"] = m + M[p + 1, pl.ds(OFF + y, 8), :]
            result[name, "yl"] = m + M[p, pl.ds(OFF + y - 1, 8), :]
            result[name, "yu"] = m + M[p, pl.ds(OFF + y + 1, 8), :]
            result[name, "zl"] = m + from_below(m, 1)
            result[name, "zu"] = m + from_above(m, 1)
        return result

    def neighbours(V, c, p, y, w):
        v = V[c, p, pl.ds(OFF + y, 8), :]
        kind = ["t" if c == a else "s" for a in range(3)]
        total = w[kind[1], "yl"] * V[c, p, pl.ds(OFF + y - 1, 8), :]
        total = total + w[kind[1], "yu"] * V[c, p, pl.ds(OFF + y + 1, 8), :]
        total = total + w[kind[2], "zl"] * from_below(v, 1)
        total = total + w[kind[2], "zu"] * from_above(v, 1)
        if p > 1:
            total = total + w[kind[0], "xl"] * V[c, p - 1, pl.ds(OFF + y, 8), :]
        if p < X:
            total = total + w[kind[0], "xu"] * V[c, p + 1, pl.ds(OFF + y, 8), :]
        return total, v

    def inner_residual(y):
        here = pl.ds(y, 8)
        for p in range(1, X + 1):
            w = weights(p, y)
            sides = {}
            for name in ("s", "t"):
                xs = [w[name, side] for side in ("xl", "xu") if (name, side) in w]
                sides[name, 0] = xs[0] if len(xs) == 1 else xs[0] + xs[1]
                sides[name, 1] = w[name, "yl"] + w[name, "yu"]
                sides[name, 2] = w[name, "zl"] + w[name, "zu"]
            for c in range(3):
                total, v = neighbours(U, c, p, y, w)
                others = [a for a in range(3) if a != c]
                diag = sides["t", c] + sides["s", others[0]] + sides["s", others[1]]
                acc = L[c, p - 1, here, :] + total
                if 1 < p < X:
                    r = acc - diag * v
                    inv = relaxation / diag
                    R[c, p - 2, here, :] = r
                    INV[c, p - 1, here, :] = inv
                    F[c, p, pl.ds(OFF + y, 8), :] = r * inv
                else:
                    L[c, p - 1, here, :] = acc
                    INV[c, p - 1, here, :] = diag

    halo_chunk = pl.multiple_of((1 - sec) * (Y - 8), 8)
    loads[3].wait()

    @pl.loop(0, Y // 8 - 1)
    def _(i):
        inner_residual(pl.multiple_of((i + sec) * 8, 8))

    cross1.wait()
    for f, ref in enumerate(faces):
        for p in range(X):
            ref[p, pl.ds(halo_row, 1), :] = S1R[pl.ds(X * f + p, 1), :]
    inner_residual(halo_chunk)

    def outer_face(p, q, y, present):
        here, there = pl.ds(y, 8), pl.ds(OFF + y, 8)
        h, k = moduli(LAB[q, here, :], DAM[q, here, :])
        if present is not None:
            h = jnp.where(present, h, 0.0)
            k = jnp.where(present, k, 0.0)
        H[q, there, :] = h
        K[q, there, :] = k
        s = h + H[p, there, :]
        t = k + K[p, there, :]
        j = (p - 1) // 2
        for c in range(3):
            w = t if c == 0 else s
            diag = INV[c, p - 1, here, :] + w
            r = L[c, p - 1, here, :] + w * U[c, q, there, :] - diag * U[c, p, there, :]
            inv = relaxation / diag
            INV[c, p - 1, here, :] = inv
            F[c, p, there, :] = r * inv
            R[c, j, here, :] = R[c, j, here, :] + r

    for copy in near1:
        copy.wait_recv()

    @pl.loop(0, Y // 8)
    def _(i):
        outer_face(p_near, q_near, pl.multiple_of(i * 8, 8), None)

    f_near = remote(F.at[:, p_near, rows], F.at[:, X + 1 - q_near, rows], base + 4, near)
    f_near.start()

    Y2, Y3 = Y // 2, Y // 4
    part2, part3 = part // 2, part // 4
    shape2, shape3 = (part2, Z), (part3, Z)
    odd2 = (lanes(shape2) & 1) == 1
    quad = lanes(shape3) & 3
    high3 = quad >= 2
    j_near, j_far = 1 - odd, odd

    def pairs(v):
        return v + jnp.where(odd2, roll(v, 1), roll(v, -1))

    def quads(v):
        return v + jnp.where(high3, roll(v, 2), roll(v, -2))

    def fine_rows(M, p, first):
        return M[p, pl.ds(first, part2, stride=2), :]

    def coarse_rows(m, slot, y2, first):
        return W2[m, slot, pl.ds(y2 + first, part3, stride=2), :]

    def kinds(c):
        return [1 if c == a else 0 for a in range(3)]

    def x_face(M, p, q, y):
        face = fine_rows(M, p, OFF + y) + fine_rows(M, p, OFF + y + 1)
        return pairs(face + fine_rows(M, q, OFF + y) + fine_rows(M, q, OFF + y + 1))

    def residual_two(c, j, y):
        return pairs(fine_rows(R.at[c], j, y) + fine_rows(R.at[c], j, y + 1))

    @pl.loop(0, PARTS)
    def _(n):
        y = pl.multiple_of(n * part, part)
        y2 = pl.multiple_of(n * part2, part2)
        y3 = pl.multiple_of(n * part3, part3)
        at2, at3 = pl.ds(y2, part2), pl.ds(y3, part3)
        sides = {}
        for m, M in enumerate((H, K)):
            mid = x_face(M, 2, 3, y)
            close = x_face(M, p_near, q_near, y)
            W2[m, 1, at2, :] = mid
            W2[m, 2 - 2 * odd, at2, :] = close
            W3[m, 1 - odd, at3, :] = quads(
                coarse_rows(m, 2 - 2 * odd, y2, 0) + coarse_rows(m, 2 - 2 * odd, y2, 1))
            for j in range(2):
                r7, r8, r9, r10 = [
                    fine_rows(M, 1 + 2 * j, OFF + y + d) + fine_rows(M, 2 + 2 * j, OFF + y + d) for d in (-1, 0, 1, 2)]
                yl, yu = pairs(r7 + r8), pairs(r9 + r10)
                cell = r8 + r9
                low = cell + from_below(cell, 1)
                high = cell + from_above(cell, 1)
                zl = jnp.where(odd2, roll(low, 1), low)
                zu = jnp.where(odd2, high, roll(high, -1))
                for slot, value in ((3, yl), (5, yu), (7, zl), (9, zu)):
                    W2[m, slot + j, at2, :] = value
                sides[m, j, 0] = mid
                sides[m, j, 1] = yl + yu
                sides[m, j, 2] = zl + zu
            W3[m, 2, at3, :] = quads(coarse_rows(m, 3, y2, 0) + coarse_rows(m, 4, y2, 0))
            W3[m, 3, at3, :] = quads(coarse_rows(m, 5, y2, 1) + coarse_rows(m, 6, y2, 1))
            low = coarse_rows(m, 7, y2, 0) + coarse_rows(m, 7, y2, 1)
            low = low + coarse_rows(m, 8, y2, 0) + coarse_rows(m, 8, y2, 1)
            high = coarse_rows(m, 9, y2, 0) + coarse_rows(m, 9, y2, 1)
            high = high + coarse_rows(m, 10, y2, 0) + coarse_rows(m, 10, y2, 1)
            W3[m, 4, at3, :] = jnp.where(high3, roll(low, 2), low)
            W3[m, 5, at3, :] = jnp.where(high3, high, roll(high, -2))
        for c in range(3):
            kx, ky, kz = kinds(c)
            for j in range(2):
                I2[c, j, at2, :] = sides[kx, j, 0] + sides[ky, j, 1] + sides[kz, j, 2]
            inv = relaxation / (I2[c, j_near, at2, :] + W2[kx, 2 - 2 * odd, at2, :])
            I2[c, j_near, at2, :] = inv
            res = residual_two(c, j_near, y)
            EX[c, j_near, at2, :] = res
            F2[c, 1 + j_near, pl.ds(OFF + y2, part2), :] = res * inv
            I3[c, at3, :] = (W3[kx, 1 - odd, at3, :] + W3[ky, 2, at3, :] + W3[ky, 3, at3, :]
                             + W3[kz, 4, at3, :] + W3[kz, 5, at3, :])

    half = part2 // 2
    odd_half = odd2[:half]

    deep_pieces = [
        (0, part3 // 2, [(0, 0), (0, part3 // 2), (1, 0), (1, part3 // 2)]),
        (part3 // 2, part3 // 4, [(2, n * (part3 // 4)) for n in range(4)]),
    ]

    def packed(V, c, p, y2):
        return jnp.where(odd_half, V[c, p, pl.ds(OFF + y2 + half, half), :], V[c, p, pl.ds(OFF + y2, half), :])

    own2 = jnp.where(sec == 0, OFF + Y2 - 1, OFF)
    own3 = jnp.where(sec == 0, OFF + Y3 - 1, OFF)
    halo2 = jnp.where(sec == 0, OFF + Y2, OFF - 1)
    halo3 = jnp.where(sec == 0, OFF + Y3, OFF - 1)
    edge2 = jnp.where(sec == 0, OFF - 1, OFF + Y2)
    edge3 = jnp.where(sec == 0, OFF - 1, OFF + Y3)
    quad_row = lanes((1, Z)) & 3
    odd_row = (quad_row & 1) == 1
    fine_faces = [(c, p) for c in range(3) for p in range(1, X + 1)]
    for c in range(3):
        F2[c, 1, pl.ds(edge2, 1), :] = zero_row
        F2[c, 2, pl.ds(edge2, 1), :] = zero_row
        F3[c, 1, pl.ds(edge3, 1), :] = zero_row

    def pack_rows():
        for r, (c, p) in enumerate(fine_faces):
            S2[pl.ds(r, 1), :] = F[c, p, pl.ds(own_row, 1), :]
        deep = zero_row
        for c in range(3):
            S2[pl.ds(12 + c, 1), :] = jnp.where(odd_row, F2[c, 2, pl.ds(own2, 1), :], F2[c, 1, pl.ds(own2, 1), :])
            deep = jnp.where(quad_row == c, F3[c, 1, pl.ds(own3, 1), :], deep)
        S2[pl.ds(15, 1), :] = deep

    def unpack_rows():
        for r, (c, p) in enumerate(fine_faces):
            F[c, p, pl.ds(halo_row, 1), :] = S2R[pl.ds(r, 1), :]
        deep = S2R[pl.ds(15, 1), :]
        for c in range(3):
            v = S2R[pl.ds(12 + c, 1), :]
            F2[c, 1, pl.ds(halo2, 1), :] = jnp.where(odd_row, roll(v, 1), v)
            F2[c, 2, pl.ds(halo2, 1), :] = jnp.where(odd_row, v, roll(v, -1))
            F3[c, 1, pl.ds(halo3, 1), :] = spread_quad(deep, c, quad_row)

    def spread_quad(v, c, quad):
        spread = v
        for lane in range(4):
            if lane != c:
                spread = jnp.where(quad == lane, roll(v, lane - c), spread)
        return spread

    cross2 = remote(S2, S2R, base + 5, across)

    @pl.loop(0, PARTS)
    def _(k):
        y = part_of(k)

        @pl.when(has_far)
        def _():
            for copy in far1(k):
                copy.wait_recv()

        for i in range(part // 8):
            outer_face(p_far, q_far, pl.multiple_of(y + i * 8, 8), has_far)

        y2, y3 = pl.multiple_of(y // 2, part2), pl.multiple_of(y // 4, part3)
        at2, at3 = pl.ds(y2, part2), pl.ds(y3, part3)
        for m, M in enumerate((H, K)):
            W2[m, 2 * odd, at2, :] = x_face(M, p_far, q_far, y)
            W3[m, odd, at3, :] = quads(coarse_rows(m, 2 * odd, y2, 0) + coarse_rows(m, 2 * odd, y2, 1))
        for c in range(3):
            kx = kinds(c)[0]
            inv = relaxation / (I2[c, j_far, at2, :] + W2[kx, 2 * odd, at2, :])
            I2[c, j_far, at2, :] = inv
            res = residual_two(c, j_far, y)
            EX[c, j_far, at2, :] = res
            F2[c, 1 + j_far, pl.ds(OFF + y2, part2), :] = res * inv
            inv = relaxation / (I3[c, at3, :] + W3[kx, odd, at3, :])
            I3[c, at3, :] = inv
            res = EX[c, 0, pl.ds(y2, part3, stride=2), :] + EX[c, 0, pl.ds(y2 + 1, part3, stride=2), :]
            res = res + EX[c, 1, pl.ds(y2, part3, stride=2), :] + EX[c, 1, pl.ds(y2 + 1, part3, stride=2), :]
            first = quads(res) * inv
            F3[c, 1, pl.ds(OFF + y3, part3), :] = first
            PF[k, pl.ds(half * c, half), :] = packed(F2, c, 1 + j_far, y2)
            PN[k, pl.ds(half * c, half), :] = packed(F2, c, 1 + j_near, y2)
        for first_row, count, pieces in deep_pieces:
            quad_now = quad[:count]
            deep = F3[pieces[0][0], 1, pl.ds(OFF + y3 + pieces[0][1], count), :]
            for slot in range(1, 4):
                c, row = pieces[slot]
                deep = jnp.where(quad_now == slot, F3[c, 1, pl.ds(OFF + y3 + row, count), :], deep)
            PF[k, pl.ds(3 * half + first_row, count), :] = deep
            PN[k, pl.ds(3 * half + first_row, count), :] = deep

        @pl.when(k == 0)
        def _():
            pack_rows()
            cross2.start()

        @pl.when(has_far)
        def _():
            c_far(k).start()
            f_far(k).start()

    c_near = remote(PN, QN, base + 6, near)
    c_near.start()

    def inner_sweep(y):
        here = pl.ds(y, 8)
        for p in range(1, X + 1):
            w = weights(p, y)
            for c in range(3):
                total, v = neighbours(F, c, p, y, w)
                E[c, p - 1, here, :] = (4.0 / 3.0) * v + INV[c, p - 1, here, :] * total

    def outer_sweep(target, p, q, y):
        here, there = pl.ds(y, 8), pl.ds(OFF + y, 8)
        s = H[q, there, :] + H[p, there, :]
        t = K[q, there, :] + K[p, there, :]
        for c in range(3):
            w = t if c == 0 else s
            target[c, p - 1, here, :] = target[c, p - 1, here, :] + INV[c, p - 1, here, :] * (w * F[c, q, there, :])

    f_near.wait_recv()

    @pl.loop(0, Y // 8 - 1)
    def _(i):
        y = pl.multiple_of((i + sec) * 8, 8)
        inner_sweep(y)
        outer_sweep(E, p_near, q_near, y)

    cross2.wait()
    unpack_rows()
    inner_sweep(halo_chunk)
    outer_sweep(E, p_near, q_near, halo_chunk)

    def unpack(Q, k, q2, q3, present):
        y = part_of(k)
        y2, y3 = y // 2, y // 4
        for c in range(3):
            v = Q[k, pl.ds(half * c, half), :]
            if present is not None:
                v = jnp.where(present, v, 0.0)
            F2[c, q2, pl.ds(OFF + y2, half), :] = jnp.where(odd_half, roll(v, 1), v)
            F2[c, q2, pl.ds(OFF + y2 + half, half), :] = jnp.where(odd_half, v, roll(v, -1))
        for first_row, count, pieces in deep_pieces:
            v = Q[k, pl.ds(3 * half + first_row, count), :]
            if present is not None:
                v = jnp.where(present, v, 0.0)
            for slot, (c, row) in enumerate(pieces):
                F3[c, q3, pl.ds(OFF + y3 + row, count), :] = spread_quad(v, slot, quad[:count])

    c_near.wait_recv()
    for k in range(PARTS):
        unpack(QN, k, 3 * (1 - odd), 2 * (1 - odd), None)

    @pl.loop(0, PARTS)
    def _(k):
        y = part_of(k)
        y2, y3 = pl.multiple_of(y // 2, part2), pl.multiple_of(y // 4, part3)
        at2, at3 = pl.ds(y2, part2), pl.ds(y3, part3)

        @pl.when(has_far)
        def _():
            c_far(k).wait_recv()

        unpack(QF, k, 3 * odd, 2 * odd, has_far)
        for c in range(3):
            kx, ky, kz = kinds(c)

            def f3(p, d):
                return F3[c, p, pl.ds(OFF + y3 + d, part3), :]

            v = f3(1, 0)
            total = W3[kx, 0, at3, :] * f3(0, 0) + W3[kx, 1, at3, :] * f3(2, 0)
            total = total + W3[ky, 2, at3, :] * f3(1, -1) + W3[ky, 3, at3, :] * f3(1, 1)
            total = total + W3[kz, 4, at3, :] * from_below(v, 4) + W3[kz, 5, at3, :] * from_above(v, 4)
            e3 = (4.0 / 3.0) * v + I3[c, at3, :] * total
            EX[c, 0, pl.ds(y2, part3, stride=2), :] = e3
            EX[c, 0, pl.ds(y2 + 1, part3, stride=2), :] = e3
            e3 = EX[c, 0, at2, :]

            def f2(p, d):
                return F2[c, p, pl.ds(OFF + y2 + d, part2), :]

            for j in range(2):
                p = 1 + j
                v = f2(p, 0)
                total = W2[kx, j, at2, :] * f2(p - 1, 0) + W2[kx, j + 1, at2, :] * f2(p + 1, 0)
                total = total + W2[ky, 3 + j, at2, :] * f2(p, -1) + W2[ky, 5 + j, at2, :] * f2(p, 1)
                total = total + W2[kz, 7 + j, at2, :] * from_below(v, 2) + W2[kz, 9 + j, at2, :] * from_above(v, 2)
                e2 = (4.0 / 3.0) * v + I2[c, j, at2, :] * total + e3
                R[c, j, pl.ds(y, part2, stride=2), :] = e2
                R[c, j, pl.ds(y + 1, part2, stride=2), :] = e2
        for i in range(part // 8):
            here = pl.ds(pl.multiple_of(y + i * 8, 8), 8)
            for p in range(X):
                for c in range(3):
                    out[c, p, here, :] = E[c, p, here, :] + R[c, p // 2, here, :]

        @pl.when(has_far)
        def _():
            f_far(k).wait_recv()

        for i in range(part // 8):
            outer_sweep(out, p_far, q_far, pl.multiple_of(y + i * 8, 8))

    for copy in near1 + [f_near, c_near]:
        copy.wait_send()

    @pl.when(has_far)
    def _():
        for k in range(PARTS):
            for copy in far1(k) + [f_far(k), c_far(k)]:
                copy.wait_send()


def per_device(tiles, load_field, iterate, phase_label, damage):
    f32, i32 = jnp.float32, jnp.int32
    padded = Y + 2 * OFF
    return pl.pallas_call(
        functools.partial(kernel, tiles),
        out_shape=jax.ShapeDtypeStruct(load_field.shape, f32),
        in_specs=[pl.BlockSpec(memory_space=pltpu.HBM)] * 4,
        out_specs=pl.BlockSpec(memory_space=pltpu.VMEM),
        scratch_shapes=[
            pltpu.VMEM((3, X + 2, padded, Z), f32),
            pltpu.VMEM((3, X + 2, padded, Z), f32),
            pltpu.VMEM((3, X, Y, Z), f32),
            pltpu.VMEM((3, X, Y, Z), f32),
            pltpu.VMEM((3, X // 2, Y, Z), f32),
            pltpu.VMEM((3, X, Y, Z), f32),
            pltpu.VMEM((X + 2, padded, Z), f32),
            pltpu.VMEM((X + 2, padded, Z), f32),
            pltpu.VMEM((2, X + 2, Y, Z), i32),
            pltpu.VMEM((20, Z), f32),
            pltpu.VMEM((20, Z), f32),
            pltpu.VMEM((16, Z), f32),
            pltpu.VMEM((16, Z), f32),
            pltpu.VMEM((PARTS, Y * 15 // (16 * PARTS), Z), f32),
            pltpu.VMEM((PARTS, Y * 15 // (16 * PARTS), Z), f32),
            pltpu.VMEM((PARTS, Y * 15 // (16 * PARTS), Z), f32),
            pltpu.VMEM((PARTS, Y * 15 // (16 * PARTS), Z), f32),
            pltpu.VMEM((2, 11, Y // 2, Z), f32),
            pltpu.VMEM((3, 4, Y // 2 + 2 * OFF, Z), f32),
            pltpu.VMEM((3, 2, Y // 2, Z), f32),
            pltpu.VMEM((2, 6, Y // 4, Z), f32),
            pltpu.VMEM((3, 3, Y // 4 + 2 * OFF, Z), f32),
            pltpu.VMEM((3, Y // 4, Z), f32),
            pltpu.VMEM((3, 2, Y // 2, Z), f32),
            pltpu.SemaphoreType.DMA((4,)),
            pltpu.SemaphoreType.DMA((5 * PARTS + 7,)),
            pltpu.SemaphoreType.DMA((5 * PARTS + 7,)),
        ],
        compiler_params=pltpu.CompilerParams(
            collective_id=0, has_side_effects=True, vmem_limit_bytes=48 * 1024 * 1024),
    )(*[pltpu.with_memory_space_constraint(a, pltpu.HBM) for a in (load_field, iterate, phase_label, damage)])


def solution(mesh):
    tiles = mesh.shape["tile"]
    in_specs = (
        P(None, "tile", "sec", None),
        P(None, "tile", "sec", None),
        P("tile", "sec", None),
        P("tile", "sec", None),
    )
    out_specs = P(None, "tile", "sec", None)
    return jax.shard_map(
        functools.partial(per_device, tiles), mesh=mesh, in_specs=in_specs, out_specs=out_specs, check_vma=False
    )
```
